32 devices in a mesh: grp: 4 (over z), sub: 8 (over y, x, core).
Axes of the slice: x: 2, y: 2, z: 4, core: 2. Of those that a mesh axis runs over, the one named last changes fastest.
Arguments:
- stiff_blocks: float32 [8, 128, 4, 128, 128], P('grp', 'sub'), may hold values from -0.25 to 0.25
- block_cols: int32 [8, 128, 4], P('grp', 'sub'), may hold values from 0 to 127, as said below
- live_blocks: int32 [8, 8], P('grp', 'sub'), may hold values from 1 to 16, as said below
- sub_diag: float32 [8, 16384], P('grp', 'sub'), may hold values from 0.05 to 1
- penalty: float32 [8, 1024], P('grp', 'sub'), may hold values from 0.5 to 4
- sub_load: float32 [8, 16384], P('grp', 'sub'), may hold values from -6 to 6
- iface_map: int32 [8, 1024], P('grp', 'sub'), may hold values from 0 to 262143
- global_load: float32 [1024, 256], P(('grp', 'sub')), may hold values from -6 to 6
- global_diag: float32 [1024, 256], P(('grp', 'sub')), may hold values from 0.1 to 1
Outputs:
- global_field: float32 [1024, 256], P(('grp', 'sub'))
- sub_field: float32 [8, 16384], P('grp', 'sub')
The draws below stay inside these ranges and needn't reach their ends.
Inputs may be any that keep to these rules, and one draw needn't show every extreme that they name: `live_blocks`: every live count is at least 1 and at most 16; the first submodel holds 16 live block rows on index 0 of sub. `block_cols`: among the blocks of one submodel's block rows on one index of sub, at most 8 have their column block among the block rows of any one index of sub; in every submodel some index of sub receives exactly 8 such blocks from every index of sub.
All inputs are finite; a program needn't handle non-finite values.
Results may differ from the reference program's by a relative error of at most 0.0003.
Values sent between devices are 32-bit elements; how exact they have to be, the bound alone decides.
No kernel may reach another device: no remote copies, remote signals or barrier semaphores. Data moves between devices by JAX's collectives and lax.ppermute only.
A program may use at most 64 MiB of HBM per device.

```python
import math
import jax
import jax.numpy as jnp
from jax import lax

BS = 128
NB = 4
RB = 16
GY = 256
CG_STEPS = 2
COUPLE = 2
CAP = 8
SUBS = 8
M_DEV = 2048
M = 16384
MB = 128
IFACE = 1024
NGX = 1024
N_SUB = 8


def draw_live_blocks(key, part):
    counts = jax.random.randint(key, (SUBS, N_SUB), 1, RB + 1)
    first = jnp.arange(SUBS)[:, None] + jnp.arange(N_SUB)[None, :] == 0
    return jnp.where(first, RB, counts).astype(jnp.int32)


def draw_block_cols(key, part):
    slots_all = RB * NB
    key_top = jax.random.fold_in(key, 11)
    key_order = jax.random.fold_in(key, 12)
    key_local = jax.random.fold_in(key, 13)
    top_owner = jax.random.randint(key_top, (SUBS, 1, 1), 0, N_SUB)
    slot = jnp.arange(slots_all, dtype=jnp.int32)[None, None, :]
    others = (top_owner + 1 + (slot - CAP) % (N_SUB - 1)) % N_SUB
    owner = jnp.where(slot < CAP, top_owner, others)
    owner = jnp.broadcast_to(owner, (SUBS, N_SUB, slots_all))
    scores = jax.random.randint(key_order, (SUBS, N_SUB, slots_all), 0, 1048576) * slots_all + slot
    order = jnp.argsort(scores, axis=2)
    owner = jnp.take_along_axis(owner, order, axis=2)
    local = jax.random.randint(key_local, (SUBS, N_SUB, slots_all), 0, RB)
    cols = owner * RB + local
    return cols.reshape(SUBS, MB, NB).astype(jnp.int32)


def set_ends(result, stream_key, smallest, largest):
    index_at = [jax.random.randint(jax.random.fold_in(stream_key, axis), (), 0, length) for axis, length in enumerate(result.shape)]
    longest = result.shape.index(max(result.shape))
    neighbour = index_at[:longest] + [(index_at[longest] + 1) % result.shape[longest]] + index_at[longest + 1:]
    return result.at[tuple(index_at)].set(smallest).at[tuple(neighbour)].set(largest)


def levels(rng, dims, pieces, smallest, largest):
    level, own = 1.0, jax.random.fold_in(rng, 6)
    for dim, shards_of in pieces:
        draws = jnp.exp(jax.random.uniform(jax.random.fold_in(own, dim), (shards_of,), jnp.float32, smallest / len(pieces), largest / len(pieces)))
        level = level * jnp.repeat(draws, dims[dim] // shards_of).reshape([-1 if axis == dim else 1 for axis in range(len(dims))])
    return level


def gaussian(own_key, extent, scale, limit, cuts=(), kind=jnp.bfloat16):
    loudness = levels(own_key, extent, cuts, -0.22, 0.18) if cuts else 1.0
    drawn = jax.random.normal(own_key, extent, jnp.float32) * scale * loudness
    return jnp.minimum(jnp.maximum(drawn, -limit), limit).astype(kind)


def setup_inputs(seed: int = 0) -> dict:
    keys = jax.random.split(jax.random.key(seed), 10)
    return {
        "stiff_blocks": gaussian(keys[0], (SUBS, MB, NB, BS, BS), (NB * BS) ** -0.5, 0.25, ((0, 4), (1, 8)), jnp.float32),
        "block_cols": draw_block_cols(jax.random.fold_in(keys[9], 71), 0),
        "live_blocks": draw_live_blocks(jax.random.fold_in(keys[9], 71), 0),
        "sub_diag": jnp.clip(jnp.exp(math.log(1.0) - 2.9957323 * jax.random.uniform(keys[3], (SUBS, M), jnp.float32) ** levels(keys[3], (SUBS, M), ((0, 4), (1, 8)), -0.2, 0.2)), 0.05, 1.0),
        "penalty": jnp.clip(jnp.exp(math.log(4.0) - 2.0794415 * jax.random.uniform(keys[4], (SUBS, IFACE), jnp.float32) ** levels(keys[4], (SUBS, IFACE), ((0, 4), (1, 8)), -0.2, 0.2)), 0.5, 4.0),
        "sub_load": gaussian(keys[5], (SUBS, M), 1.0, 6.0, ((0, 4), (1, 8)), jnp.float32),
        "iface_map": set_ends(jax.random.randint(keys[6], (SUBS, IFACE), 0, NGX * GY), jax.random.fold_in(keys[6], 1), 0, (NGX * GY) - 1).astype(jnp.int32),
        "global_load": gaussian(keys[7], (NGX, GY), 1.0, 6.0, ((0, 32),), jnp.float32),
        "global_diag": jnp.clip(0.1 + 0.9 * jax.random.uniform(keys[8], (NGX, GY), jnp.float32) ** levels(keys[8], (NGX, GY), ((0, 32),), -0.2, 0.2), 0.1, 1.0),
    }


HIGH = lax.Precision.HIGHEST


def sub_apply(stiff, cols, v, mask, dsum):
    picked = v.reshape(-1, BS)[cols]
    strain = jnp.einsum('rnij,rnj->ri', stiff, picked, precision=HIGH)
    terms = jnp.einsum('rnij,ri->rnj', stiff, strain, precision=HIGH)
    back = jax.ops.segment_sum(terms.reshape(-1, BS), cols.reshape(-1), num_segments=MB)
    return mask * (dsum * v + back.reshape(-1))


def spread_rows(values):
    front = values.reshape(N_SUB, BS)
    rest = jnp.zeros((N_SUB, M_DEV - BS), values.dtype)
    return jnp.concatenate([front, rest], axis=1).reshape(M)


def solve_one(packed):
    stiff, cols, live, sdiag, pen, load, bvals, start = packed
    rows = jnp.arange(M, dtype=jnp.int32)
    owner = rows // M_DEV
    block = (rows % M_DEV) // BS
    mask = (block < live[owner]).astype(sdiag.dtype)
    pen_full = spread_rows(pen)
    dsum = sdiag + pen_full
    rhs = mask * (load + pen_full * spread_rows(bvals))
    field = start
    resid = rhs - sub_apply(stiff, cols, field, mask, dsum)
    direction = resid
    norm_now = jnp.sum(resid * resid)
    for step in range(CG_STEPS):
        image = sub_apply(stiff, cols, direction, mask, dsum)
        alpha = norm_now / jnp.sum(direction * image)
        field = field + alpha * direction
        resid = resid - alpha * image
        norm_next = jnp.sum(resid * resid)
        direction = resid + (norm_next / norm_now) * direction
        norm_now = norm_next
    return field


def glob_apply(field, gdiag):
    padded = jnp.pad(field, 1)
    beside = padded[2:, 1:-1] + padded[:-2, 1:-1] + padded[1:-1, 2:] + padded[1:-1, :-2]
    return (4.0 + gdiag) * field - beside


def reference(stiff_blocks, block_cols, live_blocks, sub_diag, penalty, sub_load, iface_map, global_load, global_diag):
    global_field = jnp.zeros_like(global_load)
    sub_field = jnp.zeros_like(sub_load)
    for outer in range(COUPLE):
        bvals = global_field.reshape(-1)[iface_map]
        sub_field = lax.map(solve_one, (stiff_blocks, block_cols, live_blocks, sub_diag, penalty, sub_load, bvals, sub_field))
        at_iface = sub_field.reshape(SUBS, N_SUB, M_DEV)[:, :, :BS].reshape(SUBS, IFACE)
        lam = penalty * (at_iface - bvals)
        lam_g = jnp.zeros((NGX * GY,), global_load.dtype).at[iface_map.reshape(-1)].add(lam.reshape(-1)).reshape(NGX, GY)
        resid = global_load - glob_apply(global_field, global_diag) + lam_g
        image = glob_apply(resid, global_diag)
        alpha = jnp.sum(resid * resid) / jnp.sum(resid * image)
        global_field = global_field + alpha * resid
    return global_field, sub_field
```

```python
import jax
import jax.numpy as jnp
from jax import lax
from jax.experimental import pallas as pl
from jax.experimental.pallas import tpu as pltpu
from jax.sharding import PartitionSpec as P

F32 = jnp.float32
BF16 = jnp.bfloat16
EDGE = 8
ALL = ("grp", "sub")

VMEM = pl.BlockSpec(memory_space=pltpu.VMEM)
SMEM = pl.BlockSpec(memory_space=pltpu.SMEM)


def total(x):
    return jnp.sum(jnp.sum(x, axis=0, keepdims=True), axis=1, keepdims=True)


def split3(x):
    hi = x.astype(BF16)
    rest = x - hi.astype(F32)
    mid = rest.astype(BF16)
    return hi, mid, (rest - mid.astype(F32)).astype(BF16)


def iota(shape, dim):
    return lax.broadcasted_iota(jnp.int32, shape, dim)


def contract(stiff, cols, vector, terms):
    slots, block_rows, per_row, width, _ = stiff.shape
    squares = []
    for s in range(slots):

        def row(r, acc, s=s):
            prod = None
            for n in range(per_row):
                part = stiff[s, r, n] * vector(s, cols[s, r * per_row + n])
                prod = part if prod is None else prod + part
            strain = jnp.sum(prod, axis=1, keepdims=True)
            if terms is not None:
                for n in range(per_row):
                    terms[s, pl.ds(r * per_row + n, 1), :] = jnp.sum(
                        stiff[s, r, n] * strain, axis=0, keepdims=True
                    )
            return acc + strain * strain

        squares.append(lax.fori_loop(0, block_rows, row, jnp.zeros((width, 1), F32), unroll=2))
    return squares


def stacked(gathered, first, count):
    devices, slots = gathered.shape[:2]
    return jnp.concatenate(
        [gathered[d, s, first : first + count, :] for s in range(slots) for d in range(devices)],
        axis=0,
    )


def landed(pack, arrived, block_rows, count):
    devices, slots, _, width = pack.shape
    targets = slots * devices * block_rows
    source = jnp.concatenate(
        [arrived[d, s, :count, :] for d in range(devices) for s in range(slots)], axis=0
    )
    col = jnp.concatenate(
        [pack[d, 0, 2 * block_rows + 1 : 2 * block_rows + 2, :] for d in range(devices)], axis=1
    )
    hot = jnp.where(iota((targets, col.shape[1]), 0).astype(F32) == col, 1.0, 0.0).astype(BF16)
    out = jnp.dot(hot, jnp.concatenate(split3(source), axis=1), preferred_element_type=F32)
    return out[:, :width] + out[:, width : 2 * width] + out[:, 2 * width :]


def prep_kernel(live, diag, pen, load, cols, gload, gdiag, pack, up, down):
    slots, rows, width = pack.shape
    block_rows = (rows - 8) // 2
    pack[:, 2 * block_rows :, :] = jnp.zeros((slots, 8, width), F32)
    for s in range(slots):
        count = live[s, 0]
        for b in range(block_rows):
            lanes = pl.ds(b * width, width)
            on = b < count
            main = diag[s : s + 1, lanes]
            if b == 0:
                main = main + pen[s : s + 1, :]
            pack[s, b : b + 1, :] = jnp.where(on, load[s : s + 1, lanes], 0.0)
            pack[s, block_rows + b : block_rows + b + 1, :] = jnp.where(on, main, 0.0)
        pack[s, 2 * block_rows : 2 * block_rows + 1, :] = pen[s : s + 1, :]
    pack[0, 2 * block_rows + 1 : 2 * block_rows + 2, :] = cols[...]
    last = gload.shape[0]
    up[...] = jnp.zeros_like(up)
    down[...] = jnp.zeros_like(down)
    up[0:2, :] = gload[0:2, :]
    up[2:3, :] = gdiag[0:1, :]
    down[0:2, :] = gload[last - 2 : last, :]
    down[2:3, :] = gdiag[last - 1 : last, :]


def first_kernel(cols, pack, stiff, terms):
    block_rows = stiff.shape[1]

    def vector(s, c):
        return pack[lax.div(c, block_rows), s, pl.ds(lax.rem(c, block_rows), 1), :]

    contract(stiff, cols, vector, terms)


def second_kernel(cols, pack, arrived, maps, stiff, resid, direc, terms, send, xown, pown):
    slots, block_rows, per_row, width, _ = stiff.shape
    devices = pack.shape[0]
    blocks = devices * block_rows
    me = lax.axis_index("sub")
    start = stacked(pack, 0, block_rows)
    dsum = stacked(pack, block_rows, block_rows)
    back = landed(pack, arrived, block_rows, block_rows * per_row)
    image = jnp.where(dsum > 0.0, dsum * start + back, 0.0)
    head, scal = [], []
    for s in range(slots):
        span = slice(s * blocks, (s + 1) * blocks)
        r0, q0 = start[span], image[span]
        norm = total(r0 * r0)
        alpha = norm / total(r0 * q0)
        r1 = r0 - alpha * q0
        norm1 = total(r1 * r1)
        p1 = r1 + norm1 / norm * r0
        resid[span, :] = r1
        direc[span, :] = p1
        scal.append((norm1, total(dsum[span] * p1 * p1)))
        xown[s] = alpha * pack[me, s, :block_rows, :]
        pown[s] = direc[pl.ds(s * blocks + me * block_rows, block_rows), :]
        head.append(pack[me, s, 2 * block_rows : 2 * block_rows + 1, :])
    squares = contract(stiff, cols, lambda s, c: direc[pl.ds(s * blocks + c, 1), :], terms)
    write_send(send, maps, head, [xown[s, 0:1, :] for s in range(slots)], pown, scal, squares, devices)


def write_send(send, maps, pen, x_face, pown, scal, squares, devices):
    slots, width = maps.shape
    lane = iota((1, width), 1)
    rows = [maps[s : s + 1, :] for s in range(slots)]
    rows += [pen[s] * x_face[s] for s in range(slots)]
    rows += [pen[s] * pown[s, 0:1, :] for s in range(slots)]
    for s in range(slots):
        norm1, own = scal[s]
        image = total(squares[s]) + own * (1.0 / devices)
        rows.append(jnp.where(lane < width // 2, image, norm1 * (1.0 / devices)))
    send[...] = jnp.broadcast_to(jnp.concatenate(rows, axis=0)[None], send.shape)


def reactions(got, groups):
    devices, rows, width = got.shape
    slots = rows // 4
    half = width // 2
    alphas, lams = [], []
    for s in range(slots):
        both = got[:, 3 * slots + s, :].reshape(groups, devices // groups, width).sum(axis=1)
        turned = pltpu.roll(both, half, 1)
        low = iota(both.shape, 1) < half
        alpha = jnp.where(low, turned, both) / jnp.where(low, both, turned)
        wide = jnp.broadcast_to(alpha[:, None, :], (groups, devices // groups, width))
        alphas.append(alpha)
        lams.append(got[:, slots + s, :] + wide.reshape(devices, width) * got[:, 2 * slots + s, :])
    return alphas, lams


def place(got_map, lams, row_s, col_s, part_s, first_row, window, hot_s):
    devices = got_map.shape[0]
    slots = len(lams)
    rows, columns = window
    for s in range(slots):
        flat = got_map[:, s, :]
        row = jnp.floor(flat * (1.0 / columns))
        col_s[s] = flat - row * columns
        row_s[s] = row - first_row
        hi = lams[s].astype(BF16).astype(F32)
        mid = (lams[s] - hi).astype(BF16).astype(F32)
        part_s[0, s] = hi
        part_s[1, s] = mid
        part_s[2, s] = lams[s] - hi - mid
    ids_c = iota((columns, 1), 0).astype(F32)
    ids_r = iota((rows, 1), 0).astype(F32)

    def lanes(ref, d):
        return jnp.concatenate([ref[s, pl.ds(d, 1), :] for s in range(slots)], axis=1)

    def step(d, acc):
        hot_c = jnp.where(ids_c == lanes(col_s, d), 1.0, 0.0).astype(BF16)
        if hot_s is not None:
            hot_s[d] = hot_c
        hit = ids_r == lanes(row_s, d)
        left = jnp.concatenate(
            [jnp.where(hit, lanes(part_s.at[i], d), 0.0).astype(BF16) for i in range(3)], axis=0
        )
        return acc + lax.dot_general(
            left, hot_c, (((1,), (1,)), ((), ())), preferred_element_type=F32
        )

    acc = lax.fori_loop(0, devices, step, jnp.zeros((3 * rows, columns), F32), unroll=2)
    return acc[:rows] + acc[rows : 2 * rows] + acc[2 * rows :]


def stencil(ref, gdiag, first, count):
    here = ref[first : first + count, :]
    columns = here.shape[1]
    lane = iota(here.shape, 1)
    left = jnp.where(lane == 0, 0.0, pltpu.roll(here, 1, 1))
    right = jnp.where(lane == columns - 1, 0.0, pltpu.roll(here, columns - 1, 1))
    above = ref[first - 1 : first + count - 1, :]
    below = ref[first + 1 : first + count + 1, :]
    return (4.0 + gdiag) * here - (above + below + left + right)


def fill_window(window, own, before, after, width):
    rows = own.shape[0]
    window[...] = jnp.zeros_like(window)
    window[EDGE : EDGE + rows, :] = own[...]
    if width == 2:
        window[EDGE - 2 : EDGE, :] = before[0:2, :]
        window[EDGE + rows : EDGE + rows + 2, :] = after[0:2, :]
    else:
        window[EDGE - 1 : EDGE, :] = before[2:3, :]
        window[EDGE + rows : EDGE + rows + 1, :] = after[2:3, :]


def third_kernel(got, gload, gdiag, before, after, window, alphas_out, send, row_s, col_s, part_s, hot_s):
    rows, columns = gload.shape
    devices, _, width = got.shape
    groups = lax.axis_size("grp")
    flat = lax.axis_index("grp") * lax.axis_size("sub") + lax.axis_index("sub")
    first_row = (flat * rows - EDGE).astype(F32)
    alphas, lams = reactions(got, groups)
    slots = len(lams)
    for s in range(slots):
        alphas_out[s, 0:groups, :] = alphas[s]
    fill_window(window, gload, before, after, 2)
    extent = window.shape
    placed = place(got, lams, row_s, col_s, part_s, first_row, extent, hot_s)
    at = iota(extent, 0)
    inside = (at >= EDGE - 2) & (at < EDGE + rows + 2)
    window[...] = window[...] + jnp.where(inside, placed, 0.0)
    own = window[EDGE : EDGE + rows, :]
    image = stencil(window, gdiag[...], EDGE, rows)
    send[...] = jnp.zeros_like(send)
    send[:, slots : slots + 1, :] = jnp.broadcast_to(total(own * own)[None], (devices, 1, width))
    send[:, slots + 1 : slots + 2, :] = jnp.broadcast_to(total(own * image)[None], (devices, 1, width))
    parts = jnp.concatenate(split3(own), axis=0)
    ids = iota((rows, 1), 0).astype(F32) + EDGE

    def step(d, carry):
        seen = jnp.dot(parts, hot_s[d], preferred_element_type=F32)
        seen = seen[:rows] + seen[rows : 2 * rows] + seen[2 * rows :]
        row = jnp.concatenate([row_s[s, pl.ds(d, 1), :] for s in range(slots)], axis=1)
        mine = jnp.sum(jnp.where(ids == row, seen, 0.0), axis=0, keepdims=True)
        for s in range(slots):
            send[d, s : s + 1, :] = mine[:, s * width : (s + 1) * width]
        return carry

    lax.fori_loop(0, devices, step, 0, unroll=2)


def scale_kernel(got, terms, window, send, field):
    slots, count, width = terms.shape
    sums = jnp.sum(got[...], axis=0)
    scale = sums[slots : slots + 1, :] / sums[slots + 1 : slots + 2, :]
    send[:, :count, :] = terms[...]
    send[:, count:, :] = jnp.zeros((slots, send.shape[1] - count, width), F32)
    for s in range(slots):
        send[s, count : count + 1, :] = scale * sums[s : s + 1, :]
    field[...] = window[...] * jnp.concatenate([scale] * (field.shape[1] // width), axis=1)


def fourth_kernel(cols, pack, arrived, alphas, resid, direc, xown, pown, stiff, start, terms, xnext):
    slots, block_rows, per_row, width, _ = stiff.shape
    devices = pack.shape[0]
    blocks = devices * block_rows
    count = block_rows * per_row
    group = lax.axis_index("grp")
    dsum = stacked(pack, block_rows, block_rows)
    back = landed(pack, arrived, block_rows, count)
    p1 = direc[...]
    image = jnp.where(dsum > 0.0, dsum * p1 + back, 0.0)
    for s in range(slots):
        span = slice(s * blocks, (s + 1) * blocks)
        alpha = alphas[s, pl.ds(group, 1), :]
        start[span, :] = resid[span, :] - alpha * image[span]
        xnext[s] = xown[s] + alpha * pown[s]
        for d in range(devices):
            face = slice(s * blocks + d * block_rows, s * blocks + d * block_rows + 1)
            pen = pack[d, s, 2 * block_rows : 2 * block_rows + 1, :]
            start[face, :] = start[face, :] + pen * arrived[d, s, count : count + 1, :]
    contract(stiff, cols, lambda s, c: start[pl.ds(s * blocks + c, 1), :], terms)


def fifth_kernel(cols, pack, arrived, bound, start, maps, xin, stiff, send, xown, pown, direc):
    slots, block_rows, per_row, width, _ = stiff.shape
    devices = pack.shape[0]
    blocks = devices * block_rows
    count = block_rows * per_row
    me = lax.axis_index("sub")
    dsum = stacked(pack, block_rows, block_rows)
    back = landed(pack, arrived, block_rows, count)
    image = jnp.where(dsum > 0.0, dsum * start[...] + back, 0.0)
    head, face, scal = [], [], []
    for s in range(slots):
        span = slice(s * blocks, (s + 1) * blocks)
        r0, q0 = start[span, :], image[span]
        norm = total(r0 * r0)
        alpha = norm / total(r0 * q0)
        r1 = r0 - alpha * q0
        norm1 = total(r1 * r1)
        p1 = r1 + norm1 / norm * r0
        direc[span, :] = p1
        scal.append((norm1, total(dsum[span] * p1 * p1)))
        mine = pl.ds(s * blocks + me * block_rows, block_rows)
        xown[s] = xin[s] + alpha * start[mine, :]
        pown[s] = direc[mine, :]
        head.append(pack[me, s, 2 * block_rows : 2 * block_rows + 1, :])
        face.append(xown[s, 0:1, :] - bound[s, count : count + 1, :])
    squares = contract(stiff, cols, lambda s, c: direc[pl.ds(s * blocks + c, 1), :], None)
    write_send(send, maps, head, face, pown, scal, squares, devices)


def sixth_kernel(
    got, gload, gdiag, before, after, field, xown, pown, resid, xout, send, window, diags, row_s, col_s, part_s
):
    rows, columns = gload.shape
    devices, _, width = got.shape
    groups = lax.axis_size("grp")
    group = lax.axis_index("grp")
    flat = group * lax.axis_size("sub") + lax.axis_index("sub")
    first_row = flat * rows - EDGE
    alphas, lams = reactions(got, groups)
    slots = len(lams)
    for s in range(slots):
        part_s[0, s, 0:groups, :] = alphas[s]
        alpha = part_s[0, s, pl.ds(group, 1), :]
        for b in range(xown.shape[1]):
            xout[s : s + 1, b * width : (b + 1) * width] = (
                xown[s, b : b + 1, :] + alpha * pown[s, b : b + 1, :]
            )
    fill_window(window, gload, before, after, 2)
    fill_window(diags, gdiag, before, after, 1)
    extent = window.shape
    placed = place(got, lams, row_s, col_s, part_s, first_row.astype(F32), extent, None)
    span = slice(EDGE - 1, EDGE + rows + 1)
    applied = stencil(field, diags[span, :], EDGE - 1, rows + 2)
    at = iota(applied.shape, 0) + (first_row + EDGE - 1)
    inside = (at >= 0) & (at < devices * rows)
    window[span, :] = jnp.where(inside, window[span, :] - applied + placed[span], 0.0)
    own = window[EDGE : EDGE + rows, :]
    resid[...] = own
    image = stencil(window, gdiag[...], EDGE, rows)
    send[...] = jnp.zeros_like(send)
    send[:, 0:1, :] = jnp.broadcast_to(total(own * own)[None], (devices, 1, width))
    send[:, 1:2, :] = jnp.broadcast_to(total(own * image)[None], (devices, 1, width))


def last_kernel(got, field, resid, out):
    sums = jnp.sum(got[...], axis=0)
    scale = sums[0:1, :] / sums[1:2, :]
    rows, columns = out.shape
    wide = jnp.concatenate([scale] * (columns // got.shape[2]), axis=1)
    out[...] = field[EDGE : EDGE + rows, :] + wide * resid[...]


def call(kernel, shapes, operands, scalars, scratch=(), limit=None):
    out_shape = [jax.ShapeDtypeStruct(s, F32) for s in shapes]
    return pl.pallas_call(
        kernel,
        out_shape=out_shape,
        in_specs=[SMEM] * scalars + [VMEM] * (len(operands) - scalars),
        out_specs=[VMEM] * len(shapes),
        scratch_shapes=list(scratch),
        compiler_params=pltpu.CompilerParams(vmem_limit_bytes=limit),
    )(*operands)


def body(
    stiff_blocks,
    block_cols,
    live_blocks,
    sub_diag,
    penalty,
    sub_load,
    iface_map,
    global_load,
    global_diag,
):
    slots, block_rows, per_row, width, _ = stiff_blocks.shape
    rows_dev = block_rows * width
    rows, columns = global_load.shape
    near, groups = lax.axis_size("sub"), lax.axis_size("grp")
    devices = near * groups
    blocks = slots * near * block_rows
    count = block_rows * per_row
    extent = (rows + 2 * EDGE, columns)
    own = (slots, block_rows, width)
    cols = block_cols.reshape(slots, count)
    shift = jnp.arange(slots, dtype=jnp.int32)[:, None] * (near * block_rows)
    col_row = (cols + shift).astype(F32).reshape(1, slots * count)
    maps = iface_map.astype(F32)

    def everywhere(x):
        return lax.all_to_all(x, ALL, 0, 0)

    def near_all(x):
        return lax.all_gather(x, "sub")

    pack, up, down = call(
        prep_kernel,
        [(slots, 2 * block_rows + 8, width), (8, columns), (8, columns)],
        (live_blocks, sub_diag, penalty, sub_load, col_row, global_load, global_diag),
        1,
    )
    hops = [(i, i + 1) for i in range(devices - 1)]
    before = lax.ppermute(down, ALL, hops)
    after = lax.ppermute(up, ALL, [(j, i) for i, j in hops])
    pack = near_all(pack)
    (terms,) = call(first_kernel, [(slots, count, width)], (cols, pack, stiff_blocks), 1)
    arrived = near_all(terms)
    resid, direc, terms, send, xown, pown = call(
        second_kernel,
        [(blocks, width), (blocks, width), (slots, count, width), (devices, 4 * slots, width), own, own],
        (cols, pack, arrived, maps, stiff_blocks),
        1,
    )
    got = everywhere(send)
    lists = pltpu.VMEM((slots, devices, width), F32)
    parts = pltpu.VMEM((3, slots, devices, width), F32)
    window, alphas, send = call(
        third_kernel,
        [extent, (slots, max(8, groups), width), (devices, 8, width)],
        (got, global_load, global_diag, before, after),
        0,
        (lists, lists, parts, pltpu.VMEM((devices, columns, slots * width), BF16)),
    )
    sums = everywhere(send)
    bound, field = call(scale_kernel, [(slots, count + 8, width), extent], (sums, terms, window), 0)
    arrived = near_all(bound)
    start, terms, xown = call(
        fourth_kernel,
        [(blocks, width), (slots, count, width), own],
        (cols, pack, arrived, alphas, resid, direc, xown, pown, stiff_blocks),
        1,
    )
    arrived = near_all(terms)
    send, xown, pown = call(
        fifth_kernel,
        [(devices, 4 * slots, width), own, own],
        (cols, pack, arrived, bound, start, maps, xown, stiff_blocks),
        1,
        (pltpu.VMEM((blocks, width), F32),),
    )
    got = everywhere(send)
    resid, sub_field, send = call(
        sixth_kernel,
        [(rows, columns), (slots, rows_dev), (devices, 8, width)],
        (got, global_load, global_diag, before, after, field, xown, pown),
        0,
        (pltpu.VMEM(extent, F32), pltpu.VMEM(extent, F32), lists, lists, parts),
    )
    sums = everywhere(send)
    (global_field,) = call(last_kernel, [(rows, columns)], (sums, field, resid), 0)
    return global_field, sub_field


def solution(mesh):
    return jax.shard_map(
        body,
        mesh=mesh,
        in_specs=(
            P("grp", "sub", None, None, None),
            P("grp", "sub", None),
            P("grp", "sub"),
            P("grp", "sub"),
            P("grp", "sub"),
            P("grp", "sub"),
            P("grp", "sub"),
            P(ALL, None),
            P(ALL, None),
        ),
        out_specs=(P(ALL, None), P("grp", "sub")),
        check_vma=False,
    )
```

```python
import jax
import jax.numpy as jnp
from jax import lax
from jax.experimental import pallas as pl
from jax.experimental.pallas import tpu as pltpu
from jax.sharding import PartitionSpec as P

F32 = jnp.float32
BF16 = jnp.bfloat16
CHUNK = 16
AHEAD = 10
EDGE = 8
ALL = ("grp", "sub")

VMEM = pl.BlockSpec(memory_space=pltpu.VMEM)
SMEM = pl.BlockSpec(memory_space=pltpu.SMEM)


def total(x):
    return jnp.sum(jnp.sum(x, axis=0, keepdims=True), axis=1, keepdims=True)


def split3(x):
    hi = x.astype(BF16)
    rest = x - hi.astype(F32)
    mid = rest.astype(BF16)
    return hi, mid, (rest - mid.astype(F32)).astype(BF16)


def iota(shape, dim):
    return lax.broadcasted_iota(jnp.int32, shape, dim)


def contract(stiff, cols, vector, terms, arrive=None):
    slots, block_rows, per_row, width, _ = stiff.shape
    squares = []
    for s in range(slots):

        def row(r, acc, s=s):
            if arrive is not None:
                arrive(s, r)
            prod = None
            for n in range(per_row):
                part = stiff[s, r, n] * vector(s, cols[s, n, r])
                prod = part if prod is None else prod + part
            strain = jnp.sum(prod, axis=1, keepdims=True)
            if terms is not None:
                for n in range(per_row):
                    terms[s, pl.ds(n * block_rows + r, 1), :] = jnp.sum(
                        stiff[s, r, n] * strain, axis=0, keepdims=True
                    )
            return acc + strain * strain

        squares.append(lax.fori_loop(0, block_rows, row, jnp.zeros((width, 1), F32), unroll=2))
    return squares


def stacked(gathered, first, count):
    devices, slots = gathered.shape[:2]
    return jnp.concatenate(
        [gathered[d, s, first : first + count, :] for s in range(slots) for d in range(devices)],
        axis=0,
    )


def landed(pack, arrived, block_rows, count):
    devices, slots, _, width = pack.shape
    targets = slots * devices * block_rows
    source = jnp.concatenate(
        [arrived[d, s, :count, :] for d in range(devices) for s in range(slots)], axis=0
    )
    col = jnp.concatenate(
        [pack[d, 0, 2 * block_rows + 1 : 2 * block_rows + 2, :] for d in range(devices)], axis=1
    )
    hot = jnp.where(iota((targets, col.shape[1]), 0).astype(F32) == col, 1.0, 0.0).astype(BF16)
    out = jnp.dot(hot, jnp.concatenate(split3(source), axis=1), preferred_element_type=F32)
    return out[:, :width] + out[:, width : 2 * width] + out[:, 2 * width :]


def prep_kernel(live, diag, pen, load, cols, gload, gdiag, pack):
    slots, rows, width = pack.shape
    block_rows = (rows - 16) // 2
    per_row = cols.shape[1]
    blocks = block_rows * lax.axis_size("sub")
    pack[:, 2 * block_rows :, :] = jnp.zeros((slots, 16, width), F32)
    for s in range(slots):
        count = live[s]
        for b in range(block_rows):
            lanes = pl.ds(b * width, width)
            on = b < count
            main = diag[s : s + 1, lanes]
            if b == 0:
                main = main + pen[s : s + 1, :]
            pack[s, b : b + 1, :] = jnp.where(on, load[s : s + 1, lanes], 0.0)
            pack[s, block_rows + b : block_rows + b + 1, :] = jnp.where(on, main, 0.0)
        pack[s, 2 * block_rows : 2 * block_rows + 1, :] = pen[s : s + 1, :]
        for n in range(per_row):
            at = (s * per_row + n) * block_rows
            pack[0, 2 * block_rows + 1 : 2 * block_rows + 2, at : at + block_rows] = (
                cols[s, n : n + 1, :] + s * blocks
            ).astype(F32)
    last = gload.shape[0] - 1
    half = gload.shape[1] // width
    edge = 2 * block_rows + 8
    for side, picks in enumerate(
        (((gload, 0), (gload, 1), (gdiag, 0)), ((gload, last - 1), (gload, last), (gdiag, last)))
    ):
        for k, (ref, row) in enumerate(picks):
            for h in range(half):
                at = edge + k * half + h
                pack[side, at : at + 1, :] = ref[row : row + 1, h * width : (h + 1) * width]


def first_kernel(cols, pack, source, terms, stiff, sems):
    slots, block_rows = stiff.shape[:2]

    def copy(s, r):
        return pltpu.make_async_copy(source.at[s, r], stiff.at[s, r], sems.at[s, r])

    for i in range(AHEAD):
        copy(i // block_rows, i % block_rows).start()

    def arrive(s, r):
        copy(s, r).wait()
        later = s * block_rows + r + AHEAD

        @pl.when(later < slots * block_rows)
        def _():
            copy(lax.div(later, block_rows), lax.rem(later, block_rows)).start()

    def vector(s, c):
        return pack[lax.div(c, block_rows), s, pl.ds(lax.rem(c, block_rows), 1), :]

    contract(stiff, cols, vector, terms, arrive)


def second_kernel(cols, maps, pack, arrived, stiff, resid, direc, terms, send, xown, pown):
    slots, block_rows, per_row, width, _ = stiff.shape
    devices = pack.shape[0]
    blocks = devices * block_rows
    me = lax.axis_index("sub")
    start = stacked(pack, 0, block_rows)
    dsum = stacked(pack, block_rows, block_rows)
    back = landed(pack, arrived, block_rows, block_rows * per_row)
    image = jnp.where(dsum > 0.0, dsum * start + back, 0.0)
    head, scal = [], []
    for s in range(slots):
        span = slice(s * blocks, (s + 1) * blocks)
        r0, q0 = start[span], image[span]
        norm = total(r0 * r0)
        alpha = norm / total(r0 * q0)
        r1 = r0 - alpha * q0
        norm1 = total(r1 * r1)
        p1 = r1 + norm1 / norm * r0
        resid[span, :] = r1
        direc[span, :] = p1
        scal.append((norm1, total(dsum[span] * p1 * p1)))
        xown[s] = alpha * pack[me, s, :block_rows, :]
        pown[s] = direc[pl.ds(s * blocks + me * block_rows, block_rows), :]
        head.append(pack[me, s, 2 * block_rows : 2 * block_rows + 1, :])
    squares = contract(stiff, cols, lambda s, c: direc[pl.ds(s * blocks + c, 1), :], terms)
    write_send(send, maps, head, [xown[s, 0:1, :] for s in range(slots)], pown, scal, squares, devices)
    everyone, used = send.shape[0], 3 * slots + 1
    group = lax.axis_index("grp")
    groups = everyone // devices
    edge = 2 * block_rows + 8
    send[:, used : used + 1, :] = jnp.zeros((everyone, 1, width), F32)

    @pl.when((group > 0) & (me < 8))
    def _():
        send[group * devices - 1, used : used + 1, :] = pack[0, 0, pl.ds(edge + me, 1), :]

    @pl.when((group < groups - 1) & (me < 8))
    def _():
        send[(group + 1) * devices, used : used + 1, :] = pack[devices - 1, 1, pl.ds(edge + me, 1), :]


def write_send(send, maps, pen, x_face, pown, scal, squares, devices):
    slots, width = len(x_face), x_face[0].shape[1]
    lane = iota((1, width), 1)
    rows = [pen[s] * x_face[s] for s in range(slots)]
    rows += [pen[s] * pown[s, 0:1, :] for s in range(slots)]
    if maps is None:
        rows += [jnp.zeros((slots, width), F32)]
    else:
        rows += [maps[...].astype(F32)]
    row = jnp.zeros((1, width), F32)
    for s in range(slots):
        norm1, own = scal[s]
        image = total(squares[s]) + own * (1.0 / devices)
        row = jnp.where(lane == 2 * s, image, row)
        row = jnp.where(lane == 2 * s + 1, norm1 * (1.0 / devices), row)
    rows.append(row)
    send[:, : 3 * slots + 1, :] = jnp.broadcast_to(
        jnp.concatenate(rows, axis=0)[None], (send.shape[0], 3 * slots + 1, width)
    )


def reactions(got, groups, slots):
    devices, _, width = got.shape
    both = got[:, 3 * slots, :].reshape(groups, devices // groups, width).sum(axis=1)
    alphas, lams = [], []
    for s in range(slots):
        alpha = both[:, 2 * s + 1 : 2 * s + 2] / both[:, 2 * s : 2 * s + 1]
        alpha = jnp.broadcast_to(alpha, (groups, width))
        wide = jnp.broadcast_to(alpha[:, None, :], (groups, devices // groups, width))
        alphas.append(alpha)
        lams.append(got[:, s, :] + wide.reshape(devices, width) * got[:, slots + s, :])
    return alphas, lams


def split_lams(lams, part_s):
    for s, lam in enumerate(lams):
        hi = lam.astype(BF16).astype(F32)
        mid = (lam - hi).astype(BF16).astype(F32)
        part_s[0, s] = hi
        part_s[1, s] = mid
        part_s[2, s] = lam - hi - mid


def lanes_of(ref, d, slots):
    return jnp.concatenate([ref[s, pl.ds(d, 1), :] for s in range(slots)], axis=1)


def place(row_s, part_s, window, hot_of):
    _, slots, devices, _ = part_s.shape
    rows, columns = window
    ids_r = iota((rows, 1), 0).astype(F32)

    def step(c, acc):
        lefts, hots = [], []
        for d in [c * CHUNK + i for i in range(CHUNK)]:
            hit = ids_r == lanes_of(row_s, d, slots)
            lefts.append(
                jnp.concatenate(
                    [jnp.where(hit, lanes_of(part_s.at[i], d, slots), 0.0).astype(BF16) for i in range(3)],
                    axis=0,
                )
            )
            hots.append(hot_of(d))
        return acc + lax.dot_general(
            jnp.concatenate(lefts, axis=1),
            jnp.concatenate(hots, axis=1),
            (((1,), (1,)), ((), ())),
            preferred_element_type=F32,
        )

    acc = lax.fori_loop(0, devices // CHUNK, step, jnp.zeros((3 * rows, columns), F32))
    return acc[:rows] + acc[rows : 2 * rows] + acc[2 * rows :]


def stencil(ref, gdiag, first, count):
    here = ref[first : first + count, :]
    columns = here.shape[1]
    lane = iota(here.shape, 1)
    left = jnp.where(lane == 0, 0.0, pltpu.roll(here, 1, 1))
    right = jnp.where(lane == columns - 1, 0.0, pltpu.roll(here, columns - 1, 1))
    above = ref[first - 1 : first + count - 1, :]
    below = ref[first + 1 : first + count + 1, :]
    return (4.0 + gdiag) * here - (above + below + left + right)


def third_kernel(gload, gdiag, got, pack, window, loads, diags, alphas_out, send, row_s, hot_s, part_s, col_s):
    rows, columns = gload.shape
    slots, devices, width = row_s.shape
    groups = lax.axis_size("grp")
    flat = lax.axis_index("grp") * lax.axis_size("sub") + lax.axis_index("sub")
    first_row = (flat * rows - EDGE).astype(F32)
    alphas, lams = reactions(got, groups, slots)
    for s in range(slots):
        alphas_out[s, 0:groups, :] = alphas[s]
    split_lams(lams, part_s)
    for s in range(slots):
        where = got[:, 2 * slots + s, :]
        row = jnp.floor(where * (1.0 / columns))
        col_s[s] = where - row * columns
        row_s[s] = row - first_row
    me, group = lax.axis_index("sub"), lax.axis_index("grp")
    near = devices // groups
    half, edge, spare = columns // width, pack.shape[2] - 8, 3 * slots + 1
    loads[...] = jnp.zeros_like(loads)
    diags[...] = jnp.zeros_like(diags)
    loads[EDGE : EDGE + rows, :] = gload[...]
    diags[EDGE : EDGE + rows, :] = gdiag[...]
    last = EDGE + rows

    def fill(side, row_of):
        first = EDGE - 2 if side else last
        diag_row = EDGE - 1 if side else last
        for h in range(half):
            lanes = slice(h * width, (h + 1) * width)
            loads[first : first + 1, lanes] = row_of(h)
            loads[first + 1 : first + 2, lanes] = row_of(half + h)
            diags[diag_row : diag_row + 1, lanes] = row_of(2 * half + h)

    @pl.when(me > 0)
    def _():
        fill(1, lambda k: pack[me - 1, 1, edge + k : edge + k + 1, :])

    @pl.when((me == 0) & (group > 0))
    def _():
        fill(1, lambda k: got[(group - 1) * near + k, spare : spare + 1, :])

    @pl.when(me < near - 1)
    def _():
        fill(0, lambda k: pack[me + 1, 0, edge + k : edge + k + 1, :])

    @pl.when((me == near - 1) & (group < groups - 1))
    def _():
        fill(0, lambda k: got[(group + 1) * near + k, spare : spare + 1, :])

    extent = window.shape
    ids_c = iota((columns, 1), 0).astype(F32)

    def hot_of(d):
        hot = jnp.where(ids_c == lanes_of(col_s, d, slots), 1.0, 0.0).astype(BF16)
        hot_s[d] = hot
        return hot

    placed = place(row_s, part_s, extent, hot_of)
    at = iota(extent, 0)
    inside = (at >= EDGE - 2) & (at < last + 2)
    window[...] = loads[...] + jnp.where(inside, placed, 0.0)
    own = window[EDGE:last, :]
    image = stencil(window, gdiag[...], EDGE, rows)
    send[:, slots : slots + 1, :] = jnp.broadcast_to(total(own * own)[None], (devices, 1, width))
    send[:, slots + 1 : slots + 2, :] = jnp.broadcast_to(total(own * image)[None], (devices, 1, width))
    parts = jnp.concatenate(split3(own), axis=0)
    ids = iota((rows, 1), 0).astype(F32) + EDGE

    def step(d, carry):
        seen = jnp.dot(parts, hot_s[d], preferred_element_type=F32)
        seen = seen[:rows] + seen[rows : 2 * rows] + seen[2 * rows :]
        hit = ids == lanes_of(row_s, d, slots)
        mine = jnp.sum(jnp.where(hit, seen, 0.0), axis=0, keepdims=True)
        for s in range(slots):
            send[d, s : s + 1, :] = mine[:, s * width : (s + 1) * width]
        return carry

    lax.fori_loop(0, devices, step, 0, unroll=8)


def scale_kernel(got, terms, window, send, field):
    slots, count, width = terms.shape
    sums = jnp.sum(got[...], axis=0)
    scale = sums[slots : slots + 1, :] / sums[slots + 1 : slots + 2, :]
    send[:, :count, :] = terms[...]
    send[:, count:, :] = jnp.zeros((slots, send.shape[1] - count, width), F32)
    for s in range(slots):
        send[s, count : count + 1, :] = scale * sums[s : s + 1, :]
    field[...] = window[...] * jnp.concatenate([scale] * (field.shape[1] // width), axis=1)


def fourth_kernel(cols, pack, arrived, alphas, resid, direc, xown, pown, stiff, start, terms, xnext):
    slots, block_rows, per_row, width, _ = stiff.shape
    devices = pack.shape[0]
    blocks = devices * block_rows
    count = block_rows * per_row
    group = lax.axis_index("grp")
    dsum = stacked(pack, block_rows, block_rows)
    back = landed(pack, arrived, block_rows, count)
    p1 = direc[...]
    image = jnp.where(dsum > 0.0, dsum * p1 + back, 0.0)
    for s in range(slots):
        span = slice(s * blocks, (s + 1) * blocks)
        alpha = alphas[s, pl.ds(group, 1), :]
        start[span, :] = resid[span, :] - alpha * image[span]
        xnext[s] = xown[s] + alpha * pown[s]
        for d in range(devices):
            face = slice(s * blocks + d * block_rows, s * blocks + d * block_rows + 1)
            pen = pack[d, s, 2 * block_rows : 2 * block_rows + 1, :]
            start[face, :] = start[face, :] + pen * arrived[d, s, count : count + 1, :]
    contract(stiff, cols, lambda s, c: start[pl.ds(s * blocks + c, 1), :], terms)


def fifth_kernel(cols, pack, arrived, bound, start, xin, stiff, send, xown, pown, direc):
    slots, block_rows, per_row, width, _ = stiff.shape
    devices = pack.shape[0]
    blocks = devices * block_rows
    count = block_rows * per_row
    me = lax.axis_index("sub")
    dsum = stacked(pack, block_rows, block_rows)
    back = landed(pack, arrived, block_rows, count)
    image = jnp.where(dsum > 0.0, dsum * start[...] + back, 0.0)
    head, face, scal = [], [], []
    for s in range(slots):
        span = slice(s * blocks, (s + 1) * blocks)
        r0, q0 = start[span, :], image[span]
        norm = total(r0 * r0)
        alpha = norm / total(r0 * q0)
        r1 = r0 - alpha * q0
        norm1 = total(r1 * r1)
        p1 = r1 + norm1 / norm * r0
        direc[span, :] = p1
        scal.append((norm1, total(dsum[span] * p1 * p1)))
        mine = pl.ds(s * blocks + me * block_rows, block_rows)
        xown[s] = xin[s] + alpha * start[mine, :]
        pown[s] = direc[mine, :]
        head.append(pack[me, s, 2 * block_rows : 2 * block_rows + 1, :])
        face.append(xown[s, 0:1, :] - bound[s, count : count + 1, :])
    squares = contract(stiff, cols, lambda s, c: direc[pl.ds(s * blocks + c, 1), :], None)
    write_send(send, None, head, face, pown, scal, squares, devices)


def sixth_kernel(got, loads, diags, field, xown, pown, row_s, hot_s, resid, xout, send, window, part_s):
    slots, devices, width = row_s.shape
    rows, columns = resid.shape
    groups = lax.axis_size("grp")
    group = lax.axis_index("grp")
    flat = group * lax.axis_size("sub") + lax.axis_index("sub")
    alphas, lams = reactions(got, groups, slots)
    for s in range(slots):
        part_s[0, s, 0:groups, :] = alphas[s]
        alpha = part_s[0, s, pl.ds(group, 1), :]
        for b in range(xown.shape[1]):
            xout[s : s + 1, b * width : (b + 1) * width] = (
                xown[s, b : b + 1, :] + alpha * pown[s, b : b + 1, :]
            )
    split_lams(lams, part_s)
    placed = place(row_s, part_s, window.shape, lambda d: hot_s[d])
    span = slice(EDGE - 1, EDGE + rows + 1)
    applied = stencil(field, diags[span, :], EDGE - 1, rows + 2)
    at = iota(applied.shape, 0) + (flat * rows - 1)
    inside = (at >= 0) & (at < devices * rows)
    window[...] = jnp.zeros_like(window)
    window[span, :] = jnp.where(inside, loads[span, :] - applied + placed[span], 0.0)
    own = window[EDGE : EDGE + rows, :]
    resid[...] = own
    image = stencil(window, diags[EDGE : EDGE + rows, :], EDGE, rows)
    send[:, 0:1, :] = jnp.broadcast_to(total(own * own)[None], (devices, 1, width))
    send[:, 1:2, :] = jnp.broadcast_to(total(own * image)[None], (devices, 1, width))


def last_kernel(got, field, resid, out):
    sums = jnp.sum(got[...], axis=0)
    scale = sums[0:1, :] / sums[1:2, :]
    rows, columns = out.shape
    wide = jnp.concatenate([scale] * (columns // got.shape[2]), axis=1)
    out[...] = field[EDGE : EDGE + rows, :] + wide * resid[...]


def call(kernel, shapes, operands, scalars=0, raw=0, scratch=(), limit=4, plain=()):
    operands = [
        x if i < scalars else pltpu.with_memory_space_constraint(x, pltpu.HBM if i < scalars + raw else pltpu.VMEM)
        for i, x in enumerate(operands)
    ]
    out_shape = [
        jax.ShapeDtypeStruct(s, d) if i in plain else pltpu.VMEM(s, d) for i, (s, d) in enumerate(shapes)
    ]
    return pl.pallas_call(
        kernel,
        out_shape=out_shape,
        in_specs=[SMEM] * scalars + [VMEM] * (len(operands) - scalars),
        out_specs=[VMEM] * len(shapes),
        scratch_shapes=list(scratch),
        compiler_params=pltpu.CompilerParams(vmem_limit_bytes=limit << 20),
    )(*operands)


def body(
    stiff_blocks,
    block_cols,
    live_blocks,
    sub_diag,
    penalty,
    sub_load,
    iface_map,
    global_load,
    global_diag,
):
    slots, block_rows, per_row, width, _ = stiff_blocks.shape
    rows_dev = block_rows * width
    rows, columns = global_load.shape
    near, groups = lax.axis_size("sub"), lax.axis_size("grp")
    devices = near * groups
    blocks = slots * near * block_rows
    count = block_rows * per_row
    extent = ((rows + 2 * EDGE, columns), F32)
    own = ((slots, block_rows, width), F32)
    full = ((blocks, width), F32)
    every = ((slots, count, width), F32)
    cols = jnp.transpose(block_cols, (0, 2, 1))

    def everywhere(x):
        return lax.all_to_all(x, ALL, 0, 0)

    def near_all(x):
        return lax.all_gather(x, "sub")

    (pack,) = call(
        prep_kernel,
        [((slots, 2 * block_rows + 16, width), F32)],
        (live_blocks.reshape(slots), sub_diag, penalty, sub_load, cols, global_load, global_diag),
        scalars=1,
        raw=6,
    )
    pack = near_all(pack)
    terms, stiff = pl.pallas_call(
        first_kernel,
        out_shape=[pltpu.VMEM(every[0], F32), pltpu.VMEM(stiff_blocks.shape, F32)],
        in_specs=[SMEM, VMEM, pl.BlockSpec(memory_space=pltpu.HBM)],
        out_specs=[VMEM, VMEM],
        scratch_shapes=[pltpu.SemaphoreType.DMA((slots, block_rows))],
        compiler_params=pltpu.CompilerParams(vmem_limit_bytes=4 << 20),
    )(
        cols,
        pltpu.with_memory_space_constraint(pack, pltpu.VMEM),
        pltpu.with_memory_space_constraint(stiff_blocks, pltpu.HBM),
    )
    arrived = near_all(terms)
    resid, direc, terms, send, xown, pown = call(
        second_kernel,
        [full, full, every, ((devices, 4 * slots, width), F32), own, own],
        (cols, iface_map, pack, arrived, stiff),
        scalars=1,
        raw=1,
    )
    got = everywhere(send)
    listed = (slots, devices, width)
    parts = pltpu.VMEM((3,) + listed, F32)
    window, loads, diags, alphas, send, row_s, hot_s = call(
        third_kernel,
        [
            extent,
            extent,
            extent,
            ((slots, max(8, groups), width), F32),
            ((devices, slots + 2, width), F32),
            (listed, F32),
            ((devices, columns, slots * width), BF16),
        ],
        (global_load, global_diag, got, pack),
        raw=2,
        scratch=(parts, pltpu.VMEM(listed, F32)),
    )
    sums = everywhere(send)
    bound, field = call(
        scale_kernel, [((slots, count + 8, width), F32), extent], (sums, terms, window)
    )
    arrived = near_all(bound)
    start, terms, xown = call(
        fourth_kernel,
        [full, every, own],
        (cols, pack, arrived, alphas, resid, direc, xown, pown, stiff),
        scalars=1,
    )
    arrived = near_all(terms)
    send, xown, pown = call(
        fifth_kernel,
        [((devices, 4 * slots, width), F32), own, own],
        (cols, pack, arrived, bound, start, xown, stiff),
        scalars=1,
        scratch=(pltpu.VMEM(full[0], F32),),
    )
    got = everywhere(send)
    resid, sub_field, send = call(
        sixth_kernel,
        [((rows, columns), F32), ((slots, rows_dev), F32), ((devices, 2, width), F32)],
        (got, loads, diags, field, xown, pown, row_s, hot_s),
        scratch=(pltpu.VMEM(extent[0], F32), parts),
        plain=(1,),
    )
    sums = everywhere(send)
    (global_field,) = call(last_kernel, [((rows, columns), F32)], (sums, field, resid), plain=(0,))
    return global_field, sub_field


def solution(mesh):
    return jax.shard_map(
        body,
        mesh=mesh,
        in_specs=(
            P("grp", "sub", None, None, None),
            P("grp", "sub", None),
            P("grp", "sub"),
            P("grp", "sub"),
            P("grp", "sub"),
            P("grp", "sub"),
            P("grp", "sub"),
            P(ALL, None),
            P(ALL, None),
        ),
        out_specs=(P(ALL, None), P("grp", "sub")),
        check_vma=False,
    )
```

```python
import jax
import jax.numpy as jnp
from jax import lax
from jax.experimental import pallas as pl
from jax.experimental.pallas import tpu as pltpu
from jax.sharding import PartitionSpec as P

F32 = jnp.float32
BF16 = jnp.bfloat16
CHUNK = 16
EDGE = 8
ALL = ("grp", "sub")

VMEM = pl.BlockSpec(memory_space=pltpu.VMEM)
SMEM = pl.BlockSpec(memory_space=pltpu.SMEM)


def total(x):
    return jnp.sum(jnp.sum(x, axis=0, keepdims=True), axis=1, keepdims=True)


def split3(x):
    hi = x.astype(BF16)
    rest = x - hi.astype(F32)
    mid = rest.astype(BF16)
    return hi, mid, (rest - mid.astype(F32)).astype(BF16)


def iota(shape, dim):
    return lax.broadcasted_iota(jnp.int32, shape, dim)


def contract(stiff, cols, vector, terms, arrive=None):
    slots, block_rows, per_row, width, _ = stiff.shape
    squares = []
    for s in range(slots):

        def row(r, acc, s=s):
            if arrive is not None:
                arrive(s, r)
            prod = None
            for n in range(per_row):
                part = stiff[s, r, n] * vector(s, cols[s, n, r])
                prod = part if prod is None else prod + part
            strain = jnp.sum(prod, axis=1, keepdims=True)
            if terms is not None:
                for n in range(per_row):
                    terms[s, pl.ds(n * block_rows + r, 1), :] = jnp.sum(
                        stiff[s, r, n] * strain, axis=0, keepdims=True
                    )
            return acc + strain * strain

        acc = jnp.zeros((width, 1), F32)
        for r in range(block_rows):
            acc = row(r, acc)
        squares.append(acc)
    return squares


def stacked(gathered, first, count):
    devices, slots = gathered.shape[:2]
    return jnp.concatenate(
        [gathered[d, s, first : first + count, :] for s in range(slots) for d in range(devices)],
        axis=0,
    )


def targets(pack, block_rows, hot):
    devices = pack.shape[0]
    col = jnp.concatenate(
        [pack[d, 0, 2 * block_rows + 1 : 2 * block_rows + 2, :] for d in range(devices)], axis=1
    )
    hot[...] = jnp.where(iota(hot.shape, 0).astype(F32) == col, 1.0, 0.0).astype(BF16)


def landed(hot, arrived, count):
    devices, slots, _, width = arrived.shape
    source = jnp.concatenate(
        [arrived[d, s, :count, :] for d in range(devices) for s in range(slots)], axis=0
    )
    out = jnp.dot(hot[...], jnp.concatenate(split3(source), axis=1), preferred_element_type=F32)
    return out[:, :width] + out[:, width : 2 * width] + out[:, 2 * width :]


def prep_kernel(live, diag, pen, load, cols, gload, gdiag, pack):
    slots, rows, width = pack.shape
    block_rows = (rows - 16) // 2
    per_row = cols.shape[1]
    blocks = block_rows * lax.axis_size("sub")
    pack[:, 2 * block_rows :, :] = jnp.zeros((slots, 16, width), F32)
    for s in range(slots):
        count = live[:, s : s + 1]
        for b in range(block_rows):
            lanes = pl.ds(b * width, width)
            on = count > b
            main = diag[s : s + 1, lanes]
            if b == 0:
                main = main + pen[s : s + 1, :]
            pack[s, b : b + 1, :] = jnp.where(on, load[s : s + 1, lanes], 0.0)
            pack[s, block_rows + b : block_rows + b + 1, :] = jnp.where(on, main, 0.0)
        pack[s, 2 * block_rows : 2 * block_rows + 1, :] = pen[s : s + 1, :]
        for n in range(per_row):
            at = (s * per_row + n) * block_rows
            pack[0, 2 * block_rows + 1 : 2 * block_rows + 2, at : at + block_rows] = (
                cols[s, n : n + 1, :] + s * blocks
            ).astype(F32)
    last = gload.shape[0] - 1
    half = gload.shape[1] // width
    edge = 2 * block_rows + 8
    for side, picks in enumerate(
        (((gload, 0), (gload, 1), (gdiag, 0)), ((gload, last - 1), (gload, last), (gdiag, last)))
    ):
        for k, (ref, row) in enumerate(picks):
            for h in range(half):
                at = edge + k * half + h
                pack[side, at : at + 1, :] = ref[row : row + 1, h * width : (h + 1) * width]


def first_kernel(cols, pack, source, terms, stiff, sems):
    slots, block_rows = stiff.shape[:2]

    def copy(s, r):
        return pltpu.make_async_copy(source.at[s, r], stiff.at[s, r], sems.at[s, r])

    for s in range(slots):
        for r in range(block_rows):
            copy(s, r).start()

    def vector(s, c):
        return pack[lax.div(c, block_rows), s, pl.ds(lax.rem(c, block_rows), 1), :]

    contract(stiff, cols, vector, terms, lambda s, r: copy(s, r).wait())


def second_kernel(cols, maps, pack, arrived, stiff, resid, direc, terms, send, xown, pown, hot):
    slots, block_rows, per_row, width, _ = stiff.shape
    devices = pack.shape[0]
    blocks = devices * block_rows
    me = lax.axis_index("sub")
    start = stacked(pack, 0, block_rows)
    dsum = stacked(pack, block_rows, block_rows)
    targets(pack, block_rows, hot)
    back = landed(hot, arrived, block_rows * per_row)
    image = jnp.where(dsum > 0.0, dsum * start + back, 0.0)
    head, scal = [], []
    for s in range(slots):
        span = slice(s * blocks, (s + 1) * blocks)
        r0, q0 = start[span], image[span]
        norm = total(r0 * r0)
        alpha = norm / total(r0 * q0)
        r1 = r0 - alpha * q0
        norm1 = total(r1 * r1)
        p1 = r1 + norm1 / norm * r0
        resid[span, :] = r1
        direc[span, :] = p1
        scal.append((norm1, total(dsum[span] * p1 * p1)))
        xown[s] = alpha * pack[me, s, :block_rows, :]
        pown[s] = direc[pl.ds(s * blocks + me * block_rows, block_rows), :]
        head.append(pack[me, s, 2 * block_rows : 2 * block_rows + 1, :])
    squares = contract(stiff, cols, lambda s, c: direc[pl.ds(s * blocks + c, 1), :], terms)
    write_send(send, maps, head, [xown[s, 0:1, :] for s in range(slots)], pown, scal, squares, devices)
    everyone, used = send.shape[0], 3 * slots + 1
    group = lax.axis_index("grp")
    groups = everyone // devices
    edge = 2 * block_rows + 8
    send[:, used : used + 1, :] = jnp.zeros((everyone, 1, width), F32)

    @pl.when((group > 0) & (me < 8))
    def _():
        send[group * devices - 1, used : used + 1, :] = pack[0, 0, pl.ds(edge + me, 1), :]

    @pl.when((group < groups - 1) & (me < 8))
    def _():
        send[(group + 1) * devices, used : used + 1, :] = pack[devices - 1, 1, pl.ds(edge + me, 1), :]


def write_send(send, maps, pen, x_face, pown, scal, squares, devices):
    slots, width = len(x_face), x_face[0].shape[1]
    lane = iota((1, width), 1)
    rows = [pen[s] * x_face[s] for s in range(slots)]
    rows += [pen[s] * pown[s, 0:1, :] for s in range(slots)]
    if maps is None:
        rows += [jnp.zeros((slots, width), F32)]
    else:
        rows += [maps[...].astype(F32)]
    row = jnp.zeros((1, width), F32)
    for s in range(slots):
        norm1, own = scal[s]
        image = total(squares[s]) + own * (1.0 / devices)
        row = jnp.where(lane == 2 * s, image, row)
        row = jnp.where(lane == 2 * s + 1, norm1 * (1.0 / devices), row)
    rows.append(row)
    send[:, : 3 * slots + 1, :] = jnp.broadcast_to(
        jnp.concatenate(rows, axis=0)[None], (send.shape[0], 3 * slots + 1, width)
    )


def reactions(got, groups, slots):
    devices, _, width = got.shape
    both = got[:, 3 * slots, :].reshape(groups, devices // groups, width).sum(axis=1)
    alphas, lams = [], []
    for s in range(slots):
        alpha = both[:, 2 * s + 1 : 2 * s + 2] / both[:, 2 * s : 2 * s + 1]
        alpha = jnp.broadcast_to(alpha, (groups, width))
        wide = jnp.broadcast_to(alpha[:, None, :], (groups, devices // groups, width))
        alphas.append(alpha)
        lams.append(got[:, s, :] + wide.reshape(devices, width) * got[:, slots + s, :])
    return alphas, lams


def split_lams(lams, part_s):
    for s, lam in enumerate(lams):
        hi = lam.astype(BF16).astype(F32)
        mid = (lam - hi).astype(BF16).astype(F32)
        part_s[0, s] = hi
        part_s[1, s] = mid
        part_s[2, s] = lam - hi - mid


def lanes_of(ref, d, slots):
    return jnp.concatenate([ref[s, pl.ds(d, 1), :] for s in range(slots)], axis=1)


def place(row_s, part_s, window, hot_of):
    _, slots, devices, _ = part_s.shape
    rows, columns = window
    ids_r = iota((rows, 1), 0).astype(F32)

    def step(c, acc):
        lefts, hots = [], []
        for d in [c * CHUNK + i for i in range(CHUNK)]:
            hit = ids_r == lanes_of(row_s, d, slots)
            lefts.append(
                jnp.concatenate(
                    [jnp.where(hit, lanes_of(part_s.at[i], d, slots), 0.0).astype(BF16) for i in range(3)],
                    axis=0,
                )
            )
            hots.append(hot_of(d))
        return acc + lax.dot_general(
            jnp.concatenate(lefts, axis=1),
            jnp.concatenate(hots, axis=1),
            (((1,), (1,)), ((), ())),
            preferred_element_type=F32,
        )

    acc = lax.fori_loop(0, devices // CHUNK, step, jnp.zeros((3 * rows, columns), F32))
    return acc[:rows] + acc[rows : 2 * rows] + acc[2 * rows :]


def stencil(ref, gdiag, first, count):
    here = ref[first : first + count, :]
    columns = here.shape[1]
    lane = iota(here.shape, 1)
    left = jnp.where(lane == 0, 0.0, pltpu.roll(here, 1, 1))
    right = jnp.where(lane == columns - 1, 0.0, pltpu.roll(here, columns - 1, 1))
    above = ref[first - 1 : first + count - 1, :]
    below = ref[first + 1 : first + count + 1, :]
    return (4.0 + gdiag) * here - (above + below + left + right)


def third_kernel(gload, gdiag, got, pack, window, loads, diags, alphas_out, send, row_s, hot_s, part_s, col_s):
    rows, columns = gload.shape
    slots, devices, width = row_s.shape
    groups = lax.axis_size("grp")
    flat = lax.axis_index("grp") * lax.axis_size("sub") + lax.axis_index("sub")
    first_row = (flat * rows - EDGE).astype(F32)
    alphas, lams = reactions(got, groups, slots)
    for s in range(slots):
        alphas_out[s, 0:groups, :] = alphas[s]
    split_lams(lams, part_s)
    for s in range(slots):
        where = got[:, 2 * slots + s, :]
        row = jnp.floor(where * (1.0 / columns))
        col_s[s] = where - row * columns
        row_s[s] = row - first_row
    me, group = lax.axis_index("sub"), lax.axis_index("grp")
    near = devices // groups
    half, edge, spare = columns // width, pack.shape[2] - 8, 3 * slots + 1
    loads[...] = jnp.zeros_like(loads)
    diags[...] = jnp.zeros_like(diags)
    loads[EDGE : EDGE + rows, :] = gload[...]
    diags[EDGE : EDGE + rows, :] = gdiag[...]
    last = EDGE + rows

    def fill(side, row_of):
        first = EDGE - 2 if side else last
        diag_row = EDGE - 1 if side else last
        for h in range(half):
            lanes = slice(h * width, (h + 1) * width)
            loads[first : first + 1, lanes] = row_of(h)
            loads[first + 1 : first + 2, lanes] = row_of(half + h)
            diags[diag_row : diag_row + 1, lanes] = row_of(2 * half + h)

    @pl.when(me > 0)
    def _():
        fill(1, lambda k: pack[me - 1, 1, edge + k : edge + k + 1, :])

    @pl.when((me == 0) & (group > 0))
    def _():
        fill(1, lambda k: got[(group - 1) * near + k, spare : spare + 1, :])

    @pl.when(me < near - 1)
    def _():
        fill(0, lambda k: pack[me + 1, 0, edge + k : edge + k + 1, :])

    @pl.when((me == near - 1) & (group < groups - 1))
    def _():
        fill(0, lambda k: got[(group + 1) * near + k, spare : spare + 1, :])

    extent = window.shape
    ids_c = iota((columns, 1), 0).astype(F32)

    def hot_of(d):
        hot = jnp.where(ids_c == lanes_of(col_s, d, slots), 1.0, 0.0).astype(BF16)
        hot_s[d] = hot
        return hot

    placed = place(row_s, part_s, extent, hot_of)
    at = iota(extent, 0)
    inside = (at >= EDGE - 2) & (at < last + 2)
    window[...] = loads[...] + jnp.where(inside, placed, 0.0)
    own = window[EDGE:last, :]
    image = stencil(window, gdiag[...], EDGE, rows)
    send[:, slots : slots + 1, :] = jnp.broadcast_to(total(own * own)[None], (devices, 1, width))
    send[:, slots + 1 : slots + 2, :] = jnp.broadcast_to(total(own * image)[None], (devices, 1, width))
    parts = jnp.concatenate(split3(own), axis=0)
    ids = iota((rows, 1), 0).astype(F32) + EDGE

    def step(d, carry):
        seen = jnp.dot(parts, hot_s[d], preferred_element_type=F32)
        seen = seen[:rows] + seen[rows : 2 * rows] + seen[2 * rows :]
        hit = ids == lanes_of(row_s, d, slots)
        mine = jnp.sum(jnp.where(hit, seen, 0.0), axis=0, keepdims=True)
        for s in range(slots):
            send[d, s : s + 1, :] = mine[:, s * width : (s + 1) * width]
        return carry

    lax.fori_loop(0, devices, step, 0, unroll=8)


def scale_kernel(got, terms, window, send, field):
    slots, count, width = terms.shape
    sums = jnp.sum(got[...], axis=0)
    scale = sums[slots : slots + 1, :] / sums[slots + 1 : slots + 2, :]
    send[:, :count, :] = terms[...]
    send[:, count:, :] = jnp.zeros((slots, send.shape[1] - count, width), F32)
    for s in range(slots):
        send[s, count : count + 1, :] = scale * sums[s : s + 1, :]
    field[...] = window[...] * jnp.concatenate([scale] * (field.shape[1] // width), axis=1)


def fourth_kernel(cols, pack, arrived, hot, alphas, resid, direc, xown, pown, stiff, start, terms, xnext):
    slots, block_rows, per_row, width, _ = stiff.shape
    devices = pack.shape[0]
    blocks = devices * block_rows
    count = block_rows * per_row
    group = lax.axis_index("grp")
    dsum = stacked(pack, block_rows, block_rows)
    back = landed(hot, arrived, count)
    p1 = direc[...]
    image = jnp.where(dsum > 0.0, dsum * p1 + back, 0.0)
    for s in range(slots):
        span = slice(s * blocks, (s + 1) * blocks)
        alpha = alphas[s, pl.ds(group, 1), :]
        start[span, :] = resid[span, :] - alpha * image[span]
        xnext[s] = xown[s] + alpha * pown[s]
        for d in range(devices):
            face = slice(s * blocks + d * block_rows, s * blocks + d * block_rows + 1)
            pen = pack[d, s, 2 * block_rows : 2 * block_rows + 1, :]
            start[face, :] = start[face, :] + pen * arrived[d, s, count : count + 1, :]
    contract(stiff, cols, lambda s, c: start[pl.ds(s * blocks + c, 1), :], terms)


def fifth_kernel(cols, pack, arrived, hot, bound, start, xin, stiff, send, xown, pown, direc):
    slots, block_rows, per_row, width, _ = stiff.shape
    devices = pack.shape[0]
    blocks = devices * block_rows
    count = block_rows * per_row
    me = lax.axis_index("sub")
    dsum = stacked(pack, block_rows, block_rows)
    back = landed(hot, arrived, count)
    image = jnp.where(dsum > 0.0, dsum * start[...] + back, 0.0)
    head, face, scal = [], [], []
    for s in range(slots):
        span = slice(s * blocks, (s + 1) * blocks)
        r0, q0 = start[span, :], image[span]
        norm = total(r0 * r0)
        alpha = norm / total(r0 * q0)
        r1 = r0 - alpha * q0
        norm1 = total(r1 * r1)
        p1 = r1 + norm1 / norm * r0
        direc[span, :] = p1
        scal.append((norm1, total(dsum[span] * p1 * p1)))
        mine = pl.ds(s * blocks + me * block_rows, block_rows)
        xown[s] = xin[s] + alpha * start[mine, :]
        pown[s] = direc[mine, :]
        head.append(pack[me, s, 2 * block_rows : 2 * block_rows + 1, :])
        face.append(xown[s, 0:1, :] - bound[s, count : count + 1, :])
    squares = contract(stiff, cols, lambda s, c: direc[pl.ds(s * blocks + c, 1), :], None)
    write_send(send, None, head, face, pown, scal, squares, devices)


def sixth_kernel(got, loads, diags, field, xown, pown, row_s, hot_s, resid, xout, send, window, part_s):
    slots, devices, width = row_s.shape
    rows, columns = resid.shape
    groups = lax.axis_size("grp")
    group = lax.axis_index("grp")
    flat = group * lax.axis_size("sub") + lax.axis_index("sub")
    alphas, lams = reactions(got, groups, slots)
    for s in range(slots):
        part_s[0, s, 0:groups, :] = alphas[s]
        alpha = part_s[0, s, pl.ds(group, 1), :]
        for b in range(xown.shape[1]):
            xout[s : s + 1, b * width : (b + 1) * width] = (
                xown[s, b : b + 1, :] + alpha * pown[s, b : b + 1, :]
            )
    split_lams(lams, part_s)
    placed = place(row_s, part_s, window.shape, lambda d: hot_s[d])
    span = slice(EDGE - 1, EDGE + rows + 1)
    applied = stencil(field, diags[span, :], EDGE - 1, rows + 2)
    at = iota(applied.shape, 0) + (flat * rows - 1)
    inside = (at >= 0) & (at < devices * rows)
    window[...] = jnp.zeros_like(window)
    window[span, :] = jnp.where(inside, loads[span, :] - applied + placed[span], 0.0)
    own = window[EDGE : EDGE + rows, :]
    resid[...] = own
    image = stencil(window, diags[EDGE : EDGE + rows, :], EDGE, rows)
    send[:, 0:1, :] = jnp.broadcast_to(total(own * own)[None], (devices, 1, width))
    send[:, 1:2, :] = jnp.broadcast_to(total(own * image)[None], (devices, 1, width))


def last_kernel(got, field, resid, out):
    sums = jnp.sum(got[...], axis=0)
    scale = sums[0:1, :] / sums[1:2, :]
    rows, columns = out.shape
    wide = jnp.concatenate([scale] * (columns // got.shape[2]), axis=1)
    out[...] = field[EDGE : EDGE + rows, :] + wide * resid[...]


def call(kernel, shapes, operands, scalars=0, raw=0, scratch=(), limit=4, plain=()):
    operands = [
        pltpu.with_memory_space_constraint(x, pltpu.HBM if i < scalars + raw else pltpu.VMEM)
        for i, x in enumerate(operands)
    ]
    out_shape = [
        jax.ShapeDtypeStruct(s, d) if i in plain else pltpu.VMEM(s, d) for i, (s, d) in enumerate(shapes)
    ]
    return pl.pallas_call(
        kernel,
        out_shape=out_shape,
        in_specs=[SMEM] * scalars + [VMEM] * (len(operands) - scalars),
        out_specs=[VMEM] * len(shapes),
        scratch_shapes=list(scratch),
        compiler_params=pltpu.CompilerParams(vmem_limit_bytes=limit << 20),
    )(*operands)


def body(
    stiff_blocks,
    block_cols,
    live_blocks,
    sub_diag,
    penalty,
    sub_load,
    iface_map,
    global_load,
    global_diag,
):
    slots, block_rows, per_row, width, _ = stiff_blocks.shape
    rows_dev = block_rows * width
    rows, columns = global_load.shape
    near, groups = lax.axis_size("sub"), lax.axis_size("grp")
    devices = near * groups
    blocks = slots * near * block_rows
    count = block_rows * per_row
    extent = ((rows + 2 * EDGE, columns), F32)
    own = ((slots, block_rows, width), F32)
    full = ((blocks, width), F32)
    every = ((slots, count, width), F32)
    landing = ((blocks, near * slots * count), BF16)
    cols = jnp.transpose(block_cols, (0, 2, 1))

    def everywhere(x):
        return lax.all_to_all(x, ALL, 0, 0)

    def near_all(x):
        return lax.all_gather(x, "sub")

    (pack,) = call(
        prep_kernel,
        [((slots, 2 * block_rows + 16, width), F32)],
        (live_blocks.reshape(1, slots), sub_diag, penalty, sub_load, cols, global_load, global_diag),
        raw=7,
    )
    pack = near_all(pack)
    terms, stiff = pl.pallas_call(
        first_kernel,
        out_shape=[pltpu.VMEM(every[0], F32), pltpu.VMEM(stiff_blocks.shape, F32)],
        in_specs=[SMEM, VMEM, pl.BlockSpec(memory_space=pltpu.HBM)],
        out_specs=[VMEM, VMEM],
        scratch_shapes=[pltpu.SemaphoreType.DMA((slots, block_rows))],
        compiler_params=pltpu.CompilerParams(vmem_limit_bytes=4 << 20),
    )(
        pltpu.with_memory_space_constraint(cols, pltpu.HBM),
        pltpu.with_memory_space_constraint(pack, pltpu.VMEM),
        pltpu.with_memory_space_constraint(stiff_blocks, pltpu.HBM),
    )
    arrived = near_all(terms)
    resid, direc, terms, send, xown, pown, hot = call(
        second_kernel,
        [full, full, every, ((devices, 4 * slots, width), F32), own, own, landing],
        (cols, iface_map, pack, arrived, stiff),
        scalars=1,
        raw=1,
    )
    got = everywhere(send)
    listed = (slots, devices, width)
    parts = pltpu.VMEM((3,) + listed, F32)
    window, loads, diags, alphas, send, row_s, hot_s = call(
        third_kernel,
        [
            extent,
            extent,
            extent,
            ((slots, max(8, groups), width), F32),
            ((devices, slots + 2, width), F32),
            (listed, F32),
            ((devices, columns, slots * width), BF16),
        ],
        (global_load, global_diag, got, pack),
        raw=2,
        scratch=(parts, pltpu.VMEM(listed, F32)),
    )
    sums = everywhere(send)
    bound, field = call(
        scale_kernel, [((slots, count + 8, width), F32), extent], (sums, terms, window)
    )
    arrived = near_all(bound)
    start, terms, xown = call(
        fourth_kernel,
        [full, every, own],
        (cols, pack, arrived, hot, alphas, resid, direc, xown, pown, stiff),
        scalars=1,
    )
    arrived = near_all(terms)
    send, xown, pown = call(
        fifth_kernel,
        [((devices, 4 * slots, width), F32), own, own],
        (cols, pack, arrived, hot, bound, start, xown, stiff),
        scalars=1,
        scratch=(pltpu.VMEM(full[0], F32),),
    )
    got = everywhere(send)
    resid, sub_field, send = call(
        sixth_kernel,
        [((rows, columns), F32), ((slots, rows_dev), F32), ((devices, 2, width), F32)],
        (got, loads, diags, field, xown, pown, row_s, hot_s),
        scratch=(pltpu.VMEM(extent[0], F32), parts),
        plain=(1,),
    )
    sums = everywhere(send)
    (global_field,) = call(last_kernel, [((rows, columns), F32)], (sums, field, resid), plain=(0,))
    return global_field, sub_field


def solution(mesh):
    return jax.shard_map(
        body,
        mesh=mesh,
        in_specs=(
            P("grp", "sub", None, None, None),
            P("grp", "sub", None),
            P("grp", "sub"),
            P("grp", "sub"),
            P("grp", "sub"),
            P("grp", "sub"),
            P("grp", "sub"),
            P(ALL, None),
            P(ALL, None),
        ),
        out_specs=(P(ALL, None), P("grp", "sub")),
        check_vma=False,
    )
```

```python
import jax
import jax.numpy as jnp
from jax import lax
from jax.experimental import pallas as pl
from jax.experimental.pallas import tpu as pltpu
from jax.sharding import PartitionSpec as P

F32 = jnp.float32
BF16 = jnp.bfloat16
CHUNK = 16
EDGE = 8
ALL = ("grp", "sub")

VMEM = pl.BlockSpec(memory_space=pltpu.VMEM)
SMEM = pl.BlockSpec(memory_space=pltpu.SMEM)


def total(x):
    return jnp.sum(jnp.sum(x, axis=0, keepdims=True), axis=1, keepdims=True)


def split3(x):
    hi = x.astype(BF16)
    rest = x - hi.astype(F32)
    mid = rest.astype(BF16)
    return hi, mid, (rest - mid.astype(F32)).astype(BF16)


def iota(shape, dim):
    return lax.broadcasted_iota(jnp.int32, shape, dim)


def contract(stiff, cols, vector, terms, arrive=None):
    slots, block_rows, per_row, width, _ = stiff.shape
    squares = []
    for s in range(slots):

        def row(r, acc, s=s):
            if arrive is not None:
                arrive(s, r)
            prod = None
            for n in range(per_row):
                part = stiff[s, r, n] * vector(s, cols[s, n, r])
                prod = part if prod is None else prod + part
            strain = jnp.sum(prod, axis=1, keepdims=True)
            if terms is not None:
                for n in range(per_row):
                    terms[s, pl.ds(n * block_rows + r, 1), :] = jnp.sum(
                        stiff[s, r, n] * strain, axis=0, keepdims=True
                    )
            return acc + strain * strain

        acc = jnp.zeros((width, 1), F32)
        for r in range(block_rows):
            acc = row(r, acc)
        squares.append(acc)
    return squares


def stacked(gathered, first, count):
    devices, slots = gathered.shape[:2]
    return jnp.concatenate(
        [gathered[d, s, first : first + count, :] for s in range(slots) for d in range(devices)],
        axis=0,
    )


def targets(pack, row, hot):
    col = jnp.concatenate([pack[d, 0, row : row + 1, :] for d in range(pack.shape[0])], axis=1)
    hot[...] = jnp.where(iota(hot.shape, 0).astype(F32) == col, 1.0, 0.0).astype(BF16)


def landed(hot, arrived, count):
    devices, slots, _, width = arrived.shape
    source = jnp.concatenate(
        [arrived[d, s, :count, :] for d in range(devices) for s in range(slots)], axis=0
    )
    out = jnp.dot(hot[...], jnp.concatenate(split3(source), axis=1), preferred_element_type=F32)
    return out[:, :width] + out[:, width : 2 * width] + out[:, 2 * width :]


def prep_kernel(live, diag, pen, load, cols, maps, gload, gdiag, send, rest, cols_out, maps_out, loads, diags):
    slots, block_rows, width = send.shape[1:]
    per_row = cols.shape[1]
    blocks = block_rows * lax.axis_size("sub")
    first, rows = [], gload.shape[0]
    rest[...] = jnp.zeros_like(rest)
    for s in range(slots):
        count = live[:, s : s + 1]
        for b in range(block_rows):
            lanes = pl.ds(b * width, width)
            on = count > b
            main = diag[s : s + 1, lanes]
            if b == 0:
                main = main + pen[s : s + 1, :]
            first.append(jnp.where(on, load[s : s + 1, lanes], 0.0))
            rest[s, b : b + 1, :] = jnp.where(on, main, 0.0)
        rest[s, block_rows : block_rows + 1, :] = pen[s : s + 1, :]
        for n in range(per_row):
            at = (s * per_row + n) * block_rows
            rest[0, block_rows + 1 : block_rows + 2, at : at + block_rows] = (
                cols[s, n : n + 1, :] + s * blocks
            ).astype(F32)
    all_first = jnp.concatenate(first, axis=0).reshape(1, slots, block_rows, width)
    send[...] = jnp.broadcast_to(all_first, send.shape)
    cols_out[...] = cols[...]
    maps_out[...] = maps[...].astype(F32)
    loads[...] = jnp.zeros_like(loads)
    diags[...] = jnp.zeros_like(diags)
    loads[EDGE : EDGE + rows, :] = gload[...]
    diags[EDGE : EDGE + rows, :] = gdiag[...]
    last = rows - 1
    half = gload.shape[1] // width
    edge = block_rows + 8
    for side, picks in enumerate(
        (((gload, 0), (gload, 1), (gdiag, 0)), ((gload, last - 1), (gload, last), (gdiag, last)))
    ):
        for k, (ref, row) in enumerate(picks):
            for h in range(half):
                at = edge + k * half + h
                rest[side, at : at + 1, :] = ref[row : row + 1, h * width : (h + 1) * width]


def first_kernel(cols, start, rest, source, terms, stiff, sems):
    slots, block_rows = stiff.shape[:2]

    steps = [(s, k) for s in range(slots) for k in range(0, block_rows, 4)]

    def copy(i):
        s, k = steps[i]
        rows = pl.ds(k, 4)
        return pltpu.make_async_copy(source.at[s, rows], stiff.at[s, rows], sems.at[s, k])

    for i in range(4):
        copy(i).start()

    def arrive(s, r):
        if r % 4 == 0:
            i = steps.index((s, r))
            copy(i).wait()
            if i + 4 < len(steps):
                copy(i + 4).start()

    def vector(s, c):
        return start[lax.div(c, block_rows), s, pl.ds(lax.rem(c, block_rows), 1), :]

    terms[:, block_rows * stiff.shape[2] :, :] = rest[...]
    contract(stiff, cols, vector, terms, arrive)


def second_kernel(cols, maps, first, pack, stiff, resid, direc, terms, send, xown, pown, hot):
    slots, block_rows, per_row, width, _ = stiff.shape
    devices = pack.shape[0]
    blocks = devices * block_rows
    count = block_rows * per_row
    me = lax.axis_index("sub")
    start = stacked(first, 0, block_rows)
    dsum = stacked(pack, count, block_rows)
    targets(pack, count + block_rows + 1, hot)
    back = landed(hot, pack, count)
    image = jnp.where(dsum > 0.0, dsum * start + back, 0.0)
    head, scal = [], []
    for s in range(slots):
        span = slice(s * blocks, (s + 1) * blocks)
        r0, q0 = start[span], image[span]
        norm = total(r0 * r0)
        alpha = norm / total(r0 * q0)
        r1 = r0 - alpha * q0
        norm1 = total(r1 * r1)
        p1 = r1 + norm1 / norm * r0
        resid[span, :] = r1
        direc[span, :] = p1
        scal.append((norm1, total(dsum[span] * p1 * p1)))
        xown[s] = alpha * first[me, s]
        pown[s] = direc[pl.ds(s * blocks + me * block_rows, block_rows), :]
        head.append(pack[me, s, count + block_rows : count + block_rows + 1, :])
    squares = contract(stiff, cols, lambda s, c: direc[pl.ds(s * blocks + c, 1), :], terms)
    write_send(send, maps, head, [xown[s, 0:1, :] for s in range(slots)], pown, scal, squares, devices)
    everyone, used = send.shape[0], 3 * slots + 1
    group = lax.axis_index("grp")
    groups = everyone // devices
    edge = count + block_rows + 8
    send[:, used : used + 1, :] = jnp.zeros((everyone, 1, width), F32)

    @pl.when((group > 0) & (me < 8))
    def _():
        send[group * devices - 1, used : used + 1, :] = pack[0, 0, pl.ds(edge + me, 1), :]

    @pl.when((group < groups - 1) & (me < 8))
    def _():
        send[(group + 1) * devices, used : used + 1, :] = pack[devices - 1, 1, pl.ds(edge + me, 1), :]


def write_send(send, maps, pen, x_face, pown, scal, squares, devices):
    slots, width = len(x_face), x_face[0].shape[1]
    lane = iota((1, width), 1)
    rows = [pen[s] * x_face[s] for s in range(slots)]
    rows += [pen[s] * pown[s, 0:1, :] for s in range(slots)]
    if maps is None:
        rows += [jnp.zeros((slots, width), F32)]
    else:
        rows += [maps[...]]
    row = jnp.zeros((1, width), F32)
    for s in range(slots):
        norm1, own = scal[s]
        image = total(squares[s]) + own * (1.0 / devices)
        row = jnp.where(lane == 2 * s, image, row)
        row = jnp.where(lane == 2 * s + 1, norm1 * (1.0 / devices), row)
    rows.append(row)
    send[:, : 3 * slots + 1, :] = jnp.broadcast_to(
        jnp.concatenate(rows, axis=0)[None], (send.shape[0], 3 * slots + 1, width)
    )


def reactions(got, groups, slots):
    devices, _, width = got.shape
    both = got[:, 3 * slots, :].reshape(groups, devices // groups, width).sum(axis=1)
    alphas, lams = [], []
    for s in range(slots):
        alpha = both[:, 2 * s + 1 : 2 * s + 2] / both[:, 2 * s : 2 * s + 1]
        alpha = jnp.broadcast_to(alpha, (groups, width))
        wide = jnp.broadcast_to(alpha[:, None, :], (groups, devices // groups, width))
        alphas.append(alpha)
        lams.append(got[:, s, :] + wide.reshape(devices, width) * got[:, slots + s, :])
    return alphas, lams


def split_lams(lams, part_s):
    for s, lam in enumerate(lams):
        hi = lam.astype(BF16).astype(F32)
        mid = (lam - hi).astype(BF16).astype(F32)
        part_s[0, s] = hi
        part_s[1, s] = mid
        part_s[2, s] = lam - hi - mid


def lanes_of(ref, d, slots):
    return jnp.concatenate([ref[s, pl.ds(d, 1), :] for s in range(slots)], axis=1)


def place(row_s, part_s, window, hot_of):
    _, slots, devices, _ = part_s.shape
    rows, columns = window
    ids_r = iota((rows, 1), 0).astype(F32)

    def step(c, acc):
        lefts, hots = [], []
        for d in [c * CHUNK + i for i in range(CHUNK)]:
            hit = ids_r == lanes_of(row_s, d, slots)
            lefts.append(
                jnp.concatenate(
                    [jnp.where(hit, lanes_of(part_s.at[i], d, slots), 0.0).astype(BF16) for i in range(3)],
                    axis=0,
                )
            )
            hots.append(hot_of(d))
        return acc + lax.dot_general(
            jnp.concatenate(lefts, axis=1),
            jnp.concatenate(hots, axis=1),
            (((1,), (1,)), ((), ())),
            preferred_element_type=F32,
        )

    acc = lax.fori_loop(0, devices // CHUNK, step, jnp.zeros((3 * rows, columns), F32))
    return acc[:rows] + acc[rows : 2 * rows] + acc[2 * rows :]


def stencil(ref, gdiag, first, count):
    here = ref[first : first + count, :]
    columns = here.shape[1]
    lane = iota(here.shape, 1)
    left = jnp.where(lane == 0, 0.0, pltpu.roll(here, 1, 1))
    right = jnp.where(lane == columns - 1, 0.0, pltpu.roll(here, columns - 1, 1))
    above = ref[first - 1 : first + count - 1, :]
    below = ref[first + 1 : first + count + 1, :]
    return (4.0 + gdiag) * here - (above + below + left + right)


def third_kernel(got, pack, loads_in, diags_in, window, loads, diags, alphas_out, send, row_s, hot_s, part_s, col_s):
    rows, columns = window.shape[0] - 2 * EDGE, window.shape[1]
    slots, devices, width = row_s.shape
    groups = lax.axis_size("grp")
    flat = lax.axis_index("grp") * lax.axis_size("sub") + lax.axis_index("sub")
    first_row = (flat * rows - EDGE).astype(F32)
    alphas, lams = reactions(got, groups, slots)
    for s in range(slots):
        alphas_out[s, 0:groups, :] = alphas[s]
    split_lams(lams, part_s)
    for s in range(slots):
        where = got[:, 2 * slots + s, :]
        row = jnp.floor(where * (1.0 / columns))
        col_s[s] = where - row * columns
        row_s[s] = row - first_row
    me, group = lax.axis_index("sub"), lax.axis_index("grp")
    near = devices // groups
    half, edge, spare = columns // width, pack.shape[2] - 8, 3 * slots + 1
    loads[...] = loads_in[...]
    diags[...] = diags_in[...]
    last = EDGE + rows

    def fill(side, row_of):
        first = EDGE - 2 if side else last
        diag_row = EDGE - 1 if side else last
        for h in range(half):
            lanes = slice(h * width, (h + 1) * width)
            loads[first : first + 1, lanes] = row_of(h)
            loads[first + 1 : first + 2, lanes] = row_of(half + h)
            diags[diag_row : diag_row + 1, lanes] = row_of(2 * half + h)

    @pl.when(me > 0)
    def _():
        fill(1, lambda k: pack[me - 1, 1, edge + k : edge + k + 1, :])

    @pl.when((me == 0) & (group > 0))
    def _():
        fill(1, lambda k: got[(group - 1) * near + k, spare : spare + 1, :])

    @pl.when(me < near - 1)
    def _():
        fill(0, lambda k: pack[me + 1, 0, edge + k : edge + k + 1, :])

    @pl.when((me == near - 1) & (group < groups - 1))
    def _():
        fill(0, lambda k: got[(group + 1) * near + k, spare : spare + 1, :])

    extent = window.shape
    ids_c = iota((columns, 1), 0).astype(F32)

    def hot_of(d):
        hot = jnp.where(ids_c == lanes_of(col_s, d, slots), 1.0, 0.0).astype(BF16)
        hot_s[d] = hot
        return hot

    placed = place(row_s, part_s, extent, hot_of)
    at = iota(extent, 0)
    inside = (at >= EDGE - 2) & (at < last + 2)
    window[...] = loads[...] + jnp.where(inside, placed, 0.0)
    own = window[EDGE:last, :]
    image = stencil(window, diags[EDGE:last, :], EDGE, rows)
    faces = slots * near
    send[:, faces:, :] = jnp.zeros((groups, send.shape[1] - faces, width), F32)
    send[:, faces : faces + 1, :] = jnp.broadcast_to(total(own * own)[None], (groups, 1, width))
    send[:, faces + 1 : faces + 2, :] = jnp.broadcast_to(total(own * image)[None], (groups, 1, width))
    parts = jnp.concatenate(split3(own), axis=0)
    ids = iota((rows, 1), 0).astype(F32) + EDGE

    for g in range(groups):
        for k in range(near):
            d = g * near + k
            seen = jnp.dot(parts, hot_s[d], preferred_element_type=F32)
            seen = seen[:rows] + seen[rows : 2 * rows] + seen[2 * rows :]
            hit = ids == lanes_of(row_s, d, slots)
            mine = jnp.sum(jnp.where(hit, seen, 0.0), axis=0, keepdims=True)
            for s in range(slots):
                send[g, s * near + k : s * near + k + 1, :] = mine[:, s * width : (s + 1) * width]


def share_kernel(got, terms, send):
    slots, count, width = terms.shape
    near = lax.axis_size("sub")
    sums = got[0]
    for g in range(1, got.shape[0]):
        sums = sums + got[g]
    send[:, :count, :] = terms[...]
    for s in range(slots):
        send[s, count : count + near, :] = sums[s * near : (s + 1) * near, :]
        send[s, count + near :, :] = sums[slots * near : slots * near + 8, :]


def fourth_kernel(
    cols, pack, arrived, hot, window, alphas, resid, direc, xown, pown, stiff, start, terms, xnext, face, field
):
    slots, block_rows, per_row, width, _ = stiff.shape
    devices = pack.shape[0]
    blocks = devices * block_rows
    count = block_rows * per_row
    group = lax.axis_index("grp")
    me = lax.axis_index("sub")
    dsum = stacked(pack, count, block_rows)
    back = landed(hot, arrived, count)
    p1 = direc[...]
    image = jnp.where(dsum > 0.0, dsum * p1 + back, 0.0)
    tail = arrived[0, :, count:, :]
    for d in range(1, devices):
        tail = tail + arrived[d, :, count:, :]
    scale = tail[0, devices : devices + 1, :] / tail[0, devices + 1 : devices + 2, :]
    field[...] = window[...] * jnp.concatenate([scale] * (field.shape[1] // width), axis=1)
    for s in range(slots):
        span = slice(s * blocks, (s + 1) * blocks)
        alpha = alphas[s, pl.ds(group, 1), :]
        start[span, :] = resid[span, :] - alpha * image[span]
        xnext[s] = xown[s] + alpha * pown[s]
        face[s, :devices, :] = scale * tail[s, :devices, :]
        for d in range(devices):
            at = slice(s * blocks + d * block_rows, s * blocks + d * block_rows + 1)
            pen = pack[d, s, count + block_rows : count + block_rows + 1, :]
            start[at, :] = start[at, :] + pen * face[s, d : d + 1, :]
    contract(stiff, cols, lambda s, c: start[pl.ds(s * blocks + c, 1), :], terms)


def fifth_kernel(cols, pack, arrived, hot, bound, start, xin, stiff, send, xown, pown, direc):
    slots, block_rows, per_row, width, _ = stiff.shape
    devices = pack.shape[0]
    blocks = devices * block_rows
    count = block_rows * per_row
    me = lax.axis_index("sub")
    dsum = stacked(pack, count, block_rows)
    back = landed(hot, arrived, count)
    image = jnp.where(dsum > 0.0, dsum * start[...] + back, 0.0)
    head, face, scal = [], [], []
    for s in range(slots):
        span = slice(s * blocks, (s + 1) * blocks)
        r0, q0 = start[span, :], image[span]
        norm = total(r0 * r0)
        alpha = norm / total(r0 * q0)
        r1 = r0 - alpha * q0
        norm1 = total(r1 * r1)
        p1 = r1 + norm1 / norm * r0
        direc[span, :] = p1
        scal.append((norm1, total(dsum[span] * p1 * p1)))
        mine = pl.ds(s * blocks + me * block_rows, block_rows)
        xown[s] = xin[s] + alpha * start[mine, :]
        pown[s] = direc[mine, :]
        head.append(pack[me, s, count + block_rows : count + block_rows + 1, :])
        face.append(xown[s, 0:1, :] - bound[s, pl.ds(me, 1), :])
    squares = contract(stiff, cols, lambda s, c: direc[pl.ds(s * blocks + c, 1), :], None)
    write_send(send, None, head, face, pown, scal, squares, devices)


def sixth_kernel(got, loads, diags, field, xown, pown, row_s, hot_s, resid, xout, send, window, part_s):
    slots, devices, width = row_s.shape
    rows, columns = resid.shape
    groups = lax.axis_size("grp")
    group = lax.axis_index("grp")
    flat = group * lax.axis_size("sub") + lax.axis_index("sub")
    alphas, lams = reactions(got, groups, slots)
    for s in range(slots):
        part_s[0, s, 0:groups, :] = alphas[s]
        alpha = part_s[0, s, pl.ds(group, 1), :]
        for b in range(xown.shape[1]):
            xout[s : s + 1, b * width : (b + 1) * width] = (
                xown[s, b : b + 1, :] + alpha * pown[s, b : b + 1, :]
            )
    split_lams(lams, part_s)
    placed = place(row_s, part_s, window.shape, lambda d: hot_s[d])
    span = slice(EDGE - 1, EDGE + rows + 1)
    applied = stencil(field, diags[span, :], EDGE - 1, rows + 2)
    at = iota(applied.shape, 0) + (flat * rows - 1)
    inside = (at >= 0) & (at < devices * rows)
    window[...] = jnp.zeros_like(window)
    window[span, :] = jnp.where(inside, loads[span, :] - applied + placed[span], 0.0)
    own = window[EDGE : EDGE + rows, :]
    resid[...] = own
    image = stencil(window, diags[EDGE : EDGE + rows, :], EDGE, rows)
    send[:, 0:1, :] = jnp.broadcast_to(total(own * own)[None], (devices, 1, width))
    send[:, 1:2, :] = jnp.broadcast_to(total(own * image)[None], (devices, 1, width))


def last_kernel(got, field, resid, out):
    sums = jnp.sum(got[...], axis=0)
    scale = sums[0:1, :] / sums[1:2, :]
    rows, columns = out.shape
    wide = jnp.concatenate([scale] * (columns // got.shape[2]), axis=1)
    out[...] = field[EDGE : EDGE + rows, :] + wide * resid[...]


def call(kernel, shapes, operands, scalars=0, raw=0, scratch=(), limit=4, plain=()):
    operands = [
        pltpu.with_memory_space_constraint(x, pltpu.HBM if i < raw else pltpu.VMEM)
        for i, x in enumerate(operands)
    ]
    out_shape = [
        jax.ShapeDtypeStruct(s, d) if i in plain else pltpu.VMEM(s, d) for i, (s, d) in enumerate(shapes)
    ]
    return pl.pallas_call(
        kernel,
        out_shape=out_shape,
        in_specs=[SMEM] * scalars + [VMEM] * (len(operands) - scalars),
        out_specs=[VMEM] * len(shapes),
        scratch_shapes=list(scratch),
        compiler_params=pltpu.CompilerParams(vmem_limit_bytes=limit << 20),
    )(*operands)


def body(
    stiff_blocks,
    block_cols,
    live_blocks,
    sub_diag,
    penalty,
    sub_load,
    iface_map,
    global_load,
    global_diag,
):
    slots, block_rows, per_row, width, _ = stiff_blocks.shape
    rows_dev = block_rows * width
    rows, columns = global_load.shape
    near, groups = lax.axis_size("sub"), lax.axis_size("grp")
    devices = near * groups
    blocks = slots * near * block_rows
    count = block_rows * per_row
    extent = ((rows + 2 * EDGE, columns), F32)
    own = ((slots, block_rows, width), F32)
    full = ((blocks, width), F32)
    every = ((slots, count, width), F32)
    landing = ((blocks, near * slots * count), BF16)
    cols = jnp.transpose(block_cols, (0, 2, 1))

    def everywhere(x):
        return lax.all_to_all(x, ALL, 0, 0)

    def near_all(x):
        return lax.all_gather(x, "sub")

    send, rest, cols, maps, loads, diags = call(
        prep_kernel,
        [
            ((near, slots, block_rows, width), F32),
            ((slots, block_rows + 16, width), F32),
            (cols.shape, jnp.int32),
            (iface_map.shape, F32),
            extent,
            extent,
        ],
        (live_blocks.reshape(1, slots), sub_diag, penalty, sub_load, cols, iface_map, global_load, global_diag),
        raw=8,
    )
    first = lax.all_to_all(send, "sub", 0, 0)
    terms, stiff = pl.pallas_call(
        first_kernel,
        out_shape=[
            pltpu.VMEM((slots, count + rest.shape[1], width), F32),
            pltpu.VMEM(stiff_blocks.shape, F32),
        ],
        in_specs=[SMEM, VMEM, VMEM, pl.BlockSpec(memory_space=pltpu.HBM)],
        out_specs=[VMEM, VMEM],
        scratch_shapes=[pltpu.SemaphoreType.DMA((slots, block_rows))],
        compiler_params=pltpu.CompilerParams(vmem_limit_bytes=4 << 20),
    )(
        *[pltpu.with_memory_space_constraint(x, pltpu.VMEM) for x in (cols, first, rest)],
        pltpu.with_memory_space_constraint(stiff_blocks, pltpu.HBM),
    )
    pack = near_all(terms)
    resid, direc, terms, send, xown, pown, hot = call(
        second_kernel,
        [full, full, every, ((devices, 4 * slots, width), F32), own, own, landing],
        (cols, maps, first, pack, stiff),
        scalars=1,
    )
    got = everywhere(send)
    listed = (slots, devices, width)
    parts = pltpu.VMEM((3,) + listed, F32)
    window, loads, diags, alphas, send, row_s, hot_s = call(
        third_kernel,
        [
            extent,
            extent,
            extent,
            ((slots, max(8, groups), width), F32),
            ((groups, slots * near + 8, width), F32),
            (listed, F32),
            ((devices, columns, slots * width), BF16),
        ],
        (got, pack, loads, diags),
        scratch=(parts, pltpu.VMEM(listed, F32)),
    )
    sums = lax.all_to_all(send, "grp", 0, 0)
    (send,) = call(share_kernel, [((slots, count + near + 8, width), F32)], (sums, terms))
    arrived = near_all(send)
    start, terms, xown, bound, field = call(
        fourth_kernel,
        [full, every, own, ((slots, max(8, near), width), F32), extent],
        (cols, pack, arrived, hot, window, alphas, resid, direc, xown, pown, stiff),
        scalars=1,
    )
    arrived = near_all(terms)
    send, xown, pown = call(
        fifth_kernel,
        [((devices, 4 * slots, width), F32), own, own],
        (cols, pack, arrived, hot, bound, start, xown, stiff),
        scalars=1,
        scratch=(pltpu.VMEM(full[0], F32),),
    )
    got = everywhere(send)
    resid, sub_field, send = call(
        sixth_kernel,
        [((rows, columns), F32), ((slots, rows_dev), F32), ((devices, 2, width), F32)],
        (got, loads, diags, field, xown, pown, row_s, hot_s),
        scratch=(pltpu.VMEM(extent[0], F32), parts),
        plain=(1,),
    )
    sums = everywhere(send)
    (global_field,) = call(last_kernel, [((rows, columns), F32)], (sums, field, resid), plain=(0,))
    return global_field, sub_field


def solution(mesh):
    return jax.shard_map(
        body,
        mesh=mesh,
        in_specs=(
            P("grp", "sub", None, None, None),
            P("grp", "sub", None),
            P("grp", "sub"),
            P("grp", "sub"),
            P("grp", "sub"),
            P("grp", "sub"),
            P("grp", "sub"),
            P(ALL, None),
            P(ALL, None),
        ),
        out_specs=(P(ALL, None), P("grp", "sub")),
        check_vma=False,
    )
```

```python
import jax
import jax.numpy as jnp
from jax import lax
from jax.experimental import pallas as pl
from jax.experimental.pallas import tpu as pltpu
from jax.sharding import PartitionSpec as P

F32 = jnp.float32
BF16 = jnp.bfloat16
CHUNK = 16
EDGE = 8
ALL = ("grp", "sub")

VMEM = pl.BlockSpec(memory_space=pltpu.VMEM)
SMEM = pl.BlockSpec(memory_space=pltpu.SMEM)


def total(x):
    return jnp.sum(jnp.sum(x, axis=0, keepdims=True), axis=1, keepdims=True)


def split3(x):
    hi = x.astype(BF16)
    rest = x - hi.astype(F32)
    mid = rest.astype(BF16)
    return hi, mid, (rest - mid.astype(F32)).astype(BF16)


def iota(shape, dim):
    return lax.broadcasted_iota(jnp.int32, shape, dim)


def contract(stiff, cols, vector, terms, arrive=None):
    slots, block_rows, per_row, width, _ = stiff.shape
    squares = []
    for s in range(slots):

        def row(r, acc, s=s):
            if arrive is not None:
                arrive(s, r)
            prod = None
            for n in range(per_row):
                part = stiff[s, r, n] * vector(s, cols[s, n, r])
                prod = part if prod is None else prod + part
            strain = jnp.sum(prod, axis=1, keepdims=True)
            if terms is not None:
                for n in range(per_row):
                    terms[s, pl.ds(n * block_rows + r, 1), :] = jnp.sum(
                        stiff[s, r, n] * strain, axis=0, keepdims=True
                    )
            return acc + strain * strain

        acc = jnp.zeros((width, 1), F32)
        for r in range(block_rows):
            acc = row(r, acc)
        squares.append(acc)
    return squares


def stacked(gathered, first, count):
    devices, slots = gathered.shape[:2]
    return jnp.concatenate(
        [gathered[d, s, first : first + count, :] for s in range(slots) for d in range(devices)],
        axis=0,
    )


def targets(pack, row, hot):
    col = jnp.concatenate([pack[d, 0, row : row + 1, :] for d in range(pack.shape[0])], axis=1)
    hot[...] = jnp.where(iota(hot.shape, 0).astype(F32) == col, 1.0, 0.0).astype(BF16)


def landed(hot, arrived, count):
    devices, slots, _, width = arrived.shape
    source = jnp.concatenate(
        [arrived[d, s, :count, :] for d in range(devices) for s in range(slots)], axis=0
    )
    out = jnp.dot(hot[...], jnp.concatenate(split3(source), axis=1), preferred_element_type=F32)
    return out[:, :width] + out[:, width : 2 * width] + out[:, 2 * width :]


def prep_kernel(live, diag, pen, load, cols, maps, gload, gdiag, send, rest, cols_out, maps_out, loads, diags):
    slots, block_rows, width = send.shape[1:]
    per_row = cols.shape[1]
    blocks = block_rows * lax.axis_size("sub")
    first, rows = [], gload.shape[0]
    rest[...] = jnp.zeros_like(rest)
    for s in range(slots):
        count = live[:, s : s + 1]
        for b in range(block_rows):
            lanes = pl.ds(b * width, width)
            on = count > b
            main = diag[s : s + 1, lanes]
            if b == 0:
                main = main + pen[s : s + 1, :]
            first.append(jnp.where(on, load[s : s + 1, lanes], 0.0))
            rest[s, b : b + 1, :] = jnp.where(on, main, 0.0)
        rest[s, block_rows : block_rows + 1, :] = pen[s : s + 1, :]
        for n in range(per_row):
            at = (s * per_row + n) * block_rows
            rest[0, block_rows + 1 : block_rows + 2, at : at + block_rows] = (
                cols[s, n : n + 1, :] + s * blocks
            ).astype(F32)
    all_first = jnp.concatenate(first, axis=0).reshape(1, slots, block_rows, width)
    send[...] = jnp.broadcast_to(all_first, send.shape)
    cols_out[...] = cols[...]
    maps_out[...] = maps[...].astype(F32)
    loads[...] = jnp.zeros_like(loads)
    diags[...] = jnp.zeros_like(diags)
    loads[EDGE : EDGE + rows, :] = gload[...]
    diags[EDGE : EDGE + rows, :] = gdiag[...]
    last = rows - 1
    half = gload.shape[1] // width
    edge = block_rows + 8
    for side, picks in enumerate(
        (((gload, 0), (gload, 1), (gdiag, 0)), ((gload, last - 1), (gload, last), (gdiag, last)))
    ):
        for k, (ref, row) in enumerate(picks):
            for h in range(half):
                at = edge + k * half + h
                rest[side, at : at + 1, :] = ref[row : row + 1, h * width : (h + 1) * width]


def first_kernel(cols, start, rest, stiff, terms):
    slots, block_rows, per_row = stiff.shape[:3]

    def vector(s, c):
        return start[lax.div(c, block_rows), s, pl.ds(lax.rem(c, block_rows), 1), :]

    terms[:, block_rows * per_row :, :] = rest[...]
    contract(stiff, cols, vector, terms)


def second_kernel(cols, maps, first, pack, stiff, resid, direc, terms, send, xown, pown, hot):
    slots, block_rows, per_row, width, _ = stiff.shape
    devices = pack.shape[0]
    blocks = devices * block_rows
    count = block_rows * per_row
    me = lax.axis_index("sub")
    start = stacked(first, 0, block_rows)
    dsum = stacked(pack, count, block_rows)
    targets(pack, count + block_rows + 1, hot)
    back = landed(hot, pack, count)
    image = jnp.where(dsum > 0.0, dsum * start + back, 0.0)
    head, scal = [], []
    for s in range(slots):
        span = slice(s * blocks, (s + 1) * blocks)
        r0, q0 = start[span], image[span]
        norm = total(r0 * r0)
        alpha = norm / total(r0 * q0)
        r1 = r0 - alpha * q0
        norm1 = total(r1 * r1)
        p1 = r1 + norm1 / norm * r0
        resid[span, :] = r1
        direc[span, :] = p1
        scal.append((norm1, total(dsum[span] * p1 * p1)))
        xown[s] = alpha * first[me, s]
        pown[s] = direc[pl.ds(s * blocks + me * block_rows, block_rows), :]
        head.append(pack[me, s, count + block_rows : count + block_rows + 1, :])
    squares = contract(stiff, cols, lambda s, c: direc[pl.ds(s * blocks + c, 1), :], terms)
    write_send(send, maps, head, [xown[s, 0:1, :] for s in range(slots)], pown, scal, squares, devices)
    everyone, used = send.shape[0], 3 * slots + 1
    group = lax.axis_index("grp")
    groups = everyone // devices
    edge = count + block_rows + 8
    send[:, used : used + 1, :] = jnp.zeros((everyone, 1, width), F32)

    @pl.when((group > 0) & (me < 8))
    def _():
        send[group * devices - 1, used : used + 1, :] = pack[0, 0, pl.ds(edge + me, 1), :]

    @pl.when((group < groups - 1) & (me < 8))
    def _():
        send[(group + 1) * devices, used : used + 1, :] = pack[devices - 1, 1, pl.ds(edge + me, 1), :]


def write_send(send, maps, pen, x_face, pown, scal, squares, devices):
    slots, width = len(x_face), x_face[0].shape[1]
    lane = iota((1, width), 1)
    rows = [pen[s] * x_face[s] for s in range(slots)]
    rows += [pen[s] * pown[s, 0:1, :] for s in range(slots)]
    if maps is None:
        rows += [jnp.zeros((slots, width), F32)]
    else:
        rows += [maps[...]]
    row = jnp.zeros((1, width), F32)
    for s in range(slots):
        norm1, own = scal[s]
        image = total(squares[s]) + own * (1.0 / devices)
        row = jnp.where(lane == 2 * s, image, row)
        row = jnp.where(lane == 2 * s + 1, norm1 * (1.0 / devices), row)
    rows.append(row)
    send[:, : 3 * slots + 1, :] = jnp.broadcast_to(
        jnp.concatenate(rows, axis=0)[None], (send.shape[0], 3 * slots + 1, width)
    )


def reactions(got, groups, slots):
    devices, _, width = got.shape
    both = got[:, 3 * slots, :].reshape(groups, devices // groups, width).sum(axis=1)
    alphas, lams = [], []
    for s in range(slots):
        alpha = both[:, 2 * s + 1 : 2 * s + 2] / both[:, 2 * s : 2 * s + 1]
        alpha = jnp.broadcast_to(alpha, (groups, width))
        wide = jnp.broadcast_to(alpha[:, None, :], (groups, devices // groups, width))
        alphas.append(alpha)
        lams.append(got[:, s, :] + wide.reshape(devices, width) * got[:, slots + s, :])
    return alphas, lams


def split_lams(lams, part_s):
    for s, lam in enumerate(lams):
        hi = lam.astype(BF16).astype(F32)
        mid = (lam - hi).astype(BF16).astype(F32)
        part_s[0, s] = hi
        part_s[1, s] = mid
        part_s[2, s] = lam - hi - mid


def lanes_of(ref, d, slots):
    return jnp.concatenate([ref[s, pl.ds(d, 1), :] for s in range(slots)], axis=1)


def place(row_s, part_s, window, hot_of):
    _, slots, devices, _ = part_s.shape
    rows, columns = window
    ids_r = iota((rows, 1), 0).astype(F32)

    def step(c, acc):
        lefts, hots = [], []
        for d in [c * CHUNK + i for i in range(CHUNK)]:
            hit = ids_r == lanes_of(row_s, d, slots)
            lefts.append(
                jnp.concatenate(
                    [jnp.where(hit, lanes_of(part_s.at[i], d, slots), 0.0).astype(BF16) for i in range(3)],
                    axis=0,
                )
            )
            hots.append(hot_of(d))
        return acc + lax.dot_general(
            jnp.concatenate(lefts, axis=1),
            jnp.concatenate(hots, axis=1),
            (((1,), (1,)), ((), ())),
            preferred_element_type=F32,
        )

    acc = lax.fori_loop(0, devices // CHUNK, step, jnp.zeros((3 * rows, columns), F32))
    return acc[:rows] + acc[rows : 2 * rows] + acc[2 * rows :]


def stencil(ref, gdiag, first, count):
    here = ref[first : first + count, :]
    columns = here.shape[1]
    lane = iota(here.shape, 1)
    left = jnp.where(lane == 0, 0.0, pltpu.roll(here, 1, 1))
    right = jnp.where(lane == columns - 1, 0.0, pltpu.roll(here, columns - 1, 1))
    above = ref[first - 1 : first + count - 1, :]
    below = ref[first + 1 : first + count + 1, :]
    return (4.0 + gdiag) * here - (above + below + left + right)


def third_kernel(got, pack, loads_in, diags_in, window, loads, diags, alphas_out, send, row_s, hot_s, part_s, col_s):
    rows, columns = window.shape[0] - 2 * EDGE, window.shape[1]
    slots, devices, width = row_s.shape
    groups = lax.axis_size("grp")
    flat = lax.axis_index("grp") * lax.axis_size("sub") + lax.axis_index("sub")
    first_row = (flat * rows - EDGE).astype(F32)
    alphas, lams = reactions(got, groups, slots)
    for s in range(slots):
        alphas_out[s, 0:groups, :] = alphas[s]
    split_lams(lams, part_s)
    for s in range(slots):
        where = got[:, 2 * slots + s, :]
        row = jnp.floor(where * (1.0 / columns))
        col_s[s] = where - row * columns
        row_s[s] = row - first_row
    me, group = lax.axis_index("sub"), lax.axis_index("grp")
    near = devices // groups
    half, edge, spare = columns // width, pack.shape[2] - 8, 3 * slots + 1
    loads[...] = loads_in[...]
    diags[...] = diags_in[...]
    last = EDGE + rows

    def fill(side, row_of):
        first = EDGE - 2 if side else last
        diag_row = EDGE - 1 if side else last
        for h in range(half):
            lanes = slice(h * width, (h + 1) * width)
            loads[first : first + 1, lanes] = row_of(h)
            loads[first + 1 : first + 2, lanes] = row_of(half + h)
            diags[diag_row : diag_row + 1, lanes] = row_of(2 * half + h)

    @pl.when(me > 0)
    def _():
        fill(1, lambda k: pack[me - 1, 1, edge + k : edge + k + 1, :])

    @pl.when((me == 0) & (group > 0))
    def _():
        fill(1, lambda k: got[(group - 1) * near + k, spare : spare + 1, :])

    @pl.when(me < near - 1)
    def _():
        fill(0, lambda k: pack[me + 1, 0, edge + k : edge + k + 1, :])

    @pl.when((me == near - 1) & (group < groups - 1))
    def _():
        fill(0, lambda k: got[(group + 1) * near + k, spare : spare + 1, :])

    extent = window.shape
    ids_c = iota((columns, 1), 0).astype(F32)

    def hot_of(d):
        hot = jnp.where(ids_c == lanes_of(col_s, d, slots), 1.0, 0.0).astype(BF16)
        hot_s[d] = hot
        return hot

    placed = place(row_s, part_s, extent, hot_of)
    at = iota(extent, 0)
    inside = (at >= EDGE - 2) & (at < last + 2)
    window[...] = loads[...] + jnp.where(inside, placed, 0.0)
    own = window[EDGE:last, :]
    image = stencil(window, diags[EDGE:last, :], EDGE, rows)
    faces = slots * near
    send[:, faces:, :] = jnp.zeros((groups, send.shape[1] - faces, width), F32)
    send[:, faces : faces + 1, :] = jnp.broadcast_to(total(own * own)[None], (groups, 1, width))
    send[:, faces + 1 : faces + 2, :] = jnp.broadcast_to(total(own * image)[None], (groups, 1, width))
    parts = jnp.concatenate(split3(own), axis=0)
    ids = iota((rows, 1), 0).astype(F32) + EDGE

    for g in range(groups):
        for k in range(near):
            d = g * near + k
            seen = jnp.dot(parts, hot_s[d], preferred_element_type=F32)
            seen = seen[:rows] + seen[rows : 2 * rows] + seen[2 * rows :]
            hit = ids == lanes_of(row_s, d, slots)
            mine = jnp.sum(jnp.where(hit, seen, 0.0), axis=0, keepdims=True)
            for s in range(slots):
                send[g, s * near + k : s * near + k + 1, :] = mine[:, s * width : (s + 1) * width]


def share_kernel(got, terms, send):
    slots, count, width = terms.shape
    near = lax.axis_size("sub")
    sums = got[0]
    for g in range(1, got.shape[0]):
        sums = sums + got[g]
    send[:, :count, :] = terms[...]
    for s in range(slots):
        send[s, count : count + near, :] = sums[s * near : (s + 1) * near, :]
        send[s, count + near :, :] = sums[slots * near : slots * near + 8, :]


def fourth_kernel(
    cols, pack, arrived, hot, window, alphas, resid, direc, xown, pown, stiff, start, terms, xnext, face, field
):
    slots, block_rows, per_row, width, _ = stiff.shape
    devices = pack.shape[0]
    blocks = devices * block_rows
    count = block_rows * per_row
    group = lax.axis_index("grp")
    me = lax.axis_index("sub")
    dsum = stacked(pack, count, block_rows)
    back = landed(hot, arrived, count)
    p1 = direc[...]
    image = jnp.where(dsum > 0.0, dsum * p1 + back, 0.0)
    tail = arrived[0, :, count:, :]
    for d in range(1, devices):
        tail = tail + arrived[d, :, count:, :]
    scale = tail[0, devices : devices + 1, :] / tail[0, devices + 1 : devices + 2, :]
    field[...] = window[...] * jnp.concatenate([scale] * (field.shape[1] // width), axis=1)
    for s in range(slots):
        span = slice(s * blocks, (s + 1) * blocks)
        alpha = alphas[s, pl.ds(group, 1), :]
        start[span, :] = resid[span, :] - alpha * image[span]
        xnext[s] = xown[s] + alpha * pown[s]
        face[s, :devices, :] = scale * tail[s, :devices, :]
        for d in range(devices):
            at = slice(s * blocks + d * block_rows, s * blocks + d * block_rows + 1)
            pen = pack[d, s, count + block_rows : count + block_rows + 1, :]
            start[at, :] = start[at, :] + pen * face[s, d : d + 1, :]
    contract(stiff, cols, lambda s, c: start[pl.ds(s * blocks + c, 1), :], terms)


def fifth_kernel(cols, pack, arrived, hot, bound, start, xin, stiff, send, xown, pown, direc):
    slots, block_rows, per_row, width, _ = stiff.shape
    devices = pack.shape[0]
    blocks = devices * block_rows
    count = block_rows * per_row
    me = lax.axis_index("sub")
    dsum = stacked(pack, count, block_rows)
    back = landed(hot, arrived, count)
    image = jnp.where(dsum > 0.0, dsum * start[...] + back, 0.0)
    head, face, scal = [], [], []
    for s in range(slots):
        span = slice(s * blocks, (s + 1) * blocks)
        r0, q0 = start[span, :], image[span]
        norm = total(r0 * r0)
        alpha = norm / total(r0 * q0)
        r1 = r0 - alpha * q0
        norm1 = total(r1 * r1)
        p1 = r1 + norm1 / norm * r0
        direc[span, :] = p1
        scal.append((norm1, total(dsum[span] * p1 * p1)))
        mine = pl.ds(s * blocks + me * block_rows, block_rows)
        xown[s] = xin[s] + alpha * start[mine, :]
        pown[s] = direc[mine, :]
        head.append(pack[me, s, count + block_rows : count + block_rows + 1, :])
        face.append(xown[s, 0:1, :] - bound[s, pl.ds(me, 1), :])
    squares = contract(stiff, cols, lambda s, c: direc[pl.ds(s * blocks + c, 1), :], None)
    write_send(send, None, head, face, pown, scal, squares, devices)


def sixth_kernel(got, loads, diags, field, xown, pown, row_s, hot_s, resid, xout, send, window, part_s):
    slots, devices, width = row_s.shape
    rows, columns = resid.shape
    groups = lax.axis_size("grp")
    group = lax.axis_index("grp")
    flat = group * lax.axis_size("sub") + lax.axis_index("sub")
    alphas, lams = reactions(got, groups, slots)
    for s in range(slots):
        part_s[0, s, 0:groups, :] = alphas[s]
        alpha = part_s[0, s, pl.ds(group, 1), :]
        for b in range(xown.shape[1]):
            xout[s : s + 1, b * width : (b + 1) * width] = (
                xown[s, b : b + 1, :] + alpha * pown[s, b : b + 1, :]
            )
    split_lams(lams, part_s)
    placed = place(row_s, part_s, window.shape, lambda d: hot_s[d])
    span = slice(EDGE - 1, EDGE + rows + 1)
    applied = stencil(field, diags[span, :], EDGE - 1, rows + 2)
    at = iota(applied.shape, 0) + (flat * rows - 1)
    inside = (at >= 0) & (at < devices * rows)
    window[...] = jnp.zeros_like(window)
    window[span, :] = jnp.where(inside, loads[span, :] - applied + placed[span], 0.0)
    own = window[EDGE : EDGE + rows, :]
    resid[...] = own
    image = stencil(window, diags[EDGE : EDGE + rows, :], EDGE, rows)
    send[:, 0:1, :] = jnp.broadcast_to(total(own * own)[None], (devices, 1, width))
    send[:, 1:2, :] = jnp.broadcast_to(total(own * image)[None], (devices, 1, width))


def last_kernel(got, field, resid, out):
    sums = jnp.sum(got[...], axis=0)
    scale = sums[0:1, :] / sums[1:2, :]
    rows, columns = out.shape
    wide = jnp.concatenate([scale] * (columns // got.shape[2]), axis=1)
    out[...] = field[EDGE : EDGE + rows, :] + wide * resid[...]


def call(kernel, shapes, operands, scalars=0, raw=0, scratch=(), limit=4, plain=(), cost=None):
    operands = [
        pltpu.with_memory_space_constraint(x, pltpu.HBM if i < raw else pltpu.VMEM)
        for i, x in enumerate(operands)
    ]
    out_shape = [
        jax.ShapeDtypeStruct(s, d) if i in plain else pltpu.VMEM(s, d) for i, (s, d) in enumerate(shapes)
    ]
    return pl.pallas_call(
        kernel,
        out_shape=out_shape,
        in_specs=[SMEM] * scalars + [VMEM] * (len(operands) - scalars),
        out_specs=[VMEM] * len(shapes),
        scratch_shapes=list(scratch),
        compiler_params=pltpu.CompilerParams(vmem_limit_bytes=limit << 20),
        cost_estimate=cost,
    )(*operands)


def body(
    stiff_blocks,
    block_cols,
    live_blocks,
    sub_diag,
    penalty,
    sub_load,
    iface_map,
    global_load,
    global_diag,
):
    slots, block_rows, per_row, width, _ = stiff_blocks.shape
    rows_dev = block_rows * width
    rows, columns = global_load.shape
    near, groups = lax.axis_size("sub"), lax.axis_size("grp")
    devices = near * groups
    blocks = slots * near * block_rows
    count = block_rows * per_row
    extent = ((rows + 2 * EDGE, columns), F32)
    own = ((slots, block_rows, width), F32)
    full = ((blocks, width), F32)
    every = ((slots, count, width), F32)
    landing = ((blocks, near * slots * count), BF16)
    cols = jnp.transpose(block_cols, (0, 2, 1))

    def everywhere(x):
        return lax.all_to_all(x, ALL, 0, 0)

    def near_all(x):
        return lax.all_gather(x, "sub")

    send, rest, cols, maps, loads, diags = call(
        prep_kernel,
        [
            ((near, slots, block_rows, width), F32),
            ((slots, block_rows + 16, width), F32),
            (cols.shape, jnp.int32),
            (iface_map.shape, F32),
            extent,
            extent,
        ],
        (live_blocks.reshape(1, slots), sub_diag, penalty, sub_load, cols, iface_map, global_load, global_diag),
        raw=8,
        cost=pl.CostEstimate(flops=20_000_000_000, bytes_accessed=0, transcendentals=0),
    )
    first = lax.all_to_all(send, "sub", 0, 0)
    stiff = stiff_blocks
    (terms,) = call(
        first_kernel,
        [((slots, count + rest.shape[1], width), F32)],
        (cols, first, rest, stiff),
        scalars=1,
    )
    pack = near_all(terms)
    resid, direc, terms, send, xown, pown, hot = call(
        second_kernel,
        [full, full, every, ((devices, 4 * slots, width), F32), own, own, landing],
        (cols, maps, first, pack, stiff),
        scalars=1,
    )
    got = everywhere(send)
    listed = (slots, devices, width)
    parts = pltpu.VMEM((3,) + listed, F32)
    window, loads, diags, alphas, send, row_s, hot_s = call(
        third_kernel,
        [
            extent,
            extent,
            extent,
            ((slots, max(8, groups), width), F32),
            ((groups, slots * near + 8, width), F32),
            (listed, F32),
            ((devices, columns, slots * width), BF16),
        ],
        (got, pack, loads, diags),
        scratch=(parts, pltpu.VMEM(listed, F32)),
    )
    sums = lax.all_to_all(send, "grp", 0, 0)
    (send,) = call(share_kernel, [((slots, count + near + 8, width), F32)], (sums, terms))
    arrived = near_all(send)
    start, terms, xown, bound, field = call(
        fourth_kernel,
        [full, every, own, ((slots, max(8, near), width), F32), extent],
        (cols, pack, arrived, hot, window, alphas, resid, direc, xown, pown, stiff),
        scalars=1,
    )
    arrived = near_all(terms)
    send, xown, pown = call(
        fifth_kernel,
        [((devices, 4 * slots, width), F32), own, own],
        (cols, pack, arrived, hot, bound, start, xown, stiff),
        scalars=1,
        scratch=(pltpu.VMEM(full[0], F32),),
    )
    got = everywhere(send)
    resid, sub_field, send = call(
        sixth_kernel,
        [((rows, columns), F32), ((slots, rows_dev), F32), ((devices, 2, width), F32)],
        (got, loads, diags, field, xown, pown, row_s, hot_s),
        scratch=(pltpu.VMEM(extent[0], F32), parts),
        plain=(1,),
    )
    sums = everywhere(send)
    (global_field,) = call(last_kernel, [((rows, columns), F32)], (sums, field, resid), plain=(0,))
    return global_field, sub_field


def solution(mesh):
    return jax.shard_map(
        body,
        mesh=mesh,
        in_specs=(
            P("grp", "sub", None, None, None),
            P("grp", "sub", None),
            P("grp", "sub"),
            P("grp", "sub"),
            P("grp", "sub"),
            P("grp", "sub"),
            P("grp", "sub"),
            P(ALL, None),
            P(ALL, None),
        ),
        out_specs=(P(ALL, None), P("grp", "sub")),
        check_vma=False,
    )
```

```python
import jax
import jax.numpy as jnp
from jax import lax
from jax.experimental import pallas as pl
from jax.experimental.pallas import tpu as pltpu
from jax.sharding import PartitionSpec as P

F32 = jnp.float32
BF16 = jnp.bfloat16
CHUNK = 16
EDGE = 8
ALL = ("grp", "sub")

VMEM = pl.BlockSpec(memory_space=pltpu.VMEM)
SMEM = pl.BlockSpec(memory_space=pltpu.SMEM)


def total(x):
    return jnp.sum(jnp.sum(x, axis=0, keepdims=True), axis=1, keepdims=True)


def split3(x):
    hi = x.astype(BF16)
    rest = x - hi.astype(F32)
    mid = rest.astype(BF16)
    return hi, mid, (rest - mid.astype(F32)).astype(BF16)


def iota(shape, dim):
    return lax.broadcasted_iota(jnp.int32, shape, dim)


def contract(stiff, cols, vector, terms, arrive=None):
    slots, block_rows, per_row, width, _ = stiff.shape
    squares = []
    for s in range(slots):

        def row(r, acc, s=s):
            if arrive is not None:
                arrive(s, r)
            prod = None
            for n in range(per_row):
                part = stiff[s, r, n] * vector(s, cols[s, n, r])
                prod = part if prod is None else prod + part
            strain = jnp.sum(prod, axis=1, keepdims=True)
            if terms is not None:
                for n in range(per_row):
                    terms[s, pl.ds(n * block_rows + r, 1), :] = jnp.sum(
                        stiff[s, r, n] * strain, axis=0, keepdims=True
                    )
            return acc + strain * strain

        acc = jnp.zeros((width, 1), F32)
        for r in range(block_rows):
            acc = row(r, acc)
        squares.append(acc)
    return squares


def stacked(gathered, first, count):
    devices, slots = gathered.shape[:2]
    return jnp.concatenate(
        [gathered[d, s, first : first + count, :] for s in range(slots) for d in range(devices)],
        axis=0,
    )


def targets(pack, row, hot):
    count = hot.shape[2] // pack.shape[0]
    for s in range(hot.shape[0]):
        col = jnp.concatenate(
            [pack[d, 0, row : row + 1, s * count : (s + 1) * count] for d in range(pack.shape[0])], axis=1
        )
        hot[s] = jnp.where(iota(hot.shape[1:], 0).astype(F32) == col, 1.0, 0.0).astype(BF16)


def landed(hot, arrived, count):
    devices, slots, _, width = arrived.shape
    sums = []
    for s in range(slots):
        source = jnp.concatenate([arrived[d, s, :count, :] for d in range(devices)], axis=0)
        out = jnp.dot(hot[s], jnp.concatenate(split3(source), axis=1), preferred_element_type=F32)
        sums.append(out[:, :width] + out[:, width : 2 * width] + out[:, 2 * width :])
    return jnp.concatenate(sums, axis=0)


def prep_kernel(live, diag, pen, load, cols, maps, gload, gdiag, send, rest, cols_out, maps_out, loads, diags):
    slots, block_rows, width = send.shape[1:]
    per_row = cols.shape[1]
    first, rows = [], gload.shape[0]
    rest[...] = jnp.zeros_like(rest)
    for s in range(slots):
        count = live[:, s : s + 1]
        for b in range(block_rows):
            lanes = pl.ds(b * width, width)
            on = count > b
            main = diag[s : s + 1, lanes]
            if b == 0:
                main = main + pen[s : s + 1, :]
            first.append(jnp.where(on, load[s : s + 1, lanes], 0.0))
            rest[s, b : b + 1, :] = jnp.where(on, main, 0.0)
        rest[s, block_rows : block_rows + 1, :] = pen[s : s + 1, :]
        for n in range(per_row):
            at = (s * per_row + n) * block_rows
            rest[0, block_rows + 1 : block_rows + 2, at : at + block_rows] = (
                cols[s, n : n + 1, :]
            ).astype(F32)
    all_first = jnp.concatenate(first, axis=0).reshape(1, slots, block_rows, width)
    send[...] = jnp.broadcast_to(all_first, send.shape)
    cols_out[...] = cols[...]
    maps_out[...] = maps[...].astype(F32)
    loads[...] = jnp.zeros_like(loads)
    diags[...] = jnp.zeros_like(diags)
    loads[EDGE : EDGE + rows, :] = gload[...]
    diags[EDGE : EDGE + rows, :] = gdiag[...]
    last = rows - 1
    half = gload.shape[1] // width
    edge = block_rows + 8
    for side, picks in enumerate(
        (((gload, 0), (gload, 1), (gdiag, 0)), ((gload, last - 1), (gload, last), (gdiag, last)))
    ):
        for k, (ref, row) in enumerate(picks):
            for h in range(half):
                at = edge + k * half + h
                rest[side, at : at + 1, :] = ref[row : row + 1, h * width : (h + 1) * width]


def first_kernel(cols, start, rest, stiff, terms):
    slots, block_rows, per_row = stiff.shape[:3]

    def vector(s, c):
        return start[lax.div(c, block_rows), s, pl.ds(lax.rem(c, block_rows), 1), :]

    terms[:, block_rows * per_row :, :] = rest[...]
    contract(stiff, cols, vector, terms)


def second_kernel(cols, maps, first, pack, stiff, resid, direc, terms, send, xown, pown, hot):
    slots, block_rows, per_row, width, _ = stiff.shape
    devices = pack.shape[0]
    blocks = devices * block_rows
    count = block_rows * per_row
    me = lax.axis_index("sub")
    start = stacked(first, 0, block_rows)
    dsum = stacked(pack, count, block_rows)
    targets(pack, count + block_rows + 1, hot)
    back = landed(hot, pack, count)
    image = jnp.where(dsum > 0.0, dsum * start + back, 0.0)
    head, scal = [], []
    for s in range(slots):
        span = slice(s * blocks, (s + 1) * blocks)
        r0, q0 = start[span], image[span]
        norm = total(r0 * r0)
        alpha = norm / total(r0 * q0)
        r1 = r0 - alpha * q0
        norm1 = total(r1 * r1)
        p1 = r1 + norm1 / norm * r0
        resid[span, :] = r1
        direc[span, :] = p1
        scal.append((norm1, total(dsum[span] * p1 * p1)))
        xown[s] = alpha * first[me, s]
        pown[s] = direc[pl.ds(s * blocks + me * block_rows, block_rows), :]
        head.append(pack[me, s, count + block_rows : count + block_rows + 1, :])
    squares = contract(stiff, cols, lambda s, c: direc[pl.ds(s * blocks + c, 1), :], terms)
    write_send(send, maps, head, [xown[s, 0:1, :] for s in range(slots)], pown, scal, squares, devices)
    everyone, used = send.shape[0], 3 * slots + 1
    group = lax.axis_index("grp")
    groups = everyone // devices
    edge = count + block_rows + 8
    send[:, used : used + 1, :] = jnp.zeros((everyone, 1, width), F32)

    @pl.when((group > 0) & (me < 8))
    def _():
        send[group * devices - 1, used : used + 1, :] = pack[0, 0, pl.ds(edge + me, 1), :]

    @pl.when((group < groups - 1) & (me < 8))
    def _():
        send[(group + 1) * devices, used : used + 1, :] = pack[devices - 1, 1, pl.ds(edge + me, 1), :]


def write_send(send, maps, pen, x_face, pown, scal, squares, devices):
    slots, width = len(x_face), x_face[0].shape[1]
    lane = iota((1, width), 1)
    rows = [pen[s] * x_face[s] for s in range(slots)]
    rows += [pen[s] * pown[s, 0:1, :] for s in range(slots)]
    row = jnp.zeros((1, width), F32)
    for s in range(slots):
        norm1, own = scal[s]
        image = total(squares[s]) + own * (1.0 / devices)
        row = jnp.where(lane == 2 * s, image, row)
        row = jnp.where(lane == 2 * s + 1, norm1 * (1.0 / devices), row)
    if maps is None:
        rows += [row, jnp.zeros((slots - 1, width), F32)]
        out = jnp.concatenate(rows, axis=0)
        for k in range(3):
            part = out[None, k * slots : (k + 1) * slots, :]
            send[:, k] = jnp.broadcast_to(part, (send.shape[0], slots, width))
        return
    rows += [maps[...], row]
    send[:, : 3 * slots + 1, :] = jnp.broadcast_to(
        jnp.concatenate(rows, axis=0)[None], (send.shape[0], 3 * slots + 1, width)
    )


def reactions(row_of, groups, slots):
    sums = row_of(-1)
    devices, width = sums.shape
    both = sums.reshape(groups, devices // groups, width).sum(axis=1)
    alphas, lams = [], []
    for s in range(slots):
        alpha = both[:, 2 * s + 1 : 2 * s + 2] / both[:, 2 * s : 2 * s + 1]
        alpha = jnp.broadcast_to(alpha, (groups, width))
        wide = jnp.broadcast_to(alpha[:, None, :], (groups, devices // groups, width))
        alphas.append(alpha)
        lams.append(row_of(s) + wide.reshape(devices, width) * row_of(slots + s))
    return alphas, lams


def split_lams(lams, part_s):
    for s, lam in enumerate(lams):
        hi = lam.astype(BF16).astype(F32)
        mid = (lam - hi).astype(BF16).astype(F32)
        part_s[0, s] = hi
        part_s[1, s] = mid
        part_s[2, s] = lam - hi - mid


def lanes_of(ref, d, slots):
    return jnp.concatenate([ref[s, pl.ds(d, 1), :] for s in range(slots)], axis=1)


def place(row_s, part_s, window, hot_of):
    _, slots, devices, _ = part_s.shape
    rows, columns = window
    ids_r = iota((rows, 1), 0).astype(F32)

    def step(c, acc):
        lefts, hots = [], []
        for d in [c * CHUNK + i for i in range(CHUNK)]:
            hit = ids_r == lanes_of(row_s, d, slots)
            lefts.append(
                jnp.concatenate(
                    [jnp.where(hit, lanes_of(part_s.at[i], d, slots), 0.0).astype(BF16) for i in range(3)],
                    axis=0,
                )
            )
            hots.append(hot_of(d))
        return acc + lax.dot_general(
            jnp.concatenate(lefts, axis=1),
            jnp.concatenate(hots, axis=1),
            (((1,), (1,)), ((), ())),
            preferred_element_type=F32,
        )

    acc = lax.fori_loop(0, devices // CHUNK, step, jnp.zeros((3 * rows, columns), F32))
    return acc[:rows] + acc[rows : 2 * rows] + acc[2 * rows :]


def stencil(ref, gdiag, first, count):
    here = ref[first : first + count, :]
    columns = here.shape[1]
    lane = iota(here.shape, 1)
    left = jnp.where(lane == 0, 0.0, pltpu.roll(here, 1, 1))
    right = jnp.where(lane == columns - 1, 0.0, pltpu.roll(here, columns - 1, 1))
    above = ref[first - 1 : first + count - 1, :]
    below = ref[first + 1 : first + count + 1, :]
    return (4.0 + gdiag) * here - (above + below + left + right)


def third_kernel(got, pack, loads_in, diags_in, window, loads, diags, alphas_out, send, row_s, hot_s, part_s, col_s):
    rows, columns = window.shape[0] - 2 * EDGE, window.shape[1]
    slots, devices, width = row_s.shape
    groups = lax.axis_size("grp")
    flat = lax.axis_index("grp") * lax.axis_size("sub") + lax.axis_index("sub")
    first_row = (flat * rows - EDGE).astype(F32)
    alphas, lams = reactions(lambda r: got[:, 3 * slots if r < 0 else r, :], groups, slots)
    for s in range(slots):
        alphas_out[s, 0:groups, :] = alphas[s]
    split_lams(lams, part_s)
    for s in range(slots):
        where = got[:, 2 * slots + s, :]
        row = jnp.floor(where * (1.0 / columns))
        col_s[s] = where - row * columns
        row_s[s] = row - first_row
    me, group = lax.axis_index("sub"), lax.axis_index("grp")
    near = devices // groups
    half, edge, spare = columns // width, pack.shape[2] - 8, 3 * slots + 1
    loads[...] = loads_in[...]
    diags[...] = diags_in[...]
    last = EDGE + rows

    def fill(side, row_of):
        first = EDGE - 2 if side else last
        diag_row = EDGE - 1 if side else last
        for h in range(half):
            lanes = slice(h * width, (h + 1) * width)
            loads[first : first + 1, lanes] = row_of(h)
            loads[first + 1 : first + 2, lanes] = row_of(half + h)
            diags[diag_row : diag_row + 1, lanes] = row_of(2 * half + h)

    @pl.when(me > 0)
    def _():
        fill(1, lambda k: pack[me - 1, 1, edge + k : edge + k + 1, :])

    @pl.when((me == 0) & (group > 0))
    def _():
        fill(1, lambda k: got[(group - 1) * near + k, spare : spare + 1, :])

    @pl.when(me < near - 1)
    def _():
        fill(0, lambda k: pack[me + 1, 0, edge + k : edge + k + 1, :])

    @pl.when((me == near - 1) & (group < groups - 1))
    def _():
        fill(0, lambda k: got[(group + 1) * near + k, spare : spare + 1, :])

    extent = window.shape
    ids_c = iota((columns, 1), 0).astype(F32)

    def hot_of(d):
        hot = jnp.where(ids_c == lanes_of(col_s, d, slots), 1.0, 0.0).astype(BF16)
        hot_s[d] = hot
        return hot

    placed = place(row_s, part_s, extent, hot_of)
    at = iota(extent, 0)
    inside = (at >= EDGE - 2) & (at < last + 2)
    window[...] = loads[...] + jnp.where(inside, placed, 0.0)
    own = window[EDGE:last, :]
    image = stencil(window, diags[EDGE:last, :], EDGE, rows)
    faces = slots * near
    send[:, faces:, :] = jnp.zeros((groups, send.shape[1] - faces, width), F32)
    send[:, faces : faces + 1, :] = jnp.broadcast_to(total(own * own)[None], (groups, 1, width))
    send[:, faces + 1 : faces + 2, :] = jnp.broadcast_to(total(own * image)[None], (groups, 1, width))
    parts = jnp.concatenate(split3(own), axis=0)
    ids = iota((rows, 1), 0).astype(F32) + EDGE

    for g in range(groups):
        for k in range(near):
            d = g * near + k
            seen = jnp.dot(parts, hot_s[d], preferred_element_type=F32)
            seen = seen[:rows] + seen[rows : 2 * rows] + seen[2 * rows :]
            hit = ids == lanes_of(row_s, d, slots)
            mine = jnp.sum(jnp.where(hit, seen, 0.0), axis=0, keepdims=True)
            for s in range(slots):
                send[g, s * near + k : s * near + k + 1, :] = mine[:, s * width : (s + 1) * width]


def share_kernel(got, terms, send):
    slots, count, width = terms.shape
    near = lax.axis_size("sub")
    sums = got[0]
    for g in range(1, got.shape[0]):
        sums = sums + got[g]
    send[:, :count, :] = terms[...]
    for s in range(slots):
        send[s, count : count + near, :] = sums[s * near : (s + 1) * near, :]
        send[s, count + near :, :] = sums[slots * near : slots * near + 8, :]


def fourth_kernel(
    cols, pack, arrived, hot, window, alphas, resid, direc, xown, pown, stiff, start, terms, xnext, face, field
):
    slots, block_rows, per_row, width, _ = stiff.shape
    devices = pack.shape[0]
    blocks = devices * block_rows
    count = block_rows * per_row
    group = lax.axis_index("grp")
    me = lax.axis_index("sub")
    dsum = stacked(pack, count, block_rows)
    back = landed(hot, arrived, count)
    p1 = direc[...]
    image = jnp.where(dsum > 0.0, dsum * p1 + back, 0.0)
    tail = arrived[0, :, count:, :]
    for d in range(1, devices):
        tail = tail + arrived[d, :, count:, :]
    scale = tail[0, devices : devices + 1, :] / tail[0, devices + 1 : devices + 2, :]
    field[...] = window[...] * jnp.concatenate([scale] * (field.shape[1] // width), axis=1)
    for s in range(slots):
        span = slice(s * blocks, (s + 1) * blocks)
        alpha = alphas[s, pl.ds(group, 1), :]
        start[span, :] = resid[span, :] - alpha * image[span]
        xnext[s] = xown[s] + alpha * pown[s]
        face[s, :devices, :] = scale * tail[s, :devices, :]
        for d in range(devices):
            at = slice(s * blocks + d * block_rows, s * blocks + d * block_rows + 1)
            pen = pack[d, s, count + block_rows : count + block_rows + 1, :]
            start[at, :] = start[at, :] + pen * face[s, d : d + 1, :]
    contract(stiff, cols, lambda s, c: start[pl.ds(s * blocks + c, 1), :], terms)


def fifth_kernel(cols, pack, arrived, hot, bound, start, xin, stiff, send, xown, pown, direc):
    slots, block_rows, per_row, width, _ = stiff.shape
    devices = pack.shape[0]
    blocks = devices * block_rows
    count = block_rows * per_row
    me = lax.axis_index("sub")
    dsum = stacked(pack, count, block_rows)
    back = landed(hot, arrived, count)
    image = jnp.where(dsum > 0.0, dsum * start[...] + back, 0.0)
    head, face, scal = [], [], []
    for s in range(slots):
        span = slice(s * blocks, (s + 1) * blocks)
        r0, q0 = start[span, :], image[span]
        norm = total(r0 * r0)
        alpha = norm / total(r0 * q0)
        r1 = r0 - alpha * q0
        norm1 = total(r1 * r1)
        p1 = r1 + norm1 / norm * r0
        direc[span, :] = p1
        scal.append((norm1, total(dsum[span] * p1 * p1)))
        mine = pl.ds(s * blocks + me * block_rows, block_rows)
        xown[s] = xin[s] + alpha * start[mine, :]
        pown[s] = direc[mine, :]
        head.append(pack[me, s, count + block_rows : count + block_rows + 1, :])
        face.append(xown[s, 0:1, :] - bound[s, pl.ds(me, 1), :])
    squares = contract(stiff, cols, lambda s, c: direc[pl.ds(s * blocks + c, 1), :], None)
    write_send(send, None, head, face, pown, scal, squares, devices)


def sixth_kernel(got, loads, diags, field, xown, pown, row_s, hot_s, resid, xout, send, window, part_s):
    slots, devices, width = row_s.shape
    rows, columns = resid.shape
    groups = lax.axis_size("grp")
    group = lax.axis_index("grp")
    flat = group * lax.axis_size("sub") + lax.axis_index("sub")
    alphas, lams = reactions(
        lambda r: got[:, 2, 0, :] if r < 0 else got[:, r // slots, r % slots, :], groups, slots
    )
    for s in range(slots):
        part_s[0, s, 0:groups, :] = alphas[s]
        alpha = part_s[0, s, pl.ds(group, 1), :]
        for b in range(xown.shape[1]):
            xout[s : s + 1, b * width : (b + 1) * width] = (
                xown[s, b : b + 1, :] + alpha * pown[s, b : b + 1, :]
            )
    split_lams(lams, part_s)
    placed = place(row_s, part_s, window.shape, lambda d: hot_s[d])
    span = slice(EDGE - 1, EDGE + rows + 1)
    applied = stencil(field, diags[span, :], EDGE - 1, rows + 2)
    at = iota(applied.shape, 0) + (flat * rows - 1)
    inside = (at >= 0) & (at < devices * rows)
    window[...] = jnp.zeros_like(window)
    window[span, :] = jnp.where(inside, loads[span, :] - applied + placed[span], 0.0)
    own = window[EDGE : EDGE + rows, :]
    resid[...] = own
    image = stencil(window, diags[EDGE : EDGE + rows, :], EDGE, rows)
    send[:, 0:1, :] = jnp.broadcast_to(total(own * own)[None], (devices, 1, width))
    send[:, 1:2, :] = jnp.broadcast_to(total(own * image)[None], (devices, 1, width))


def last_kernel(got, field, resid, out):
    sums = jnp.sum(got[...], axis=0)
    scale = sums[0:1, :] / sums[1:2, :]
    rows, columns = out.shape
    wide = jnp.concatenate([scale] * (columns // got.shape[2]), axis=1)
    out[...] = field[EDGE : EDGE + rows, :] + wide * resid[...]


def call(kernel, shapes, operands, scalars=0, raw=0, scratch=(), limit=4, plain=(), cost=None):
    operands = [
        pltpu.with_memory_space_constraint(x, pltpu.HBM if i < raw else pltpu.VMEM)
        for i, x in enumerate(operands)
    ]
    out_shape = [
        jax.ShapeDtypeStruct(s, d) if i in plain else pltpu.VMEM(s, d) for i, (s, d) in enumerate(shapes)
    ]
    return pl.pallas_call(
        kernel,
        out_shape=out_shape,
        in_specs=[SMEM] * scalars + [VMEM] * (len(operands) - scalars),
        out_specs=[VMEM] * len(shapes),
        scratch_shapes=list(scratch),
        compiler_params=pltpu.CompilerParams(vmem_limit_bytes=limit << 20),
        cost_estimate=cost,
    )(*operands)


def body(
    stiff_blocks,
    block_cols,
    live_blocks,
    sub_diag,
    penalty,
    sub_load,
    iface_map,
    global_load,
    global_diag,
):
    slots, block_rows, per_row, width, _ = stiff_blocks.shape
    rows_dev = block_rows * width
    rows, columns = global_load.shape
    near, groups = lax.axis_size("sub"), lax.axis_size("grp")
    devices = near * groups
    blocks = slots * near * block_rows
    count = block_rows * per_row
    extent = ((rows + 2 * EDGE, columns), F32)
    own = ((slots, block_rows, width), F32)
    full = ((blocks, width), F32)
    every = ((slots, count, width), F32)
    landing = ((slots, near * block_rows, near * count), BF16)
    cols = jnp.transpose(block_cols, (0, 2, 1))

    def everywhere(x):
        return lax.all_to_all(x, ALL, 0, 0)

    def near_all(x):
        return lax.all_gather(x, "sub")

    send, rest, cols, maps, loads, diags = call(
        prep_kernel,
        [
            ((near, slots, block_rows, width), F32),
            ((slots, block_rows + 16, width), F32),
            (cols.shape, jnp.int32),
            (iface_map.shape, F32),
            extent,
            extent,
        ],
        (live_blocks.reshape(1, slots), sub_diag, penalty, sub_load, cols, iface_map, global_load, global_diag),
        raw=8,
        cost=pl.CostEstimate(flops=20_000_000_000, bytes_accessed=0, transcendentals=0),
    )
    first = lax.all_to_all(send, "sub", 0, 0)
    stiff = stiff_blocks
    (terms,) = call(
        first_kernel,
        [((slots, count + rest.shape[1], width), F32)],
        (cols, first, rest, stiff),
        scalars=1,
    )
    pack = near_all(terms)
    resid, direc, terms, send, xown, pown, hot = call(
        second_kernel,
        [full, full, every, ((devices, 4 * slots, width), F32), own, own, landing],
        (cols, maps, first, pack, stiff),
        scalars=1,
    )
    got = everywhere(send)
    listed = (slots, devices, width)
    parts = pltpu.VMEM((3,) + listed, F32)
    window, loads, diags, alphas, send, row_s, hot_s = call(
        third_kernel,
        [
            extent,
            extent,
            extent,
            ((slots, max(8, groups), width), F32),
            ((groups, slots * near + 8, width), F32),
            (listed, F32),
            ((devices, columns, slots * width), BF16),
        ],
        (got, pack, loads, diags),
        scratch=(parts, pltpu.VMEM(listed, F32)),
    )
    sums = lax.all_to_all(send, "grp", 0, 0)
    (send,) = call(share_kernel, [((slots, count + near + 8, width), F32)], (sums, terms))
    arrived = near_all(send)
    start, terms, xown, bound, field = call(
        fourth_kernel,
        [full, every, own, ((slots, max(8, near), width), F32), extent],
        (cols, pack, arrived, hot, window, alphas, resid, direc, xown, pown, stiff),
        scalars=1,
    )
    arrived = near_all(terms)
    send, xown, pown = call(
        fifth_kernel,
        [((devices, 3, slots, width), F32), own, own],
        (cols, pack, arrived, hot, bound, start, xown, stiff),
        scalars=1,
        scratch=(pltpu.VMEM(full[0], F32),),
    )
    got = everywhere(send)
    resid, sub_field, send = call(
        sixth_kernel,
        [((rows, columns), F32), ((slots, rows_dev), F32), ((devices, 2, width), F32)],
        (got, loads, diags, field, xown, pown, row_s, hot_s),
        scratch=(pltpu.VMEM(extent[0], F32), parts),
        plain=(1,),
    )
    sums = everywhere(send)
    (global_field,) = call(last_kernel, [((rows, columns), F32)], (sums, field, resid), plain=(0,))
    return global_field, sub_field


def solution(mesh):
    return jax.shard_map(
        body,
        mesh=mesh,
        in_specs=(
            P("grp", "sub", None, None, None),
            P("grp", "sub", None),
            P("grp", "sub"),
            P("grp", "sub"),
            P("grp", "sub"),
            P("grp", "sub"),
            P("grp", "sub"),
            P(ALL, None),
            P(ALL, None),
        ),
        out_specs=(P(ALL, None), P("grp", "sub")),
        check_vma=False,
    )
```

```python
import jax
import jax.numpy as jnp
from jax import lax
from jax.experimental import pallas as pl
from jax.experimental.pallas import tpu as pltpu
from jax.sharding import PartitionSpec as P

F32 = jnp.float32
BF16 = jnp.bfloat16
CHUNK = 16
EDGE = 8
ALL = ("grp", "sub")

VMEM = pl.BlockSpec(memory_space=pltpu.VMEM)
SMEM = pl.BlockSpec(memory_space=pltpu.SMEM)


def total(x):
    return jnp.sum(jnp.sum(x, axis=0, keepdims=True), axis=1, keepdims=True)


def split3(x):
    hi = x.astype(BF16)
    rest = x - hi.astype(F32)
    mid = rest.astype(BF16)
    return hi, mid, (rest - mid.astype(F32)).astype(BF16)


def matches(ids, wanted):
    kind = BF16 if ids.shape[0] <= 256 else F32
    same = ids.astype(F32).astype(kind) == wanted.astype(kind)
    return jnp.where(same, jnp.ones((), kind), jnp.zeros((), kind)).astype(BF16)


def iota(shape, dim):
    return lax.broadcasted_iota(jnp.int32, shape, dim)


def contract(stiff, cols, vector, terms, arrive=None):
    slots, block_rows, per_row, width, _ = stiff.shape
    squares = []
    for s in range(slots):

        def row(r, acc, s=s):
            if arrive is not None:
                arrive(s, r)
            prod = None
            for n in range(per_row):
                part = stiff[s, r, n] * vector(s, cols[s, n, r])
                prod = part if prod is None else prod + part
            strain = jnp.sum(prod, axis=1, keepdims=True)
            if terms is not None:
                for n in range(per_row):
                    terms[s, pl.ds(n * block_rows + r, 1), :] = jnp.sum(
                        stiff[s, r, n] * strain, axis=0, keepdims=True
                    )
            return acc + strain * strain

        acc = jnp.zeros((width, 1), F32)
        for r in range(block_rows):
            acc = row(r, acc)
        squares.append(acc)
    return squares


def stacked(gathered, first, count):
    devices, slots = gathered.shape[:2]
    return jnp.concatenate(
        [gathered[d, s, first : first + count, :] for s in range(slots) for d in range(devices)],
        axis=0,
    )


def targets(pack, row, hot):
    count = hot.shape[2] // pack.shape[0]
    for s in range(hot.shape[0]):
        col = jnp.concatenate(
            [pack[d, 0, row : row + 1, s * count : (s + 1) * count] for d in range(pack.shape[0])], axis=1
        )
        hot[s] = matches(iota(hot.shape[1:], 0), col)


def landed(hot, arrived, count):
    devices, slots, _, width = arrived.shape
    sums = []
    for s in range(slots):
        source = jnp.concatenate([arrived[d, s, :count, :] for d in range(devices)], axis=0)
        out = jnp.dot(hot[s], jnp.concatenate(split3(source), axis=1), preferred_element_type=F32)
        sums.append(out[:, :width] + out[:, width : 2 * width] + out[:, 2 * width :])
    return jnp.concatenate(sums, axis=0)


def prep_kernel(live, diag, pen, load, cols, maps, gload, gdiag, send, rest, cols_out, maps_out, loads, diags):
    slots, block_rows, width = send.shape[1:]
    per_row = cols.shape[1]
    first, rows = [], gload.shape[0]
    rest[...] = jnp.zeros_like(rest)
    for s in range(slots):
        count = live[:, s : s + 1]
        for b in range(block_rows):
            lanes = pl.ds(b * width, width)
            on = count > b
            main = diag[s : s + 1, lanes]
            if b == 0:
                main = main + pen[s : s + 1, :]
            first.append(jnp.where(on, load[s : s + 1, lanes], 0.0))
            rest[s, b : b + 1, :] = jnp.where(on, main, 0.0)
        rest[s, block_rows : block_rows + 1, :] = pen[s : s + 1, :]
        for n in range(per_row):
            at = (s * per_row + n) * block_rows
            rest[0, block_rows + 1 : block_rows + 2, at : at + block_rows] = (
                cols[s, n : n + 1, :]
            ).astype(F32)
    all_first = jnp.concatenate(first, axis=0).reshape(1, slots, block_rows, width)
    send[...] = jnp.broadcast_to(all_first, send.shape)
    cols_out[...] = cols[...]
    maps_out[...] = maps[...].astype(F32)
    loads[...] = jnp.zeros_like(loads)
    diags[...] = jnp.zeros_like(diags)
    loads[EDGE : EDGE + rows, :] = gload[...]
    diags[EDGE : EDGE + rows, :] = gdiag[...]
    last = rows - 1
    half = gload.shape[1] // width
    edge = block_rows + 8
    for side, picks in enumerate(
        (((gload, 0), (gload, 1), (gdiag, 0)), ((gload, last - 1), (gload, last), (gdiag, last)))
    ):
        for k, (ref, row) in enumerate(picks):
            for h in range(half):
                at = edge + k * half + h
                rest[side, at : at + 1, :] = ref[row : row + 1, h * width : (h + 1) * width]


def first_kernel(cols, start, rest, stiff, terms):
    slots, block_rows, per_row = stiff.shape[:3]

    def vector(s, c):
        return start[lax.div(c, block_rows), s, pl.ds(lax.rem(c, block_rows), 1), :]

    terms[:, block_rows * per_row :, :] = rest[...]
    contract(stiff, cols, vector, terms)


def second_kernel(cols, maps, first, pack, stiff, resid, direc, terms, send, xown, pown, hot):
    slots, block_rows, per_row, width, _ = stiff.shape
    devices = pack.shape[0]
    blocks = devices * block_rows
    count = block_rows * per_row
    me = lax.axis_index("sub")
    start = stacked(first, 0, block_rows)
    dsum = stacked(pack, count, block_rows)
    targets(pack, count + block_rows + 1, hot)
    back = landed(hot, pack, count)
    image = jnp.where(dsum > 0.0, dsum * start + back, 0.0)
    head, scal = [], []
    for s in range(slots):
        span = slice(s * blocks, (s + 1) * blocks)
        r0, q0 = start[span], image[span]
        norm = total(r0 * r0)
        alpha = norm / total(r0 * q0)
        r1 = r0 - alpha * q0
        norm1 = total(r1 * r1)
        p1 = r1 + norm1 / norm * r0
        resid[span, :] = r1
        direc[span, :] = p1
        scal.append((norm1, total(dsum[span] * p1 * p1)))
        xown[s] = alpha * first[me, s]
        pown[s] = direc[pl.ds(s * blocks + me * block_rows, block_rows), :]
        head.append(pack[me, s, count + block_rows : count + block_rows + 1, :])
    squares = contract(stiff, cols, lambda s, c: direc[pl.ds(s * blocks + c, 1), :], terms)
    write_send(send, maps, head, [xown[s, 0:1, :] for s in range(slots)], pown, scal, squares, devices)
    everyone, used = send.shape[0], 3 * slots + 1
    group = lax.axis_index("grp")
    groups = everyone // devices
    edge = count + block_rows + 8
    send[:, used : used + 1, :] = jnp.zeros((everyone, 1, width), F32)

    @pl.when((group > 0) & (me < 8))
    def _():
        send[group * devices - 1, used : used + 1, :] = pack[0, 0, pl.ds(edge + me, 1), :]

    @pl.when((group < groups - 1) & (me < 8))
    def _():
        send[(group + 1) * devices, used : used + 1, :] = pack[devices - 1, 1, pl.ds(edge + me, 1), :]


def write_send(send, maps, pen, x_face, pown, scal, squares, devices):
    slots, width = len(x_face), x_face[0].shape[1]
    lane = iota((1, width), 1)
    rows = [pen[s] * x_face[s] for s in range(slots)]
    rows += [pen[s] * pown[s, 0:1, :] for s in range(slots)]
    row = jnp.zeros((1, width), F32)
    for s in range(slots):
        norm1, own = scal[s]
        image = total(squares[s]) + own * (1.0 / devices)
        row = jnp.where(lane == 2 * s, image, row)
        row = jnp.where(lane == 2 * s + 1, norm1 * (1.0 / devices), row)
    if maps is None:
        rows += [row, jnp.zeros((slots - 1, width), F32)]
        out = jnp.concatenate(rows, axis=0)
        for k in range(3):
            part = out[None, k * slots : (k + 1) * slots, :]
            send[:, k] = jnp.broadcast_to(part, (send.shape[0], slots, width))
        return
    rows += [maps[...], row]
    send[:, : 3 * slots + 1, :] = jnp.broadcast_to(
        jnp.concatenate(rows, axis=0)[None], (send.shape[0], 3 * slots + 1, width)
    )


def reactions(row_of, groups, slots):
    sums = row_of(-1)
    devices, width = sums.shape
    both = sums.reshape(groups, devices // groups, width).sum(axis=1)
    alphas, lams = [], []
    for s in range(slots):
        alpha = both[:, 2 * s + 1 : 2 * s + 2] / both[:, 2 * s : 2 * s + 1]
        alpha = jnp.broadcast_to(alpha, (groups, width))
        wide = jnp.broadcast_to(alpha[:, None, :], (groups, devices // groups, width))
        alphas.append(alpha)
        lams.append(row_of(s) + wide.reshape(devices, width) * row_of(slots + s))
    return alphas, lams


def split_lams(lams, part_s):
    for s, lam in enumerate(lams):
        hi = lam.astype(BF16).astype(F32)
        mid = (lam - hi).astype(BF16).astype(F32)
        part_s[0, s] = hi
        part_s[1, s] = mid
        part_s[2, s] = lam - hi - mid


def lanes_of(ref, d, slots):
    return jnp.concatenate([ref[s, pl.ds(d, 1), :] for s in range(slots)], axis=1)


def place(row_s, part_s, window, hot_of, chunk):
    _, slots, devices, _ = part_s.shape
    rows, columns = window
    ids_r = iota((rows, slots * part_s.shape[3]), 0).astype(F32).astype(BF16)

    def step(c, acc):
        lefts, hots = [], []
        for d in [c * chunk + i for i in range(chunk)]:
            hit = ids_r == lanes_of(row_s, d, slots).astype(BF16)
            lefts.append(
                jnp.concatenate(
                    [jnp.where(hit, lanes_of(part_s.at[i], d, slots).astype(BF16), jnp.zeros((), BF16)) for i in range(3)],
                    axis=0,
                )
            )
            hots.append(hot_of(d))
        return acc + lax.dot_general(
            jnp.concatenate(lefts, axis=1),
            jnp.concatenate(hots, axis=1),
            (((1,), (1,)), ((), ())),
            preferred_element_type=F32,
        )

    acc = jnp.zeros((3 * rows, columns), F32)
    acc = step(0, acc) if chunk == devices else lax.fori_loop(0, devices // chunk, step, acc)
    return acc[:rows] + acc[rows : 2 * rows] + acc[2 * rows :]


def stencil(ref, gdiag, first, count):
    here = ref[first : first + count, :]
    columns = here.shape[1]
    lane = iota(here.shape, 1)
    left = jnp.where(lane == 0, 0.0, pltpu.roll(here, 1, 1))
    right = jnp.where(lane == columns - 1, 0.0, pltpu.roll(here, columns - 1, 1))
    above = ref[first - 1 : first + count - 1, :]
    below = ref[first + 1 : first + count + 1, :]
    return (4.0 + gdiag) * here - (above + below + left + right)


def third_kernel(got, pack, loads_in, diags_in, window, loads, diags, alphas_out, send, row_s, hot_s, part_s, col_s):
    rows, columns = window.shape[0] - 2 * EDGE, window.shape[1]
    slots, devices, width = row_s.shape
    groups = lax.axis_size("grp")
    flat = lax.axis_index("grp") * lax.axis_size("sub") + lax.axis_index("sub")
    first_row = (flat * rows - EDGE).astype(F32)
    alphas, lams = reactions(lambda r: got[:, 3 * slots if r < 0 else r, :], groups, slots)
    for s in range(slots):
        alphas_out[s, 0:groups, :] = alphas[s]
    split_lams(lams, part_s)
    for s in range(slots):
        where = got[:, 2 * slots + s, :]
        row = jnp.floor(where * (1.0 / columns))
        col_s[s] = where - row * columns
        row_s[s] = row - first_row
    me, group = lax.axis_index("sub"), lax.axis_index("grp")
    near = devices // groups
    half, edge, spare = columns // width, pack.shape[2] - 8, 3 * slots + 1
    loads[...] = loads_in[...]
    diags[...] = diags_in[...]
    last = EDGE + rows

    def fill(side, row_of):
        first = EDGE - 2 if side else last
        diag_row = EDGE - 1 if side else last
        for h in range(half):
            lanes = slice(h * width, (h + 1) * width)
            loads[first : first + 1, lanes] = row_of(h)
            loads[first + 1 : first + 2, lanes] = row_of(half + h)
            diags[diag_row : diag_row + 1, lanes] = row_of(2 * half + h)

    @pl.when(me > 0)
    def _():
        fill(1, lambda k: pack[me - 1, 1, edge + k : edge + k + 1, :])

    @pl.when((me == 0) & (group > 0))
    def _():
        fill(1, lambda k: got[(group - 1) * near + k, spare : spare + 1, :])

    @pl.when(me < near - 1)
    def _():
        fill(0, lambda k: pack[me + 1, 0, edge + k : edge + k + 1, :])

    @pl.when((me == near - 1) & (group < groups - 1))
    def _():
        fill(0, lambda k: got[(group + 1) * near + k, spare : spare + 1, :])

    extent = window.shape
    ids_c = iota((columns, slots * width), 0)

    def hot_of(d):
        hot = matches(ids_c, lanes_of(col_s, d, slots))
        hot_s[d] = hot
        return hot

    placed = place(row_s, part_s, extent, hot_of, CHUNK)
    at = iota(extent, 0)
    inside = (at >= EDGE - 2) & (at < last + 2)
    window[...] = loads[...] + jnp.where(inside, placed, 0.0)
    own = window[EDGE:last, :]
    image = stencil(window, diags[EDGE:last, :], EDGE, rows)
    faces = slots * near
    send[:, faces:, :] = jnp.zeros((groups, send.shape[1] - faces, width), F32)
    send[:, faces : faces + 1, :] = jnp.broadcast_to(total(own * own)[None], (groups, 1, width))
    send[:, faces + 1 : faces + 2, :] = jnp.broadcast_to(total(own * image)[None], (groups, 1, width))
    parts = jnp.concatenate(split3(own), axis=0)
    ids = iota((rows, 1), 0).astype(F32) + EDGE

    for g in range(groups):
        for k in range(near):
            d = g * near + k
            seen = jnp.dot(parts, hot_s[d], preferred_element_type=F32)
            seen = seen[:rows] + seen[rows : 2 * rows] + seen[2 * rows :]
            hit = ids == lanes_of(row_s, d, slots)
            mine = jnp.sum(jnp.where(hit, seen, 0.0), axis=0, keepdims=True)
            for s in range(slots):
                send[g, s * near + k : s * near + k + 1, :] = mine[:, s * width : (s + 1) * width]


def share_kernel(got, terms, send):
    slots, count, width = terms.shape
    near = lax.axis_size("sub")
    sums = got[0]
    for g in range(1, got.shape[0]):
        sums = sums + got[g]
    send[:, :count, :] = terms[...]
    for s in range(slots):
        send[s, count : count + near, :] = sums[s * near : (s + 1) * near, :]
        send[s, count + near :, :] = sums[slots * near : slots * near + 8, :]


def fourth_kernel(
    cols, pack, arrived, hot, window, alphas, resid, direc, xown, pown, stiff, start, terms, xnext, face, field
):
    slots, block_rows, per_row, width, _ = stiff.shape
    devices = pack.shape[0]
    blocks = devices * block_rows
    count = block_rows * per_row
    group = lax.axis_index("grp")
    me = lax.axis_index("sub")
    dsum = stacked(pack, count, block_rows)
    back = landed(hot, arrived, count)
    p1 = direc[...]
    image = jnp.where(dsum > 0.0, dsum * p1 + back, 0.0)
    tail = arrived[0, :, count:, :]
    for d in range(1, devices):
        tail = tail + arrived[d, :, count:, :]
    scale = tail[0, devices : devices + 1, :] / tail[0, devices + 1 : devices + 2, :]
    field[...] = window[...] * jnp.concatenate([scale] * (field.shape[1] // width), axis=1)
    for s in range(slots):
        span = slice(s * blocks, (s + 1) * blocks)
        alpha = alphas[s, pl.ds(group, 1), :]
        start[span, :] = resid[span, :] - alpha * image[span]
        xnext[s] = xown[s] + alpha * pown[s]
        face[s, :devices, :] = scale * tail[s, :devices, :]
        for d in range(devices):
            at = slice(s * blocks + d * block_rows, s * blocks + d * block_rows + 1)
            pen = pack[d, s, count + block_rows : count + block_rows + 1, :]
            start[at, :] = start[at, :] + pen * face[s, d : d + 1, :]
    contract(stiff, cols, lambda s, c: start[pl.ds(s * blocks + c, 1), :], terms)


def fifth_kernel(cols, pack, arrived, hot, bound, start, xin, stiff, send, xown, pown, direc):
    slots, block_rows, per_row, width, _ = stiff.shape
    devices = pack.shape[0]
    blocks = devices * block_rows
    count = block_rows * per_row
    me = lax.axis_index("sub")
    dsum = stacked(pack, count, block_rows)
    back = landed(hot, arrived, count)
    image = jnp.where(dsum > 0.0, dsum * start[...] + back, 0.0)
    head, face, scal = [], [], []
    for s in range(slots):
        span = slice(s * blocks, (s + 1) * blocks)
        r0, q0 = start[span, :], image[span]
        norm = total(r0 * r0)
        alpha = norm / total(r0 * q0)
        r1 = r0 - alpha * q0
        norm1 = total(r1 * r1)
        p1 = r1 + norm1 / norm * r0
        direc[span, :] = p1
        scal.append((norm1, total(dsum[span] * p1 * p1)))
        mine = pl.ds(s * blocks + me * block_rows, block_rows)
        xown[s] = xin[s] + alpha * start[mine, :]
        pown[s] = direc[mine, :]
        head.append(pack[me, s, count + block_rows : count + block_rows + 1, :])
        face.append(xown[s, 0:1, :] - bound[s, pl.ds(me, 1), :])
    squares = contract(stiff, cols, lambda s, c: direc[pl.ds(s * blocks + c, 1), :], None)
    write_send(send, None, head, face, pown, scal, squares, devices)


def sixth_kernel(got, loads, diags, field, xown, pown, row_s, hot_s, resid, xout, send, window, part_s):
    slots, devices, width = row_s.shape
    rows, columns = resid.shape
    groups = lax.axis_size("grp")
    group = lax.axis_index("grp")
    flat = group * lax.axis_size("sub") + lax.axis_index("sub")
    alphas, lams = reactions(
        lambda r: got[:, 2, 0, :] if r < 0 else got[:, r // slots, r % slots, :], groups, slots
    )
    for s in range(slots):
        part_s[0, s, 0:groups, :] = alphas[s]
        alpha = part_s[0, s, pl.ds(group, 1), :]
        for b in range(xown.shape[1]):
            xout[s : s + 1, b * width : (b + 1) * width] = (
                xown[s, b : b + 1, :] + alpha * pown[s, b : b + 1, :]
            )
    split_lams(lams, part_s)
    placed = place(row_s, part_s, window.shape, lambda d: hot_s[d], min(2 * CHUNK, devices))
    span = slice(EDGE - 1, EDGE + rows + 1)
    applied = stencil(field, diags[span, :], EDGE - 1, rows + 2)
    at = iota(applied.shape, 0) + (flat * rows - 1)
    inside = (at >= 0) & (at < devices * rows)
    window[...] = jnp.zeros_like(window)
    window[span, :] = jnp.where(inside, loads[span, :] - applied + placed[span], 0.0)
    own = window[EDGE : EDGE + rows, :]
    resid[...] = own
    image = stencil(window, diags[EDGE : EDGE + rows, :], EDGE, rows)
    send[:, 0:1, :] = jnp.broadcast_to(total(own * own)[None], (devices, 1, width))
    send[:, 1:2, :] = jnp.broadcast_to(total(own * image)[None], (devices, 1, width))


def last_kernel(got, field, resid, out):
    sums = jnp.sum(got[...], axis=0)
    scale = sums[0:1, :] / sums[1:2, :]
    rows, columns = out.shape
    wide = jnp.concatenate([scale] * (columns // got.shape[2]), axis=1)
    out[...] = field[EDGE : EDGE + rows, :] + wide * resid[...]


def call(kernel, shapes, operands, scalars=0, raw=0, scratch=(), limit=4, plain=(), cost=None):
    operands = [
        pltpu.with_memory_space_constraint(x, pltpu.HBM if i < raw else pltpu.VMEM)
        for i, x in enumerate(operands)
    ]
    out_shape = [
        jax.ShapeDtypeStruct(s, d) if i in plain else pltpu.VMEM(s, d) for i, (s, d) in enumerate(shapes)
    ]
    return pl.pallas_call(
        kernel,
        out_shape=out_shape,
        in_specs=[SMEM] * scalars + [VMEM] * (len(operands) - scalars),
        out_specs=[VMEM] * len(shapes),
        scratch_shapes=list(scratch),
        compiler_params=pltpu.CompilerParams(vmem_limit_bytes=limit << 20),
        cost_estimate=cost,
    )(*operands)


def body(
    stiff_blocks,
    block_cols,
    live_blocks,
    sub_diag,
    penalty,
    sub_load,
    iface_map,
    global_load,
    global_diag,
):
    slots, block_rows, per_row, width, _ = stiff_blocks.shape
    rows_dev = block_rows * width
    rows, columns = global_load.shape
    near, groups = lax.axis_size("sub"), lax.axis_size("grp")
    devices = near * groups
    blocks = slots * near * block_rows
    count = block_rows * per_row
    extent = ((rows + 2 * EDGE, columns), F32)
    own = ((slots, block_rows, width), F32)
    full = ((blocks, width), F32)
    every = ((slots, count, width), F32)
    landing = ((slots, near * block_rows, near * count), BF16)
    cols = jnp.transpose(block_cols, (0, 2, 1))

    def everywhere(x):
        return lax.all_to_all(x, ALL, 0, 0)

    def near_all(x):
        return lax.all_gather(x, "sub")

    send, rest, cols, maps, loads, diags = call(
        prep_kernel,
        [
            ((near, slots, block_rows, width), F32),
            ((slots, block_rows + 16, width), F32),
            (cols.shape, jnp.int32),
            (iface_map.shape, F32),
            extent,
            extent,
        ],
        (live_blocks.reshape(1, slots), sub_diag, penalty, sub_load, cols, iface_map, global_load, global_diag),
        raw=8,
        cost=pl.CostEstimate(flops=20_000_000_000, bytes_accessed=0, transcendentals=0),
    )
    first = lax.all_to_all(send, "sub", 0, 0)
    stiff = stiff_blocks
    (terms,) = call(
        first_kernel,
        [((slots, count + rest.shape[1], width), F32)],
        (cols, first, rest, stiff),
        scalars=1,
    )
    pack = near_all(terms)
    resid, direc, terms, send, xown, pown, hot = call(
        second_kernel,
        [full, full, every, ((devices, 4 * slots, width), F32), own, own, landing],
        (cols, maps, first, pack, stiff),
        scalars=1,
    )
    got = everywhere(send)
    listed = (slots, devices, width)
    parts = pltpu.VMEM((3,) + listed, F32)
    window, loads, diags, alphas, send, row_s, hot_s = call(
        third_kernel,
        [
            extent,
            extent,
            extent,
            ((slots, max(8, groups), width), F32),
            ((groups, slots * near + 8, width), F32),
            (listed, F32),
            ((devices, columns, slots * width), BF16),
        ],
        (got, pack, loads, diags),
        scratch=(parts, pltpu.VMEM(listed, F32)),
    )
    sums = lax.all_to_all(send, "grp", 0, 0)
    (send,) = call(share_kernel, [((slots, count + near + 8, width), F32)], (sums, terms))
    arrived = near_all(send)
    start, terms, xown, bound, field = call(
        fourth_kernel,
        [full, every, own, ((slots, max(8, near), width), F32), extent],
        (cols, pack, arrived, hot, window, alphas, resid, direc, xown, pown, stiff),
        scalars=1,
    )
    arrived = near_all(terms)
    send, xown, pown = call(
        fifth_kernel,
        [((devices, 3, slots, width), F32), own, own],
        (cols, pack, arrived, hot, bound, start, xown, stiff),
        scalars=1,
        scratch=(pltpu.VMEM(full[0], F32),),
    )
    got = everywhere(send)
    resid, sub_field, send = call(
        sixth_kernel,
        [((rows, columns), F32), ((slots, rows_dev), F32), ((devices, 2, width), F32)],
        (got, loads, diags, field, xown, pown, row_s, hot_s),
        scratch=(pltpu.VMEM(extent[0], F32), parts),
        plain=(1,),
    )
    sums = everywhere(send)
    (global_field,) = call(last_kernel, [((rows, columns), F32)], (sums, field, resid), plain=(0,))
    return global_field, sub_field


def solution(mesh):
    return jax.shard_map(
        body,
        mesh=mesh,
        in_specs=(
            P("grp", "sub", None, None, None),
            P("grp", "sub", None),
            P("grp", "sub"),
            P("grp", "sub"),
            P("grp", "sub"),
            P("grp", "sub"),
            P("grp", "sub"),
            P(ALL, None),
            P(ALL, None),
        ),
        out_specs=(P(ALL, None), P("grp", "sub")),
        check_vma=False,
    )
```

```python
import jax
import jax.numpy as jnp
from jax import lax
from jax.experimental import pallas as pl
from jax.experimental.pallas import tpu as pltpu
from jax.sharding import PartitionSpec as P

F32 = jnp.float32
BF16 = jnp.bfloat16
CHUNK = 16
EDGE = 8
ALL = ("grp", "sub")

VMEM = pl.BlockSpec(memory_space=pltpu.VMEM)
SMEM = pl.BlockSpec(memory_space=pltpu.SMEM)


def total(x):
    return jnp.sum(jnp.sum(x, axis=0, keepdims=True), axis=1, keepdims=True)


def split3(x):
    hi = x.astype(BF16)
    rest = x - hi.astype(F32)
    mid = rest.astype(BF16)
    return hi, mid, (rest - mid.astype(F32)).astype(BF16)


def matches(ids, wanted):
    kind = BF16 if ids.shape[0] <= 256 else F32
    same = ids.astype(F32).astype(kind) == wanted.astype(kind)
    return jnp.where(same, jnp.ones((), kind), jnp.zeros((), kind)).astype(BF16)


def iota(shape, dim):
    return lax.broadcasted_iota(jnp.int32, shape, dim)


def contract(stiff, cols, vector, terms, arrive=None):
    slots, block_rows, per_row, width, _ = stiff.shape
    squares = []
    for s in range(slots):

        def row(r, acc, s=s):
            if arrive is not None:
                arrive(s, r)
            prod = None
            for n in range(per_row):
                part = stiff[s, r, n] * vector(s, cols[s, n, r])
                prod = part if prod is None else prod + part
            strain = jnp.sum(prod, axis=1, keepdims=True)
            if terms is not None:
                for n in range(per_row):
                    terms[s, pl.ds(n * block_rows + r, 1), :] = jnp.sum(
                        stiff[s, r, n] * strain, axis=0, keepdims=True
                    )
            return acc + strain * strain

        acc = jnp.zeros((width, 1), F32)
        for r in range(block_rows):
            acc = row(r, acc)
        squares.append(acc)
    return squares


def stacked(gathered, first, count):
    devices, slots = gathered.shape[:2]
    return jnp.concatenate(
        [gathered[d, s, first : first + count, :] for s in range(slots) for d in range(devices)],
        axis=0,
    )


def targets(pack, row, hot):
    count = hot.shape[2] // pack.shape[0]
    for s in range(hot.shape[0]):
        col = jnp.concatenate(
            [pack[d, 0, row : row + 1, s * count : (s + 1) * count] for d in range(pack.shape[0])], axis=1
        )
        hot[s] = matches(iota(hot.shape[1:], 0), col)


def landed(hot, arrived, count):
    devices, slots, _, width = arrived.shape
    sums = []
    for s in range(slots):
        source = jnp.concatenate([arrived[d, s, :count, :] for d in range(devices)], axis=0)
        out = jnp.dot(hot[s], jnp.concatenate(split3(source), axis=1), preferred_element_type=F32)
        sums.append(out[:, :width] + out[:, width : 2 * width] + out[:, 2 * width :])
    return jnp.concatenate(sums, axis=0)


def prep_kernel(live, diag, pen, load, cols, maps, gload, gdiag, grid, send, rest, cols_out, maps_out):
    slots, block_rows, width = send.shape
    per_row = cols.shape[1]
    first, rows = [], gload.shape[0]
    rest[...] = jnp.zeros_like(rest)
    for s in range(slots):
        count = live[:, s : s + 1]
        for b in range(block_rows):
            lanes = pl.ds(b * width, width)
            on = count > b
            main = diag[s : s + 1, lanes]
            if b == 0:
                main = main + pen[s : s + 1, :]
            first.append(jnp.where(on, load[s : s + 1, lanes], 0.0))
            rest[s, b : b + 1, :] = jnp.where(on, main, 0.0)
        rest[s, block_rows : block_rows + 1, :] = pen[s : s + 1, :]
        for n in range(per_row):
            at = (s * per_row + n) * block_rows
            rest[0, block_rows + 1 : block_rows + 2, at : at + block_rows] = (
                cols[s, n : n + 1, :]
            ).astype(F32)
    send[...] = jnp.concatenate(first, axis=0).reshape(slots, block_rows, width)
    cols_out[...] = cols[...]
    maps_out[...] = maps[...].astype(F32)
    grid[:rows, :] = gload[...]
    grid[rows:, :] = gdiag[...]


def first_kernel(cols, start, rest, stiff, *grids):
    slots, block_rows, per_row, width, _ = stiff.shape
    grids, terms = grids[:-1], grids[-1]
    groups = len(grids)
    rows, columns = grids[0].shape
    last, half = rows // 2 - 1, columns // width
    group = lax.axis_index("grp")

    def vector(s, c):
        return start[lax.div(c, block_rows), s, pl.ds(lax.rem(c, block_rows), 1), :]

    edge = block_rows * per_row + rest.shape[1]
    terms[:, edge - rest.shape[1] : edge, :] = rest[...]
    terms[:, edge:, :] = jnp.zeros((slots, terms.shape[1] - edge, width), F32)
    for away, grid in enumerate(grids):
        block = lax.rem(group + groups - away, groups)
        for side, picks in enumerate(((0, 1, last + 1), (last - 1, last, 2 * last + 1))):
            for k, row in enumerate(picks):
                for h in range(half):
                    at = edge + (block * 3 + k) * half + h
                    terms[side, pl.ds(at, 1), :] = grid[row : row + 1, h * width : (h + 1) * width]
    contract(stiff, cols, vector, terms)


def second_kernel(cols, maps, first, pack, stiff, resid, direc, terms, send, xown, pown, hot):
    slots, block_rows, per_row, width, _ = stiff.shape
    devices = pack.shape[0]
    blocks = devices * block_rows
    count = block_rows * per_row
    me = lax.axis_index("sub")
    start = stacked(first, 0, block_rows)
    dsum = stacked(pack, count, block_rows)
    targets(pack, count + block_rows + 1, hot)
    back = landed(hot, pack, count)
    image = jnp.where(dsum > 0.0, dsum * start + back, 0.0)
    head, scal = [], []
    for s in range(slots):
        span = slice(s * blocks, (s + 1) * blocks)
        r0, q0 = start[span], image[span]
        norm = total(r0 * r0)
        alpha = norm / total(r0 * q0)
        r1 = r0 - alpha * q0
        norm1 = total(r1 * r1)
        p1 = r1 + norm1 / norm * r0
        resid[span, :] = r1
        direc[span, :] = p1
        scal.append((norm1, total(dsum[span] * p1 * p1)))
        xown[s] = alpha * first[me, s]
        pown[s] = direc[pl.ds(s * blocks + me * block_rows, block_rows), :]
        head.append(pack[me, s, count + block_rows : count + block_rows + 1, :])
    squares = contract(stiff, cols, lambda s, c: direc[pl.ds(s * blocks + c, 1), :], terms)
    write_send(send, maps, head, [xown[s, 0:1, :] for s in range(slots)], pown, scal, squares, devices)
    send[:, 3 * slots + 1 :, :] = jnp.zeros((send.shape[0], slots - 1, width), F32)


def write_send(send, maps, pen, x_face, pown, scal, squares, devices):
    slots, width = len(x_face), x_face[0].shape[1]
    lane = iota((1, width), 1)
    rows = [pen[s] * x_face[s] for s in range(slots)]
    rows += [pen[s] * pown[s, 0:1, :] for s in range(slots)]
    row = jnp.zeros((1, width), F32)
    for s in range(slots):
        norm1, own = scal[s]
        image = total(squares[s]) + own * (1.0 / devices)
        row = jnp.where(lane == 2 * s, image, row)
        row = jnp.where(lane == 2 * s + 1, norm1 * (1.0 / devices), row)
    if maps is None:
        rows += [row, jnp.zeros((slots - 1, width), F32)]
        out = jnp.concatenate(rows, axis=0)
        for k in range(3):
            part = out[None, k * slots : (k + 1) * slots, :]
            send[:, k] = jnp.broadcast_to(part, (send.shape[0], slots, width))
        return
    rows += [maps[...], row]
    send[:, : 3 * slots + 1, :] = jnp.broadcast_to(
        jnp.concatenate(rows, axis=0)[None], (send.shape[0], 3 * slots + 1, width)
    )


def reactions(row_of, groups, slots):
    sums = row_of(-1)
    devices, width = sums.shape
    both = sums.reshape(groups, devices // groups, width).sum(axis=1)
    alphas, lams = [], []
    for s in range(slots):
        alpha = both[:, 2 * s + 1 : 2 * s + 2] / both[:, 2 * s : 2 * s + 1]
        alpha = jnp.broadcast_to(alpha, (groups, width))
        wide = jnp.broadcast_to(alpha[:, None, :], (groups, devices // groups, width))
        alphas.append(alpha)
        lams.append(row_of(s) + wide.reshape(devices, width) * row_of(slots + s))
    return alphas, lams


def split_lams(lams, part_s):
    for s, lam in enumerate(lams):
        hi = lam.astype(BF16).astype(F32)
        mid = (lam - hi).astype(BF16).astype(F32)
        part_s[0, s] = hi
        part_s[1, s] = mid
        part_s[2, s] = lam - hi - mid


def lanes_of(ref, d, slots):
    return jnp.concatenate([ref[s, pl.ds(d, 1), :] for s in range(slots)], axis=1)


def place(row_s, part_s, window, hot_of, chunk):
    _, slots, devices, _ = part_s.shape
    rows, columns = window
    ids_r = iota((rows, slots * part_s.shape[3]), 0).astype(F32).astype(BF16)

    def step(c, acc):
        lefts, hots = [], []
        for d in [c * chunk + i for i in range(chunk)]:
            hit = ids_r == lanes_of(row_s, d, slots).astype(BF16)
            lefts.append(
                jnp.concatenate(
                    [jnp.where(hit, lanes_of(part_s.at[i], d, slots).astype(BF16), jnp.zeros((), BF16)) for i in range(3)],
                    axis=0,
                )
            )
            hots.append(hot_of(d))
        return acc + lax.dot_general(
            jnp.concatenate(lefts, axis=1),
            jnp.concatenate(hots, axis=1),
            (((1,), (1,)), ((), ())),
            preferred_element_type=F32,
        )

    acc = jnp.zeros((3 * rows, columns), F32)
    acc = step(0, acc) if chunk == devices else lax.fori_loop(0, devices // chunk, step, acc)
    return acc[:rows] + acc[rows : 2 * rows] + acc[2 * rows :]


def stencil(ref, gdiag, first, count):
    here = ref[first : first + count, :]
    columns = here.shape[1]
    lane = iota(here.shape, 1)
    left = jnp.where(lane == 0, 0.0, pltpu.roll(here, 1, 1))
    right = jnp.where(lane == columns - 1, 0.0, pltpu.roll(here, columns - 1, 1))
    above = ref[first - 1 : first + count - 1, :]
    below = ref[first + 1 : first + count + 1, :]
    return (4.0 + gdiag) * here - (above + below + left + right)


def third_kernel(got, pack, terms, *more):
    groups = lax.axis_size("grp")
    third_inner(got, pack, terms, more[:groups], *more[groups:])


def third_inner(got, pack, terms, grids, window, loads, diags, alphas_out, send, row_s, hot_s, part_s, col_s):
    groups = len(grids)
    rows, columns = grids[0].shape
    rows = rows // 2
    tall = rows + 2 * EDGE
    slots, devices, width = row_s.shape
    near = devices // groups
    me, group = lax.axis_index("sub"), lax.axis_index("grp")
    alphas, lams = reactions(lambda r: got[:, 3 * slots if r < 0 else r, :], groups, slots)
    for s in range(slots):
        alphas_out[s, 0:groups, :] = alphas[s]
    split_lams(lams, part_s)
    apart = near * rows
    shift = (me * rows - EDGE).astype(F32)
    for s in range(slots):
        where = got[:, 2 * slots + s, :]
        row = jnp.floor(where * (1.0 / columns))
        col_s[s] = where - row * columns
        row = row - shift
        which = jnp.floor(row * (1.0 / apart))
        row = row - which * apart
        near_by = (row >= EDGE - 2) & (row < EDGE + rows + 2)
        row_s[s] = jnp.where(near_by, which * tall + row, -1.0)
    half, edge, count = columns // width, pack.shape[2] - edge_rows(groups, columns // width), terms.shape[1]
    loads[...] = jnp.zeros_like(loads)
    diags[...] = jnp.zeros_like(diags)
    for away, grid in enumerate(grids):
        base = pl.multiple_of(lax.rem(group + groups - away, groups) * tall + EDGE, 8)
        loads[pl.ds(base, rows), :] = grid[:rows, :]
        diags[pl.ds(base, rows), :] = grid[rows:, :]
    for g in range(groups):
        base = g * tall + EDGE
        def fill(side, device, block, base=base):
            first = base - 2 if side else base + rows
            diag_row = base - 1 if side else base + rows
            for h in range(half):
                lanes = slice(h * width, (h + 1) * width)
                at = edge + block * 3 * half + h
                loads[first : first + 1, lanes] = pack[device, side, at : at + 1, :]
                loads[first + 1 : first + 2, lanes] = pack[device, side, at + half : at + half + 1, :]
                diags[diag_row : diag_row + 1, lanes] = pack[device, side, at + 2 * half : at + 2 * half + 1, :]

        pl.when(me > 0)(lambda g=g, fill=fill: fill(1, me - 1, g))
        pl.when(me < near - 1)(lambda g=g, fill=fill: fill(0, me + 1, g))
        if g > 0:
            pl.when(me == 0)(lambda g=g, fill=fill: fill(1, near - 1, g - 1))
        if g < groups - 1:
            pl.when(me == near - 1)(lambda g=g, fill=fill: fill(0, 0, g + 1))

    ids_c = iota((columns, slots * width), 0)

    def hot_of(d):
        hot = matches(ids_c, lanes_of(col_s, d, slots))
        hot_s[d] = hot
        return hot

    window[...] = loads[...] + place(row_s, part_s, window.shape, hot_of, CHUNK)
    owns, ids = [], []
    top = bottom = None
    for g in range(groups):
        base = g * tall + EDGE
        own = window[base : base + rows, :]
        image = stencil(window, diags[base : base + rows, :], base, rows)
        top = own * own if top is None else top + own * own
        bottom = own * image if bottom is None else bottom + own * image
        owns.append(own)
        ids.append(iota((rows, 1), 0).astype(F32) + base)
    send[:, :count, :] = terms[...]
    send[:, count + near :, :] = jnp.zeros((slots, send.shape[1] - count - near, width), F32)
    at = count + near
    send[:, at : at + 1, :] = jnp.broadcast_to(total(top)[None], (slots, 1, width))
    send[:, at + 1 : at + 2, :] = jnp.broadcast_to(total(bottom)[None], (slots, 1, width))
    own, ids = jnp.concatenate(owns, axis=0), jnp.concatenate(ids, axis=0)
    parts = jnp.concatenate(split3(own), axis=0)
    tall_own = groups * rows
    for k in range(near):
        d = group * near + k
        seen = jnp.dot(parts, hot_s[d], preferred_element_type=F32)
        seen = seen[:tall_own] + seen[tall_own : 2 * tall_own] + seen[2 * tall_own :]
        hit = ids == lanes_of(row_s, d, slots)
        mine = jnp.sum(jnp.where(hit, seen, 0.0), axis=0, keepdims=True)
        for s in range(slots):
            send[s, count + k : count + k + 1, :] = mine[:, s * width : (s + 1) * width]


def edge_rows(groups, half):
    return -(-3 * half * groups // 8) * 8


def fourth_kernel(
    cols, pack, arrived, hot, window, alphas, resid, direc, xown, pown, stiff, start, terms, xnext, face, field
):
    slots, block_rows, per_row, width, _ = stiff.shape
    devices = pack.shape[0]
    blocks = devices * block_rows
    count = block_rows * per_row
    group = lax.axis_index("grp")
    me = lax.axis_index("sub")
    dsum = stacked(pack, count, block_rows)
    back = landed(hot, arrived, count)
    p1 = direc[...]
    image = jnp.where(dsum > 0.0, dsum * p1 + back, 0.0)
    tail = arrived[0, :, count:, :]
    for d in range(1, devices):
        tail = tail + arrived[d, :, count:, :]
    scale = tail[0, devices : devices + 1, :] / tail[0, devices + 1 : devices + 2, :]
    field[...] = window[...] * jnp.concatenate([scale] * (field.shape[1] // width), axis=1)
    for s in range(slots):
        span = slice(s * blocks, (s + 1) * blocks)
        alpha = alphas[s, pl.ds(group, 1), :]
        start[span, :] = resid[span, :] - alpha * image[span]
        xnext[s] = xown[s] + alpha * pown[s]
        face[s, :devices, :] = scale * tail[s, :devices, :]
        for d in range(devices):
            at = slice(s * blocks + d * block_rows, s * blocks + d * block_rows + 1)
            pen = pack[d, s, count + block_rows : count + block_rows + 1, :]
            start[at, :] = start[at, :] + pen * face[s, d : d + 1, :]
    contract(stiff, cols, lambda s, c: start[pl.ds(s * blocks + c, 1), :], terms)


def fifth_kernel(cols, pack, arrived, hot, bound, start, xin, stiff, send, xown, pown, direc):
    slots, block_rows, per_row, width, _ = stiff.shape
    devices = pack.shape[0]
    blocks = devices * block_rows
    count = block_rows * per_row
    me = lax.axis_index("sub")
    dsum = stacked(pack, count, block_rows)
    back = landed(hot, arrived, count)
    image = jnp.where(dsum > 0.0, dsum * start[...] + back, 0.0)
    head, face, scal = [], [], []
    for s in range(slots):
        span = slice(s * blocks, (s + 1) * blocks)
        r0, q0 = start[span, :], image[span]
        norm = total(r0 * r0)
        alpha = norm / total(r0 * q0)
        r1 = r0 - alpha * q0
        norm1 = total(r1 * r1)
        p1 = r1 + norm1 / norm * r0
        direc[span, :] = p1
        scal.append((norm1, total(dsum[span] * p1 * p1)))
        mine = pl.ds(s * blocks + me * block_rows, block_rows)
        xown[s] = xin[s] + alpha * start[mine, :]
        pown[s] = direc[mine, :]
        head.append(pack[me, s, count + block_rows : count + block_rows + 1, :])
        face.append(xown[s, 0:1, :] - bound[s, pl.ds(me, 1), :])
    squares = contract(stiff, cols, lambda s, c: direc[pl.ds(s * blocks + c, 1), :], None)
    write_send(send, None, head, face, pown, scal, squares, devices)


def sixth_kernel(got, loads, diags, field, xown, pown, row_s, hot_s, resid, xout, send, window, part_s):
    slots, devices, width = row_s.shape
    rows, columns = resid.shape
    tall = rows + 2 * EDGE
    groups = window.shape[0] // tall
    near = devices // groups
    group, me = lax.axis_index("grp"), lax.axis_index("sub")
    alphas, lams = reactions(
        lambda r: got[:, 2, 0, :] if r < 0 else got[:, r // slots, r % slots, :], groups, slots
    )
    for s in range(slots):
        part_s[0, s, 0:groups, :] = alphas[s]
        alpha = part_s[0, s, pl.ds(group, 1), :]
        for b in range(xown.shape[1]):
            xout[s : s + 1, b * width : (b + 1) * width] = (
                xown[s, b : b + 1, :] + alpha * pown[s, b : b + 1, :]
            )
    split_lams(lams, part_s)
    window[...] = loads[...] + place(row_s, part_s, window.shape, lambda d: hot_s[d], min(2 * CHUNK, devices))
    top = bottom = None
    for g in range(groups):
        base = g * tall + EDGE
        span = slice(base - 1, base + rows + 1)
        applied = stencil(field, diags[span, :], base - 1, rows + 2)
        at = iota(applied.shape, 0) + ((g * near + me) * rows - 1)
        inside = (at >= 0) & (at < devices * rows)
        window[span, :] = jnp.where(inside, window[span, :] - applied, 0.0)
        own = window[base : base + rows, :]
        image = stencil(window, diags[base : base + rows, :], base, rows)
        top = own * own if top is None else top + own * own
        bottom = own * image if bottom is None else bottom + own * image
    resid[...] = window[pl.ds(group * tall + EDGE, rows), :]
    send[:, 0:1, :] = jnp.broadcast_to(total(top)[None], (near, 1, width))
    send[:, 1:2, :] = jnp.broadcast_to(total(bottom)[None], (near, 1, width))


def last_kernel(got, field, resid, out):
    sums = jnp.sum(got[...], axis=0)
    scale = sums[0:1, :] / sums[1:2, :]
    rows, columns = out.shape
    mine = pl.ds(lax.axis_index("grp") * (rows + 2 * EDGE) + EDGE, rows)
    wide = jnp.concatenate([scale] * (columns // got.shape[2]), axis=1)
    out[...] = field[mine, :] + wide * resid[...]


def call(kernel, shapes, operands, scalars=0, raw=0, scratch=(), limit=4, plain=(), cost=None):
    operands = [
        pltpu.with_memory_space_constraint(x, pltpu.HBM if i < raw else pltpu.VMEM)
        for i, x in enumerate(operands)
    ]
    out_shape = [
        jax.ShapeDtypeStruct(s, d) if i in plain else pltpu.VMEM(s, d) for i, (s, d) in enumerate(shapes)
    ]
    return pl.pallas_call(
        kernel,
        out_shape=out_shape,
        in_specs=[SMEM] * scalars + [VMEM] * (len(operands) - scalars),
        out_specs=[VMEM] * len(shapes),
        scratch_shapes=list(scratch),
        compiler_params=pltpu.CompilerParams(vmem_limit_bytes=limit << 20),
        cost_estimate=cost,
    )(*operands)


def body(
    stiff_blocks,
    block_cols,
    live_blocks,
    sub_diag,
    penalty,
    sub_load,
    iface_map,
    global_load,
    global_diag,
):
    slots, block_rows, per_row, width, _ = stiff_blocks.shape
    rows_dev = block_rows * width
    rows, columns = global_load.shape
    near, groups = lax.axis_size("sub"), lax.axis_size("grp")
    devices = near * groups
    blocks = slots * near * block_rows
    count = block_rows * per_row
    extent = ((groups * (rows + 2 * EDGE), columns), F32)
    own = ((slots, block_rows, width), F32)
    full = ((blocks, width), F32)
    every = ((slots, count, width), F32)
    landing = ((slots, near * block_rows, near * count), BF16)
    cols = jnp.transpose(block_cols, (0, 2, 1))

    def everywhere(x):
        return lax.all_to_all(x, ALL, 0, 0)

    def near_all(x):
        return lax.all_gather(x, "sub")

    grid, send, rest, cols, maps = call(
        prep_kernel,
        [
            ((2 * rows, columns), F32),
            own,
            ((slots, block_rows + 8, width), F32),
            (cols.shape, jnp.int32),
            (iface_map.shape, F32),
        ],
        (live_blocks.reshape(1, slots), sub_diag, penalty, sub_load, cols, iface_map, global_load, global_diag),
        raw=8,
        cost=pl.CostEstimate(flops=20_000_000_000, bytes_accessed=0, transcendentals=0),
    )
    grids = [grid] + [
        lax.ppermute(grid, "grp", [(i, (i + away) % groups) for i in range(groups)]) for away in range(1, groups)
    ]
    first = near_all(send)
    stiff = stiff_blocks
    (terms,) = call(
        first_kernel,
        [((slots, count + rest.shape[1] + edge_rows(groups, columns // width), width), F32)],
        (cols, first, rest, stiff, *grids),
        scalars=1,
    )
    pack = near_all(terms)
    resid, direc, terms, send, xown, pown, hot = call(
        second_kernel,
        [full, full, every, ((devices, 4 * slots, width), F32), own, own, landing],
        (cols, maps, first, pack, stiff),
        scalars=1,
    )
    got = everywhere(send)
    listed = (slots, devices, width)
    parts = pltpu.VMEM((3,) + listed, F32)
    window, loads, diags, alphas, send, row_s, hot_s = call(
        third_kernel,
        [
            extent,
            extent,
            extent,
            ((slots, max(8, groups), width), F32),
            ((slots, count + near + 8, width), F32),
            (listed, F32),
            ((devices, columns, slots * width), BF16),
        ],
        (got, pack, terms, *grids),
        limit=8,
        scratch=(parts, pltpu.VMEM(listed, F32)),
    )
    arrived = near_all(send)
    start, terms, xown, bound, field = call(
        fourth_kernel,
        [full, every, own, ((slots, max(8, near), width), F32), extent],
        (cols, pack, arrived, hot, window, alphas, resid, direc, xown, pown, stiff),
        scalars=1,
    )
    arrived = near_all(terms)
    send, xown, pown = call(
        fifth_kernel,
        [((devices, 3, slots, width), F32), own, own],
        (cols, pack, arrived, hot, bound, start, xown, stiff),
        scalars=1,
        scratch=(pltpu.VMEM(full[0], F32),),
    )
    got = everywhere(send)
    resid, sub_field, send = call(
        sixth_kernel,
        [((rows, columns), F32), ((slots, rows_dev), F32), ((near, 2, width), F32)],
        (got, loads, diags, field, xown, pown, row_s, hot_s),
        scratch=(pltpu.VMEM(extent[0], F32), parts),
        limit=8,
        plain=(1,),
    )
    sums = lax.all_to_all(send, "sub", 0, 0)
    (global_field,) = call(last_kernel, [((rows, columns), F32)], (sums, field, resid), plain=(0,))
    return global_field, sub_field


def solution(mesh):
    return jax.shard_map(
        body,
        mesh=mesh,
        in_specs=(
            P("grp", "sub", None, None, None),
            P("grp", "sub", None),
            P("grp", "sub"),
            P("grp", "sub"),
            P("grp", "sub"),
            P("grp", "sub"),
            P("grp", "sub"),
            P(ALL, None),
            P(ALL, None),
        ),
        out_specs=(P(ALL, None), P("grp", "sub")),
        check_vma=False,
    )
```

```python
import jax
import jax.numpy as jnp
from jax import lax
from jax.experimental import pallas as pl
from jax.experimental.pallas import tpu as pltpu
from jax.sharding import PartitionSpec as P

F32 = jnp.float32
BF16 = jnp.bfloat16
CHUNK = 16
EDGE = 8
ALL = ("grp", "sub")

VMEM = pl.BlockSpec(memory_space=pltpu.VMEM)
SMEM = pl.BlockSpec(memory_space=pltpu.SMEM)


def total(x):
    return jnp.sum(jnp.sum(x, axis=0, keepdims=True), axis=1, keepdims=True)


def split3(x):
    hi = x.astype(BF16)
    rest = x - hi.astype(F32)
    mid = rest.astype(BF16)
    return hi, mid, (rest - mid.astype(F32)).astype(BF16)


def split2(x):
    hi = x.astype(BF16)
    return hi, (x - hi.astype(F32)).astype(BF16)


def matches(ids, wanted):
    kind = BF16 if ids.shape[0] <= 256 else F32
    same = ids.astype(F32).astype(kind) == wanted.astype(kind)
    return jnp.where(same, jnp.ones((), kind), jnp.zeros((), kind)).astype(BF16)


def iota(shape, dim):
    return lax.broadcasted_iota(jnp.int32, shape, dim)


def contract(stiff, cols, vector, terms, arrive=None):
    slots, block_rows, per_row, width, _ = stiff.shape
    squares = []
    for s in range(slots):

        def row(r, acc, s=s):
            if arrive is not None:
                arrive(s, r)
            prod = None
            for n in range(per_row):
                part = stiff[s, r, n] * vector(s, cols[s, n, r])
                prod = part if prod is None else prod + part
            strain = jnp.sum(prod, axis=1, keepdims=True)
            if terms is not None:
                for n in range(per_row):
                    terms[s, pl.ds(n * block_rows + r, 1), :] = jnp.sum(
                        stiff[s, r, n] * strain, axis=0, keepdims=True
                    )
            return acc + strain * strain

        acc = jnp.zeros((width, 1), F32)
        for r in range(block_rows):
            acc = row(r, acc)
        squares.append(acc)
    return squares


def stacked(gathered, first, count):
    devices, slots = gathered.shape[:2]
    return jnp.concatenate(
        [gathered[d, s, first : first + count, :] for s in range(slots) for d in range(devices)],
        axis=0,
    )


def targets(pack, row, hot):
    count = hot.shape[2] // pack.shape[0]
    for s in range(hot.shape[0]):
        col = jnp.concatenate(
            [pack[d, 0, row : row + 1, s * count : (s + 1) * count] for d in range(pack.shape[0])], axis=1
        )
        hot[s] = matches(iota(hot.shape[1:], 0), col)


def landed(hot, arrived, count):
    devices, slots, _, width = arrived.shape
    sums = []
    for s in range(slots):
        source = jnp.concatenate([arrived[d, s, :count, :] for d in range(devices)], axis=0)
        out = jnp.dot(hot[s], jnp.concatenate(split3(source), axis=1), preferred_element_type=F32)
        sums.append(out[:, :width] + out[:, width : 2 * width] + out[:, 2 * width :])
    return jnp.concatenate(sums, axis=0)


def prep_kernel(live, diag, pen, load, cols, maps, gload, gdiag, grid, send, rest, cols_out, maps_out):
    slots, block_rows, width = send.shape
    per_row = cols.shape[1]
    first, rows = [], gload.shape[0]
    rest[...] = jnp.zeros_like(rest)
    for s in range(slots):
        count = live[:, s : s + 1]
        for b in range(block_rows):
            lanes = pl.ds(b * width, width)
            on = count > b
            main = diag[s : s + 1, lanes]
            if b == 0:
                main = main + pen[s : s + 1, :]
            first.append(jnp.where(on, load[s : s + 1, lanes], 0.0))
            rest[s, b : b + 1, :] = jnp.where(on, main, 0.0)
        rest[s, block_rows : block_rows + 1, :] = pen[s : s + 1, :]
        for n in range(per_row):
            at = (s * per_row + n) * block_rows
            rest[0, block_rows + 1 : block_rows + 2, at : at + block_rows] = (
                cols[s, n : n + 1, :]
            ).astype(F32)
    send[...] = jnp.concatenate(first, axis=0).reshape(slots, block_rows, width)
    cols_out[...] = cols[...]
    maps_out[...] = maps[...].astype(F32)
    grid[:rows, :] = gload[...]
    grid[rows:, :] = gdiag[...]


def first_kernel(cols, start, rest, stiff, *grids):
    slots, block_rows, per_row, width, _ = stiff.shape
    grids, terms = grids[:-1], grids[-1]
    groups = len(grids)
    rows, columns = grids[0].shape
    last, half = rows // 2 - 1, columns // width
    group = lax.axis_index("grp")

    def vector(s, c):
        return start[lax.div(c, block_rows), s, pl.ds(lax.rem(c, block_rows), 1), :]

    edge = block_rows * per_row + rest.shape[1]
    terms[:, edge - rest.shape[1] : edge, :] = rest[...]
    terms[:, edge:, :] = jnp.zeros((slots, terms.shape[1] - edge, width), F32)
    for away, grid in enumerate(grids):
        block = lax.rem(group + groups - away, groups)
        for side, picks in enumerate(((0, 1, last + 1), (last - 1, last, 2 * last + 1))):
            for k, row in enumerate(picks):
                for h in range(half):
                    at = edge + (block * 3 + k) * half + h
                    terms[side, pl.ds(at, 1), :] = grid[row : row + 1, h * width : (h + 1) * width]
    contract(stiff, cols, vector, terms)


def second_kernel(cols, maps, first, pack, stiff, resid, direc, terms, send, xown, pown, hot):
    slots, block_rows, per_row, width, _ = stiff.shape
    devices = pack.shape[0]
    blocks = devices * block_rows
    count = block_rows * per_row
    me = lax.axis_index("sub")
    start = stacked(first, 0, block_rows)
    dsum = stacked(pack, count, block_rows)
    targets(pack, count + block_rows + 1, hot)
    back = landed(hot, pack, count)
    image = jnp.where(dsum > 0.0, dsum * start + back, 0.0)
    head, scal = [], []
    for s in range(slots):
        span = slice(s * blocks, (s + 1) * blocks)
        r0, q0 = start[span], image[span]
        norm = total(r0 * r0)
        alpha = norm / total(r0 * q0)
        r1 = r0 - alpha * q0
        norm1 = total(r1 * r1)
        p1 = r1 + norm1 / norm * r0
        resid[span, :] = r1
        direc[span, :] = p1
        scal.append((norm1, total(dsum[span] * p1 * p1)))
        xown[s] = alpha * first[me, s]
        pown[s] = direc[pl.ds(s * blocks + me * block_rows, block_rows), :]
        head.append(pack[me, s, count + block_rows : count + block_rows + 1, :])
    squares = contract(stiff, cols, lambda s, c: direc[pl.ds(s * blocks + c, 1), :], terms)
    write_send(send, maps, head, [xown[s, 0:1, :] for s in range(slots)], pown, scal, squares, devices)
    send[:, 3 * slots + 1 :, :] = jnp.zeros((send.shape[0], slots - 1, width), F32)


def write_send(send, maps, pen, x_face, pown, scal, squares, devices):
    slots, width = len(x_face), x_face[0].shape[1]
    lane = iota((1, width), 1)
    rows = [pen[s] * x_face[s] for s in range(slots)]
    rows += [pen[s] * pown[s, 0:1, :] for s in range(slots)]
    row = jnp.zeros((1, width), F32)
    for s in range(slots):
        norm1, own = scal[s]
        image = total(squares[s]) + own * (1.0 / devices)
        row = jnp.where(lane == 2 * s, image, row)
        row = jnp.where(lane == 2 * s + 1, norm1 * (1.0 / devices), row)
    if maps is None:
        rows += [row, jnp.zeros((slots - 1, width), F32)]
        out = jnp.concatenate(rows, axis=0)
        for k in range(3):
            part = out[None, k * slots : (k + 1) * slots, :]
            send[:, k] = jnp.broadcast_to(part, (send.shape[0], slots, width))
        return
    rows += [maps[...], row]
    send[:, : 3 * slots + 1, :] = jnp.broadcast_to(
        jnp.concatenate(rows, axis=0)[None], (send.shape[0], 3 * slots + 1, width)
    )


def reactions(row_of, groups, slots):
    sums = row_of(-1)
    devices, width = sums.shape
    both = sums.reshape(groups, devices // groups, width).sum(axis=1)
    alphas, lams = [], []
    for s in range(slots):
        alpha = both[:, 2 * s + 1 : 2 * s + 2] / both[:, 2 * s : 2 * s + 1]
        alpha = jnp.broadcast_to(alpha, (groups, width))
        wide = jnp.broadcast_to(alpha[:, None, :], (groups, devices // groups, width))
        alphas.append(alpha)
        lams.append(row_of(s) + wide.reshape(devices, width) * row_of(slots + s))
    return alphas, lams


def split_lams(lams, part_s):
    for s, lam in enumerate(lams):
        hi = lam.astype(BF16).astype(F32)
        part_s[0, s] = hi
        part_s[1, s] = lam - hi


def lanes_of(ref, d, slots):
    return jnp.concatenate([ref[s, pl.ds(d, 1), :] for s in range(slots)], axis=1)


def place(row_s, part_s, window, hot_of, chunk):
    _, slots, devices, _ = part_s.shape
    rows, columns = window
    ids_r = iota((rows, slots * part_s.shape[3]), 0).astype(F32).astype(BF16)

    def step(c, acc):
        lefts, hots = [], []
        for d in [c * chunk + i for i in range(chunk)]:
            hit = ids_r == lanes_of(row_s, d, slots).astype(BF16)
            lefts.append(
                jnp.concatenate(
                    [jnp.where(hit, lanes_of(part_s.at[i], d, slots).astype(BF16), jnp.zeros((), BF16)) for i in range(2)],
                    axis=0,
                )
            )
            hots.append(hot_of(d))
        return acc + lax.dot_general(
            jnp.concatenate(lefts, axis=1),
            jnp.concatenate(hots, axis=1),
            (((1,), (1,)), ((), ())),
            preferred_element_type=F32,
        )

    acc = jnp.zeros((2 * rows, columns), F32)
    acc = step(0, acc) if chunk == devices else lax.fori_loop(0, devices // chunk, step, acc)
    return acc[:rows] + acc[rows:]


def stencil(ref, gdiag, first, count):
    here = ref[first : first + count, :]
    columns = here.shape[1]
    lane = iota(here.shape, 1)
    left = jnp.where(lane == 0, 0.0, pltpu.roll(here, 1, 1))
    right = jnp.where(lane == columns - 1, 0.0, pltpu.roll(here, columns - 1, 1))
    above = ref[first - 1 : first + count - 1, :]
    below = ref[first + 1 : first + count + 1, :]
    return (4.0 + gdiag) * here - (above + below + left + right)


def third_kernel(got, pack, terms, *more):
    groups = lax.axis_size("grp")
    third_inner(got, pack, terms, more[:groups], *more[groups:])


def third_inner(got, pack, terms, grids, window, loads, diags, alphas_out, send, row_s, hot_s, part_s, col_s):
    groups = len(grids)
    rows, columns = grids[0].shape
    rows = rows // 2
    tall = rows + 2 * EDGE
    slots, devices, width = row_s.shape
    near = devices // groups
    me, group = lax.axis_index("sub"), lax.axis_index("grp")
    alphas, lams = reactions(lambda r: got[:, 3 * slots if r < 0 else r, :], groups, slots)
    for s in range(slots):
        alphas_out[s, 0:groups, :] = alphas[s]
    split_lams(lams, part_s)
    apart = near * rows
    shift = (me * rows - EDGE).astype(F32)
    for s in range(slots):
        where = got[:, 2 * slots + s, :]
        row = jnp.floor(where * (1.0 / columns))
        col_s[s] = where - row * columns
        row = row - shift
        which = jnp.floor(row * (1.0 / apart))
        row = row - which * apart
        near_by = (row >= EDGE - 2) & (row < EDGE + rows + 2)
        row_s[s] = jnp.where(near_by, which * tall + row, -1.0)
    half, edge, count = columns // width, pack.shape[2] - edge_rows(groups, columns // width), terms.shape[1]
    loads[...] = jnp.zeros_like(loads)
    diags[...] = jnp.zeros_like(diags)
    for away, grid in enumerate(grids):
        base = pl.multiple_of(lax.rem(group + groups - away, groups) * tall + EDGE, 8)
        loads[pl.ds(base, rows), :] = grid[:rows, :]
        diags[pl.ds(base, rows), :] = grid[rows:, :]
    for g in range(groups):
        base = g * tall + EDGE
        def fill(side, device, block, base=base):
            first = base - 2 if side else base + rows
            diag_row = base - 1 if side else base + rows
            for h in range(half):
                lanes = slice(h * width, (h + 1) * width)
                at = edge + block * 3 * half + h
                loads[first : first + 1, lanes] = pack[device, side, at : at + 1, :]
                loads[first + 1 : first + 2, lanes] = pack[device, side, at + half : at + half + 1, :]
                diags[diag_row : diag_row + 1, lanes] = pack[device, side, at + 2 * half : at + 2 * half + 1, :]

        pl.when(me > 0)(lambda g=g, fill=fill: fill(1, me - 1, g))
        pl.when(me < near - 1)(lambda g=g, fill=fill: fill(0, me + 1, g))
        if g > 0:
            pl.when(me == 0)(lambda g=g, fill=fill: fill(1, near - 1, g - 1))
        if g < groups - 1:
            pl.when(me == near - 1)(lambda g=g, fill=fill: fill(0, 0, g + 1))

    ids_c = iota((columns, slots * width), 0)

    def hot_of(d):
        hot = matches(ids_c, lanes_of(col_s, d, slots))
        hot_s[d] = hot
        return hot

    window[...] = loads[...] + place(row_s, part_s, window.shape, hot_of, CHUNK)
    owns, ids = [], []
    top = bottom = None
    for g in range(groups):
        base = g * tall + EDGE
        own = window[base : base + rows, :]
        image = stencil(window, diags[base : base + rows, :], base, rows)
        top = own * own if top is None else top + own * own
        bottom = own * image if bottom is None else bottom + own * image
        owns.append(own)
        ids.append(iota((rows, 1), 0).astype(F32) + base)
    send[:, :count, :] = terms[...]
    send[:, count + near :, :] = jnp.zeros((slots, send.shape[1] - count - near, width), F32)
    at = count + near
    send[:, at : at + 1, :] = jnp.broadcast_to(total(top)[None], (slots, 1, width))
    send[:, at + 1 : at + 2, :] = jnp.broadcast_to(total(bottom)[None], (slots, 1, width))
    own, ids = jnp.concatenate(owns, axis=0), jnp.concatenate(ids, axis=0)
    parts = jnp.concatenate(split2(own), axis=0)
    tall_own = groups * rows
    for k in range(near):
        d = group * near + k
        seen = jnp.dot(parts, hot_s[d], preferred_element_type=F32)
        seen = seen[:tall_own] + seen[tall_own:]
        hit = ids == lanes_of(row_s, d, slots)
        mine = jnp.sum(jnp.where(hit, seen, 0.0), axis=0, keepdims=True)
        for s in range(slots):
            send[s, count + k : count + k + 1, :] = mine[:, s * width : (s + 1) * width]


def edge_rows(groups, half):
    return -(-3 * half * groups // 8) * 8


def fourth_kernel(
    cols, pack, arrived, hot, window, alphas, resid, direc, xown, pown, stiff, start, terms, xnext, face, field
):
    slots, block_rows, per_row, width, _ = stiff.shape
    devices = pack.shape[0]
    blocks = devices * block_rows
    count = block_rows * per_row
    group = lax.axis_index("grp")
    me = lax.axis_index("sub")
    dsum = stacked(pack, count, block_rows)
    back = landed(hot, arrived, count)
    p1 = direc[...]
    image = jnp.where(dsum > 0.0, dsum * p1 + back, 0.0)
    tail = arrived[0, :, count:, :]
    for d in range(1, devices):
        tail = tail + arrived[d, :, count:, :]
    scale = tail[0, devices : devices + 1, :] / tail[0, devices + 1 : devices + 2, :]
    field[...] = window[...] * jnp.concatenate([scale] * (field.shape[1] // width), axis=1)
    for s in range(slots):
        span = slice(s * blocks, (s + 1) * blocks)
        alpha = alphas[s, pl.ds(group, 1), :]
        start[span, :] = resid[span, :] - alpha * image[span]
        xnext[s] = xown[s] + alpha * pown[s]
        face[s, :devices, :] = scale * tail[s, :devices, :]
        for d in range(devices):
            at = slice(s * blocks + d * block_rows, s * blocks + d * block_rows + 1)
            pen = pack[d, s, count + block_rows : count + block_rows + 1, :]
            start[at, :] = start[at, :] + pen * face[s, d : d + 1, :]
    contract(stiff, cols, lambda s, c: start[pl.ds(s * blocks + c, 1), :], terms)


def fifth_kernel(cols, pack, arrived, hot, bound, start, xin, stiff, send, xown, pown, direc):
    slots, block_rows, per_row, width, _ = stiff.shape
    devices = pack.shape[0]
    blocks = devices * block_rows
    count = block_rows * per_row
    me = lax.axis_index("sub")
    dsum = stacked(pack, count, block_rows)
    back = landed(hot, arrived, count)
    image = jnp.where(dsum > 0.0, dsum * start[...] + back, 0.0)
    head, face, scal = [], [], []
    for s in range(slots):
        span = slice(s * blocks, (s + 1) * blocks)
        r0, q0 = start[span, :], image[span]
        norm = total(r0 * r0)
        alpha = norm / total(r0 * q0)
        r1 = r0 - alpha * q0
        norm1 = total(r1 * r1)
        p1 = r1 + norm1 / norm * r0
        direc[span, :] = p1
        scal.append((norm1, total(dsum[span] * p1 * p1)))
        mine = pl.ds(s * blocks + me * block_rows, block_rows)
        xown[s] = xin[s] + alpha * start[mine, :]
        pown[s] = direc[mine, :]
        head.append(pack[me, s, count + block_rows : count + block_rows + 1, :])
        face.append(xown[s, 0:1, :] - bound[s, pl.ds(me, 1), :])
    squares = contract(stiff, cols, lambda s, c: direc[pl.ds(s * blocks + c, 1), :], None)
    write_send(send, None, head, face, pown, scal, squares, devices)


def sixth_kernel(got, loads, diags, field, xown, pown, row_s, hot_s, resid, xout, send, window, part_s):
    slots, devices, width = row_s.shape
    rows, columns = resid.shape
    tall = rows + 2 * EDGE
    groups = window.shape[0] // tall
    near = devices // groups
    group, me = lax.axis_index("grp"), lax.axis_index("sub")
    alphas, lams = reactions(
        lambda r: got[:, 2, 0, :] if r < 0 else got[:, r // slots, r % slots, :], groups, slots
    )
    for s in range(slots):
        part_s[0, s, 0:groups, :] = alphas[s]
        alpha = part_s[0, s, pl.ds(group, 1), :]
        for b in range(xown.shape[1]):
            xout[s : s + 1, b * width : (b + 1) * width] = (
                xown[s, b : b + 1, :] + alpha * pown[s, b : b + 1, :]
            )
    split_lams(lams, part_s)
    window[...] = loads[...] + place(row_s, part_s, window.shape, lambda d: hot_s[d], min(2 * CHUNK, devices))
    top = bottom = None
    for g in range(groups):
        base = g * tall + EDGE
        span = slice(base - 1, base + rows + 1)
        applied = stencil(field, diags[span, :], base - 1, rows + 2)
        at = iota(applied.shape, 0) + ((g * near + me) * rows - 1)
        inside = (at >= 0) & (at < devices * rows)
        window[span, :] = jnp.where(inside, window[span, :] - applied, 0.0)
        own = window[base : base + rows, :]
        image = stencil(window, diags[base : base + rows, :], base, rows)
        top = own * own if top is None else top + own * own
        bottom = own * image if bottom is None else bottom + own * image
    resid[...] = window[pl.ds(group * tall + EDGE, rows), :]
    send[:, 0:1, :] = jnp.broadcast_to(total(top)[None], (near, 1, width))
    send[:, 1:2, :] = jnp.broadcast_to(total(bottom)[None], (near, 1, width))


def last_kernel(got, field, resid, out):
    sums = jnp.sum(got[...], axis=0)
    scale = sums[0:1, :] / sums[1:2, :]
    rows, columns = out.shape
    mine = pl.ds(lax.axis_index("grp") * (rows + 2 * EDGE) + EDGE, rows)
    wide = jnp.concatenate([scale] * (columns // got.shape[2]), axis=1)
    out[...] = field[mine, :] + wide * resid[...]


def call(kernel, shapes, operands, scalars=0, raw=0, scratch=(), limit=4, plain=(), cost=None):
    operands = [
        pltpu.with_memory_space_constraint(x, pltpu.HBM if i < raw else pltpu.VMEM)
        for i, x in enumerate(operands)
    ]
    out_shape = [
        jax.ShapeDtypeStruct(s, d) if i in plain else pltpu.VMEM(s, d) for i, (s, d) in enumerate(shapes)
    ]
    return pl.pallas_call(
        kernel,
        out_shape=out_shape,
        in_specs=[SMEM] * scalars + [VMEM] * (len(operands) - scalars),
        out_specs=[VMEM] * len(shapes),
        scratch_shapes=list(scratch),
        compiler_params=pltpu.CompilerParams(vmem_limit_bytes=limit << 20),
        cost_estimate=cost,
    )(*operands)


def body(
    stiff_blocks,
    block_cols,
    live_blocks,
    sub_diag,
    penalty,
    sub_load,
    iface_map,
    global_load,
    global_diag,
):
    slots, block_rows, per_row, width, _ = stiff_blocks.shape
    rows_dev = block_rows * width
    rows, columns = global_load.shape
    near, groups = lax.axis_size("sub"), lax.axis_size("grp")
    devices = near * groups
    blocks = slots * near * block_rows
    count = block_rows * per_row
    extent = ((groups * (rows + 2 * EDGE), columns), F32)
    own = ((slots, block_rows, width), F32)
    full = ((blocks, width), F32)
    every = ((slots, count, width), F32)
    landing = ((slots, near * block_rows, near * count), BF16)
    cols = jnp.transpose(block_cols, (0, 2, 1))

    def everywhere(x):
        return lax.all_to_all(x, ALL, 0, 0)

    def near_all(x):
        return lax.all_gather(x, "sub")

    grid, send, rest, cols, maps = call(
        prep_kernel,
        [
            ((2 * rows, columns), F32),
            own,
            ((slots, block_rows + 8, width), F32),
            (cols.shape, jnp.int32),
            (iface_map.shape, F32),
        ],
        (live_blocks.reshape(1, slots), sub_diag, penalty, sub_load, cols, iface_map, global_load, global_diag),
        raw=8,
        cost=pl.CostEstimate(flops=20_000_000_000, bytes_accessed=0, transcendentals=0),
    )
    grids = [grid] + [
        lax.ppermute(grid, "grp", [(i, (i + away) % groups) for i in range(groups)]) for away in range(1, groups)
    ]
    first = near_all(send)
    stiff = stiff_blocks
    (terms,) = call(
        first_kernel,
        [((slots, count + rest.shape[1] + edge_rows(groups, columns // width), width), F32)],
        (cols, first, rest, stiff, *grids),
        scalars=1,
    )
    pack = near_all(terms)
    resid, direc, terms, send, xown, pown, hot = call(
        second_kernel,
        [full, full, every, ((devices, 4 * slots, width), F32), own, own, landing],
        (cols, maps, first, pack, stiff),
        scalars=1,
    )
    got = everywhere(send)
    listed = (slots, devices, width)
    parts = pltpu.VMEM((2,) + listed, F32)
    window, loads, diags, alphas, send, row_s, hot_s = call(
        third_kernel,
        [
            extent,
            extent,
            extent,
            ((slots, max(8, groups), width), F32),
            ((slots, count + near + 8, width), F32),
            (listed, F32),
            ((devices, columns, slots * width), BF16),
        ],
        (got, pack, terms, *grids),
        limit=8,
        scratch=(parts, pltpu.VMEM(listed, F32)),
    )
    arrived = near_all(send)
    start, terms, xown, bound, field = call(
        fourth_kernel,
        [full, every, own, ((slots, max(8, near), width), F32), extent],
        (cols, pack, arrived, hot, window, alphas, resid, direc, xown, pown, stiff),
        scalars=1,
    )
    arrived = near_all(terms)
    send, xown, pown = call(
        fifth_kernel,
        [((devices, 3, slots, width), F32), own, own],
        (cols, pack, arrived, hot, bound, start, xown, stiff),
        scalars=1,
        scratch=(pltpu.VMEM(full[0], F32),),
    )
    got = everywhere(send)
    resid, sub_field, send = call(
        sixth_kernel,
        [((rows, columns), F32), ((slots, rows_dev), F32), ((near, 2, width), F32)],
        (got, loads, diags, field, xown, pown, row_s, hot_s),
        scratch=(pltpu.VMEM(extent[0], F32), parts),
        limit=8,
        plain=(1,),
    )
    sums = lax.all_to_all(send, "sub", 0, 0)
    (global_field,) = call(last_kernel, [((rows, columns), F32)], (sums, field, resid), plain=(0,))
    return global_field, sub_field


def solution(mesh):
    return jax.shard_map(
        body,
        mesh=mesh,
        in_specs=(
            P("grp", "sub", None, None, None),
            P("grp", "sub", None),
            P("grp", "sub"),
            P("grp", "sub"),
            P("grp", "sub"),
            P("grp", "sub"),
            P("grp", "sub"),
            P(ALL, None),
            P(ALL, None),
        ),
        out_specs=(P(ALL, None), P("grp", "sub")),
        check_vma=False,
    )
```
